128 devices in a mesh: grp: 32 (over z, x_hi, y), head: 4 (over x_lo, core).
Axes of the slice: x: 4 (x_hi: 2, x_lo: 2; x = x_hi * 2 + x_lo), y: 4, z: 4, core: 2. Of those that a mesh axis runs over, the one named last changes fastest.
Arguments:
- hidden_in: bfloat16 [32, 128, 2048], P('grp'), may hold values from -6 to 6
- attn_gain: float32 [2048], replicated, may hold values from 0.1 to 1.9
- w_query: bfloat16 [2048, 2048], P(None, 'head'), may hold values from -0.125 to 0.125
- w_key: bfloat16 [2048, 2048], P(None, 'head'), may hold values from -0.125 to 0.125
- w_value: bfloat16 [2048, 2048], P(None, 'head'), may hold values from -0.125 to 0.125
- w_out: bfloat16 [2048, 2048], P('head'), may hold values from -0.125 to 0.125
- cache: bfloat16 [2, 32, 4096, 2048], P(None, None, 'grp', 'head'), may hold values from -900 to 900
- prefix_len: int32 [32], replicated, may hold values from 1 to 4096, 65536 in all
- mlp_gain: float32 [2048], replicated, may hold values from 0.1 to 1.9
- expert_ids: int32 [32, 128, 8], P('grp'), may hold values from 0 to 63, all different within a row; in each aligned block of 128 rows (0 to 127, 128 to 255, ..., all dimensions but the last counted through in order) at most 24 rows name the same one
- route_weight: float32 [32, 128, 8], P('grp'), may hold values from 0.05 to 1
- w_gate: bfloat16 [64, 2048, 1024], P('grp', None, 'head'), may hold values from -0.125 to 0.125
- w_up: bfloat16 [64, 2048, 1024], P('grp', None, 'head'), may hold values from -0.125 to 0.125
- w_down: bfloat16 [64, 1024, 2048], P('grp', 'head'), may hold values from -0.1875 to 0.1875
Outputs:
- layer_out: bfloat16 [32, 128, 2048], P('grp', None, 'head')
The draws below stay inside these ranges and needn't reach their ends.
Inputs may be any that keep to these rules, and one draw needn't show every extreme that they name: `expert_ids`: among one prompt's 128 tokens no expert is chosen more than 24 times; a token's 8 experts are distinct.
All inputs are finite; a program needn't handle non-finite values.
Results may differ from the reference program's by a relative error of at most 0.017.
The reference program's roundings to bfloat16 on the way count: a program that leaves them out, or rounds other values in their place, can miss the bound.
Values may be sent and summed in bfloat16 or wider, within the bound.
A program may use at most 128 MiB of HBM per device.

```python
import math
import jax
import jax.numpy as jnp
import numpy as np
from jax import lax

D = 2048
HEADS = 16
HD = 128
FF = 1024
TOPK = 8
NEW_TOK = 128
CTX = 4096
PROMPTS = 32
EXPERTS = 64
CAP = 24
N_GRP = 32
N_HEAD = 4


def draw_cache(key, part):
    base = jax.random.normal(key, (2, PROMPTS, CTX, D), jnp.float32)
    offset = jax.random.normal(jax.random.fold_in(key, 3), (PROMPTS, CTX // 64, D), jnp.float32)
    base = base.at[1].add(1.5 * jnp.repeat(offset, 64, axis=1))
    return jnp.clip(base, -900.0, 900.0).astype(jnp.bfloat16)


def steps_of(key, extent, pieces, smallest, high):
    def one(axis_at, shards_of):
        draws = jax.random.uniform(jax.random.fold_in(jax.random.fold_in(key, 6), axis_at), (shards_of,), jnp.float32, smallest / len(pieces), high / len(pieces))
        return jnp.repeat(jnp.exp(draws), extent[axis_at] // shards_of).reshape((-1,) + (1,) * (len(extent) - axis_at - 1))

    factor_of = one(*pieces[0])
    for cut in pieces[1:]:
        factor_of = factor_of * one(*cut)
    return factor_of


def profile(count, total, reach, skew):
    loads = [(1 << 20) // math.isqrt(rank ** skew) + 1 for rank in range(2, count + 1)]
    surplus, holding = total - reach - (count - 1), [1] * (count - 1)
    while surplus > 0:
        candidates = [i for i in range(count - 1) if holding[i] < reach]
        pool, budget = sum([loads[i] for i in candidates]), surplus
        for i in candidates:
            extra = min(reach - holding[i], max(1, budget * loads[i] // pool), surplus)
            holding[i] = holding[i] + extra
            surplus = surplus - extra
    return np.array([reach] + holding)


def ragged(key, amount, total, bound, slope):
    if amount == 2:
        one = jax.random.randint(key, (), max(1, total - bound), min(bound, total - 1) + 1)
        return jnp.stack([one, total - one])
    lengths = jnp.asarray(profile(amount, total, bound, slope), jnp.int32)
    twos = (amount - 1) // 2
    source_of, receiver = lengths[1:1 + 2 * twos:2], lengths[2:2 + 2 * twos:2]
    room = jnp.minimum(source_of - 1, bound - receiver)
    passed = jax.random.randint(jax.random.fold_in(key, 1), (twos,), 0, 1 << 20) % (room + 1)
    lengths = lengths.at[1:1 + 2 * twos:2].set(source_of - passed).at[2:2 + 2 * twos:2].set(receiver + passed)
    return lengths[jax.random.permutation(jax.random.fold_in(key, 2), amount)]


def routed_block(key, own, number, rows, number_of, top, bound, lean):
    ranking = jax.random.permutation(key, number_of)
    crowded, ordinary = load_shares(number_of, rows * top, bound, lean, True), load_shares(number_of, rows * top, bound, lean, False)
    places = jnp.arange(number_of)

    def named(lengths, offset_by):
        used = int((lengths > 0).sum())
        fixed = max(1, used // 4)
        shifted = fixed + (places - fixed + offset_by * (used - fixed)) % max(1, number_of - fixed)
        return jnp.zeros((number_of,), jnp.int32).at[ranking[jnp.where(places < fixed, places, shifted)]].set(jnp.asarray(lengths, jnp.int32))

    lengths = jnp.where(number % 4 == 0, named(crowded, number // 4), named(ordinary, number - number // 4 - 1))
    mixed = jax.random.permutation(jax.random.fold_in(own, 3), number_of)
    donor, receiver = mixed[0:number_of // 2 * 2:2], mixed[1:number_of // 2 * 2:2]
    room = jnp.minimum(lengths[donor] - 1, bound - lengths[receiver]) // 2
    room = jnp.where((donor == ranking[0]) | (receiver == ranking[0]) | (lengths[receiver] == 0), 0, jnp.maximum(room, 0))
    shifted = jax.random.randint(jax.random.fold_in(own, 4), (number_of // 2,), 0, 1 << 20) % (room + 1)
    lengths = lengths.at[donor].add(-shifted).at[receiver].add(shifted)
    items = jnp.searchsorted(jnp.cumsum(lengths), jnp.arange(rows * top), side="right").astype(jnp.int32)
    listing = items.reshape(top, rows).T
    listing = listing[jax.random.permutation(jax.random.fold_in(own, 1), rows)]
    offset_by = jax.random.randint(jax.random.fold_in(own, 2), (rows, 1), 0, top)
    return jnp.take_along_axis(listing, (jnp.arange(top)[None, :] + offset_by) % top, axis=1)


def load_shares(count, total, most, skew, full):
    portions = [(1 << 20) // math.isqrt(standing ** skew) + 1 for standing in range(1, count + 1)]
    largest = most if full else min(most, max(-(-total // count), total * portions[0] // sum(portions)))
    least = 1 if total - largest >= count - 1 else 0
    given, surplus = [largest] + [least] * (count - 1), total - largest - least * (count - 1)
    while surplus > 0:
        candidates = [i for i in range(1, count) if given[i] < largest] or [i for i in range(1, count) if given[i] < most]
        pool, remaining = sum([portions[i] for i in candidates]), surplus
        for i in candidates:
            extra = min(most - given[i], max(1, remaining * portions[i] // pool), surplus)
            given[i] = given[i] + extra
            surplus = surplus - extra
    return np.array(given)


def gaussian(stream_key, dims, scale, most, cuts=(), held_as=jnp.bfloat16):
    result = jax.random.normal(stream_key, dims, jnp.float32) * scale
    if len(cuts) > 0:
        result = steps_of(stream_key, dims, cuts, -0.22, 0.18) * result
    return jnp.clip(result, min=-most, max=most).astype(held_as)


def setup_inputs(seed: int = 0) -> dict:
    key_list = jax.random.split(jax.random.key(seed), 15)
    hidden_in = gaussian(key_list[0], (PROMPTS, NEW_TOK, D), 1.0, 6.0, ((0, 32),))
    attn_gain = jnp.clip(1.0 + 0.18 * jax.random.normal(key_list[1], (D,), jnp.float32), 0.1, 1.9)
    w_query = gaussian(key_list[2], (D, D), D ** -0.5, 0.125, ((1, 4),))
    w_key = gaussian(key_list[3], (D, D), D ** -0.5, 0.125, ((1, 4),))
    w_value = gaussian(key_list[4], (D, D), D ** -0.5, 0.125, ((1, 4),))
    w_out = gaussian(key_list[5], (D, D), D ** -0.5, 0.125, ((0, 4),))
    cache = draw_cache(jax.random.fold_in(key_list[14], 71), 0)
    prefix_len = ragged(key_list[7], PROMPTS, PROMPTS * CTX // 2, CTX, 2).astype(jnp.int32)
    mlp_gain = jnp.clip(1.0 + 0.18 * jax.random.normal(key_list[8], (D,), jnp.float32), 0.1, 1.9)
    expert_ids_keys = jax.random.split(jax.random.fold_in(key_list[9], 1), PROMPTS * NEW_TOK // NEW_TOK)
    expert_ids_turns = jax.random.permutation(jax.random.fold_in(key_list[9], 3), PROMPTS * NEW_TOK // NEW_TOK)
    expert_ids = jax.vmap(lambda own, number: routed_block(jax.random.fold_in(key_list[9], 2), own, number, NEW_TOK, EXPERTS, TOPK, CAP, 2))(expert_ids_keys, expert_ids_turns).reshape((PROMPTS, NEW_TOK, TOPK))
    route_weight = jnp.clip(0.05 + 0.95 * jax.random.uniform(key_list[10], (PROMPTS, NEW_TOK, TOPK), jnp.float32) ** steps_of(key_list[10], (PROMPTS, NEW_TOK, TOPK), ((0, 32),), -0.2, 0.2), 0.05, 1.0)
    w_gate = gaussian(key_list[11], (EXPERTS, D, FF), D ** -0.5, 0.125, ((0, 32), (2, 4)))
    w_up = gaussian(key_list[12], (EXPERTS, D, FF), D ** -0.5, 0.125, ((0, 32), (2, 4)))
    w_down = gaussian(key_list[13], (EXPERTS, FF, D), FF ** -0.5, 0.1875, ((0, 32), (1, 4)))
    return {"hidden_in": hidden_in, "attn_gain": attn_gain, "w_query": w_query, "w_key": w_key, "w_value": w_value, "w_out": w_out, "cache": cache, "prefix_len": prefix_len, "mlp_gain": mlp_gain, "expert_ids": expert_ids, "route_weight": route_weight, "w_gate": w_gate, "w_up": w_up, "w_down": w_down}


def rms_norm(values, gain):
    scale = lax.rsqrt(lax.optimization_barrier(jnp.mean(values * values, axis=-1, keepdims=True)) + 1e-05)
    return values * scale * gain

def rotate(tensor, position):
    half = HD // 2
    inverse = 10000.0 ** (-(jnp.arange(half).astype(jnp.float32) * 2.0) / HD)
    angle = position[:, None] * inverse[None, :]
    cosine = jnp.cos(angle)[:, None, :]
    sine = jnp.sin(angle)[:, None, :]
    first = tensor[..., :half]
    second = tensor[..., half:]
    return jnp.concatenate([first * cosine - second * sine, second * cosine + first * sine], axis=-1)

def one_prompt(prompt, hidden_in, attn_gain, w_query, w_key, w_value, w_out, cache, prefix_len):
    rows = hidden_in[prompt].astype(jnp.float32)
    normed = rms_norm(rows, attn_gain).astype(jnp.bfloat16)
    length = prefix_len[prompt]
    position = (length + jnp.arange(NEW_TOK)).astype(jnp.float32)
    query = jnp.dot(normed, w_query, preferred_element_type=jnp.float32).reshape(NEW_TOK, HEADS, HD)
    key_new = jnp.dot(normed, w_key, preferred_element_type=jnp.float32).reshape(NEW_TOK, HEADS, HD)
    value_new = jnp.dot(normed, w_value, preferred_element_type=jnp.float32).reshape(NEW_TOK, HEADS, HD)
    query = (rotate(query, position) * HD ** (-0.5)).astype(jnp.bfloat16).astype(jnp.float32)
    key_new = rotate(key_new, position).astype(jnp.bfloat16).astype(jnp.float32)
    value_new = value_new.astype(jnp.bfloat16).astype(jnp.float32)
    cache_key = cache[0, prompt].astype(jnp.float32).reshape(CTX, HEADS, HD)
    cache_value = cache[1, prompt].astype(jnp.float32).reshape(CTX, HEADS, HD)
    score_old = jnp.einsum('qhd,khd->hqk', query, cache_key)
    score_new = jnp.einsum('qhd,khd->hqk', query, key_new)
    allow_old = (jnp.arange(CTX) < length)[None, None, :]
    allow_new = (jnp.arange(NEW_TOK)[None, :] <= jnp.arange(NEW_TOK)[:, None])[None, :, :]
    score_old = jnp.where(allow_old, score_old, -1e+30)
    score_new = jnp.where(allow_new, score_new, -1e+30)
    top = jnp.maximum(lax.optimization_barrier(jnp.max(score_old, axis=-1, keepdims=True)), lax.optimization_barrier(jnp.max(score_new, axis=-1, keepdims=True)))
    prob_old = jnp.where(allow_old, jnp.exp(score_old - top), 0.0)
    prob_new = jnp.where(allow_new, jnp.exp(score_new - top), 0.0)
    total = lax.optimization_barrier(jnp.sum(prob_old, axis=-1)) + lax.optimization_barrier(jnp.sum(prob_new, axis=-1))
    numer = jnp.einsum('hqk,khd->qhd', prob_old.astype(jnp.bfloat16).astype(jnp.float32), cache_value)
    numer = numer + jnp.einsum('hqk,khd->qhd', prob_new.astype(jnp.bfloat16).astype(jnp.float32), value_new)
    attended = (numer / jnp.transpose(total)[:, :, None]).reshape(NEW_TOK, D).astype(jnp.bfloat16)
    return rows + jnp.dot(attended, w_out, preferred_element_type=jnp.float32)

def reference(hidden_in, attn_gain, w_query, w_key, w_value, w_out, cache, prefix_len, mlp_gain, expert_ids, route_weight, w_gate, w_up, w_down):
    resid = lax.map(lambda prompt: one_prompt(prompt, hidden_in, attn_gain, w_query, w_key, w_value, w_out, cache, prefix_len), jnp.arange(PROMPTS))
    resid = resid.reshape(PROMPTS * NEW_TOK, D)
    mixed_in = rms_norm(resid, mlp_gain).astype(jnp.bfloat16)
    chosen = expert_ids.reshape(PROMPTS * NEW_TOK, TOPK)
    weights = route_weight.reshape(PROMPTS * NEW_TOK, TOPK)
    room = N_GRP * CAP
    group = FF // N_HEAD

    def per_expert(acc, expert):
        hit = chosen == expert
        weight_sum = lax.optimization_barrier(jnp.sum(jnp.where(hit, weights, 0.0), axis=-1))
        picked = jnp.any(hit, axis=-1)
        index = jnp.nonzero(picked, size=room, fill_value=0)[0].astype(jnp.int32)
        count = jnp.sum(picked.astype(jnp.int32))
        valid = jnp.arange(room).astype(jnp.int32) < count
        rows = mixed_in[index]
        gate = jnp.dot(rows, w_gate[expert], preferred_element_type=jnp.float32)
        upper = jnp.dot(rows, w_up[expert], preferred_element_type=jnp.float32)
        act = (jax.nn.silu(gate) * upper).astype(jnp.bfloat16).astype(jnp.float32)
        parts = jnp.einsum('rhf,hfd->hrd', act.reshape(room, N_HEAD, group), w_down[expert].astype(jnp.float32).reshape(N_HEAD, group, D))
        summed = lax.optimization_barrier(jnp.sum(parts.astype(jnp.bfloat16).astype(jnp.float32), axis=0))
        scale = jnp.where(valid, weight_sum[index], 0.0)
        return (acc.at[index].add(scale[:, None] * summed), None)
    moe, unused = lax.scan(per_expert, jnp.zeros((PROMPTS * NEW_TOK, D), jnp.float32), jnp.arange(EXPERTS).astype(jnp.int32))
    return (resid + moe).astype(jnp.bfloat16).reshape(PROMPTS, NEW_TOK, D)
```

```python
import jax
import jax.numpy as jnp
from jax import lax
from jax.experimental import pallas as pl
from jax.experimental.pallas import tpu as pltpu
from jax.sharding import PartitionSpec as P

HD = 128
TOPK = 8


def rms_norm(values, gain):
    scale = lax.rsqrt(jnp.mean(values * values, axis=-1, keepdims=True) + 1e-05)
    return values * scale * gain


def rotate(tensor, position):
    half = HD // 2
    inverse = 10000.0 ** (-(jnp.arange(half).astype(jnp.float32) * 2.0) / HD)
    angle = position[:, None] * inverse[None, :]
    cosine = jnp.cos(angle)[:, None, :]
    sine = jnp.sin(angle)[:, None, :]
    first = tensor[..., :half]
    second = tensor[..., half:]
    return jnp.concatenate(
        [first * cosine - second * sine, second * cosine + first * sine], axis=-1
    )


def head_exchange(x, count, same_source, ident):
    rows, cols = x.shape[-2], x.shape[-1]
    mesh_kind = pl.DeviceIdType.MESH

    def kernel(x_ref, o_ref, send_sem, recv_sem):
        me = lax.axis_index("head")
        group = lax.axis_index("grp")
        barrier = pltpu.get_barrier_semaphore()
        for step in range(1, count):
            peer = lax.rem(me + step, count)
            pl.semaphore_signal(barrier, inc=1, device_id=(group, peer), device_id_type=mesh_kind)
        pl.semaphore_wait(barrier, count - 1)
        copies = []
        for step in range(1, count):
            peer = lax.rem(me + step, count)
            source = x_ref if same_source else x_ref.at[peer]
            copy = pltpu.make_async_remote_copy(
                src_ref=source,
                dst_ref=o_ref.at[me],
                send_sem=send_sem.at[step - 1],
                recv_sem=recv_sem.at[step - 1],
                device_id=(group, peer),
                device_id_type=mesh_kind,
            )
            copy.start()
            copies.append(copy)
        o_ref[me] = x_ref[...] if same_source else x_ref[me]
        for copy in copies:
            copy.wait()

    return pl.pallas_call(
        kernel,
        out_shape=jax.ShapeDtypeStruct((count, rows, cols), x.dtype),
        in_specs=[pl.BlockSpec(memory_space=pltpu.VMEM)],
        out_specs=pl.BlockSpec(memory_space=pltpu.VMEM),
        scratch_shapes=[pltpu.SemaphoreType.DMA((count - 1,)), pltpu.SemaphoreType.DMA((count - 1,))],
        compiler_params=pltpu.CompilerParams(collective_id=ident, has_side_effects=True),
    )(x)


def on_device(
    hidden_in,
    attn_gain,
    w_query,
    w_key,
    w_value,
    w_out,
    cache,
    prefix_len,
    mlp_gain,
    expert_ids,
    route_weight,
    w_gate,
    w_up,
    w_down,
):
    group_count = lax.axis_size("grp")
    head_count = lax.axis_size("head")
    my_prompt = lax.axis_index("grp")
    tokens = hidden_in.shape[1]
    width = hidden_in.shape[2]
    heads_here = w_query.shape[1] // HD
    length = prefix_len[my_prompt]
    rows = hidden_in[0].astype(jnp.float32)
    normed = rms_norm(rows, attn_gain).astype(jnp.bfloat16)
    position = (length + jnp.arange(tokens)).astype(jnp.float32)
    query = jnp.dot(normed, w_query, preferred_element_type=jnp.float32).reshape(
        tokens, heads_here, HD
    )
    key_new = jnp.dot(normed, w_key, preferred_element_type=jnp.float32).reshape(
        tokens, heads_here, HD
    )
    value_new = jnp.dot(normed, w_value, preferred_element_type=jnp.float32).reshape(
        tokens, heads_here, HD
    )
    query = (rotate(query, position) * HD ** (-0.5)).astype(jnp.bfloat16)
    key_new = rotate(key_new, position).astype(jnp.bfloat16)
    value_new = value_new.astype(jnp.bfloat16)
    relaid = lax.all_to_all(cache, "grp", split_axis=1, concat_axis=2, tiled=True)
    context = relaid.shape[2]
    cache_key = relaid[0, 0].reshape(context, heads_here, HD)
    cache_value = relaid[1, 0].reshape(context, heads_here, HD)
    score_old = jnp.einsum("qhd,khd->hqk", query, cache_key, preferred_element_type=jnp.float32)
    score_new = jnp.einsum("qhd,khd->hqk", query, key_new, preferred_element_type=jnp.float32)
    allow_old = (jnp.arange(context) < length)[None, None, :]
    allow_new = (jnp.arange(tokens)[None, :] <= jnp.arange(tokens)[:, None])[None, :, :]
    score_old = jnp.where(allow_old, score_old, -1e30)
    score_new = jnp.where(allow_new, score_new, -1e30)
    top = jnp.maximum(
        jnp.max(score_old, axis=-1, keepdims=True), jnp.max(score_new, axis=-1, keepdims=True)
    )
    prob_old = jnp.where(allow_old, jnp.exp(score_old - top), 0.0)
    prob_new = jnp.where(allow_new, jnp.exp(score_new - top), 0.0)
    total = jnp.sum(prob_old, axis=-1) + jnp.sum(prob_new, axis=-1)
    numer = jnp.einsum(
        "hqk,khd->qhd",
        prob_old.astype(jnp.bfloat16),
        cache_value,
        preferred_element_type=jnp.float32,
    )
    numer = numer + jnp.einsum(
        "hqk,khd->qhd", prob_new.astype(jnp.bfloat16), value_new, preferred_element_type=jnp.float32
    )
    attended = (
        (numer / jnp.transpose(total)[:, :, None])
        .reshape(tokens, heads_here * HD)
        .astype(jnp.bfloat16)
    )
    projected = jnp.dot(attended, w_out, preferred_element_type=jnp.float32)
    gathered = head_exchange(projected.astype(jnp.bfloat16), head_count, True, 0)
    resid = rows + jnp.sum(gathered.astype(jnp.float32), axis=0)
    mixed_in = rms_norm(resid, mlp_gain).astype(jnp.bfloat16)
    experts_here = w_gate.shape[0]
    expert_total = experts_here * group_count
    capacity = max(2, 3 * tokens * TOPK // (2 * expert_total))
    chosen = expert_ids[0].reshape(tokens * TOPK)
    weights = route_weight[0]
    pairs = tokens * TOPK
    slots = expert_total * capacity
    one_hot = (chosen[:, None] == jnp.arange(expert_total)[None, :]).astype(jnp.bfloat16)
    earlier = (jnp.arange(pairs)[None, :] < jnp.arange(pairs)[:, None]).astype(jnp.bfloat16)
    before = jnp.dot(earlier, one_hot, preferred_element_type=jnp.float32)
    slot = jnp.sum(before * one_hot.astype(jnp.float32), axis=1).astype(jnp.int32)
    target = chosen * capacity + slot
    place = (target[:, None] == jnp.arange(slots)[None, :]).reshape(tokens, TOPK, slots)
    dispatch = jnp.sum(place.astype(jnp.float32), axis=1).astype(jnp.bfloat16)
    outgoing = lax.dot_general(
        dispatch, mixed_in, (((0,), (0,)), ((), ())), preferred_element_type=jnp.float32
    ).astype(jnp.bfloat16)
    outgoing = outgoing.reshape(group_count, experts_here, capacity, width)
    arrived = lax.all_to_all(outgoing, "grp", split_axis=0, concat_axis=0, tiled=True)
    results = []
    for expert in range(experts_here):
        inputs = arrived[:, expert].reshape(group_count * capacity, width)
        gate = jnp.dot(inputs, w_gate[expert], preferred_element_type=jnp.float32)
        upper = jnp.dot(inputs, w_up[expert], preferred_element_type=jnp.float32)
        act = (jax.nn.silu(gate) * upper).astype(jnp.bfloat16)
        output = jnp.dot(act, w_down[expert], preferred_element_type=jnp.float32).astype(
            jnp.bfloat16
        )
        results.append(output.reshape(group_count, capacity, width))
    expert_out = jnp.stack(results, axis=1)
    share_width = width // head_count
    returned = lax.all_to_all(expert_out, "grp", split_axis=0, concat_axis=0, tiled=True)
    returned = returned.reshape(slots, width)
    weighting = jnp.sum(jnp.where(place, weights[:, :, None], 0.0), axis=1)
    combined = jnp.zeros((tokens, width), jnp.float32)
    for _ in range(3):
        piece = weighting.astype(jnp.bfloat16)
        weighting = weighting - piece.astype(jnp.float32)
        combined = combined + jnp.dot(piece, returned, preferred_element_type=jnp.float32)
    blocks = combined.reshape(tokens, head_count, share_width).transpose(1, 0, 2)
    exchanged = head_exchange(blocks.astype(jnp.bfloat16), head_count, False, 1)
    moe_share = jnp.sum(exchanged.astype(jnp.float32), axis=0)
    resid_share = lax.dynamic_slice_in_dim(
        resid, lax.axis_index("head") * share_width, share_width, 1
    )
    return (resid_share + moe_share).astype(jnp.bfloat16)[None]


def solution(mesh):
    placed = (
        P("grp", None, None),
        P(),
        P(None, "head"),
        P(None, "head"),
        P(None, "head"),
        P("head", None),
        P(None, None, "grp", "head"),
        P(),
        P(),
        P("grp", None, None),
        P("grp", None, None),
        P("grp", None, "head"),
        P("grp", None, "head"),
        P("grp", "head", None),
    )
    return jax.shard_map(
        on_device, mesh=mesh, in_specs=placed, out_specs=P("grp", None, "head"), check_vma=False
    )
```

```python
import jax
import jax.numpy as jnp
from jax import lax
from jax.experimental import pallas as pl
from jax.experimental.pallas import tpu as pltpu
from jax.sharding import PartitionSpec as P

HD = 128
TOPK = 8


def rms_norm(values, gain):
    scale = lax.rsqrt(jnp.mean(values * values, axis=-1, keepdims=True) + 1e-05)
    return values * scale * gain


def rotate(tensor, position):
    half = HD // 2
    inverse = 10000.0 ** (-(jnp.arange(half).astype(jnp.float32) * 2.0) / HD)
    angle = position[:, None] * inverse[None, :]
    cosine = jnp.cos(angle)[:, None, :]
    sine = jnp.sin(angle)[:, None, :]
    first = tensor[..., :half]
    second = tensor[..., half:]
    return jnp.concatenate(
        [first * cosine - second * sine, second * cosine + first * sine], axis=-1
    )


def head_exchange(x, count, same_source, ident):
    rows, cols = x.shape[-2], x.shape[-1]
    mesh_kind = pl.DeviceIdType.MESH

    def kernel(x_ref, o_ref, send_sem, recv_sem):
        me = lax.axis_index("head")
        group = lax.axis_index("grp")
        barrier = pltpu.get_barrier_semaphore()
        for step in range(1, count):
            peer = lax.rem(me + step, count)
            pl.semaphore_signal(barrier, inc=1, device_id=(group, peer), device_id_type=mesh_kind)
        pl.semaphore_wait(barrier, count - 1)
        copies = []
        for step in range(1, count):
            peer = lax.rem(me + step, count)
            source = x_ref if same_source else x_ref.at[peer]
            copy = pltpu.make_async_remote_copy(
                src_ref=source,
                dst_ref=o_ref.at[me],
                send_sem=send_sem.at[step - 1],
                recv_sem=recv_sem.at[step - 1],
                device_id=(group, peer),
                device_id_type=mesh_kind,
            )
            copy.start()
            copies.append(copy)
        o_ref[me] = x_ref[...] if same_source else x_ref[me]
        for copy in copies:
            copy.wait()

    return pl.pallas_call(
        kernel,
        out_shape=jax.ShapeDtypeStruct((count, rows, cols), x.dtype),
        in_specs=[pl.BlockSpec(memory_space=pltpu.VMEM)],
        out_specs=pl.BlockSpec(memory_space=pltpu.VMEM),
        scratch_shapes=[pltpu.SemaphoreType.DMA((count - 1,)), pltpu.SemaphoreType.DMA((count - 1,))],
        compiler_params=pltpu.CompilerParams(collective_id=ident, has_side_effects=True),
    )(x)


def head_gather(x, ident):
    mesh_kind = pl.DeviceIdType.MESH

    def kernel(x_ref, o_ref, own_sem, send_sem, recv_sem):
        me = lax.axis_index("head")
        group = lax.axis_index("grp")
        partner = me + 1 - 2 * lax.rem(me, 2)
        across = lax.rem(me + 2, 4)
        barrier = pltpu.get_barrier_semaphore()
        for peer in (partner, across):
            pl.semaphore_signal(barrier, inc=1, device_id=(group, peer), device_id_type=mesh_kind)
        pl.semaphore_wait(barrier, 2)
        own = pltpu.make_async_copy(x_ref, o_ref.at[me], own_sem)
        own.start()
        near = pltpu.make_async_remote_copy(
            src_ref=x_ref, dst_ref=o_ref.at[me], send_sem=send_sem.at[0], recv_sem=recv_sem.at[0],
            device_id=(group, partner), device_id_type=mesh_kind,
        )
        far = pltpu.make_async_remote_copy(
            src_ref=x_ref, dst_ref=o_ref.at[me], send_sem=send_sem.at[1], recv_sem=recv_sem.at[1],
            device_id=(group, across), device_id_type=mesh_kind,
        )
        near.start()
        far.start()
        far.wait_recv()
        relay = pltpu.make_async_remote_copy(
            src_ref=o_ref.at[across], dst_ref=o_ref.at[across], send_sem=send_sem.at[2],
            recv_sem=recv_sem.at[2], device_id=(group, partner), device_id_type=mesh_kind,
        )
        relay.start()
        own.wait()
        near.wait()
        far.wait_send()
        relay.wait()

    return pl.pallas_call(
        kernel,
        out_shape=jax.ShapeDtypeStruct((4,) + x.shape, x.dtype),
        in_specs=[pl.BlockSpec(memory_space=pl.ANY)],
        out_specs=pl.BlockSpec(memory_space=pl.ANY),
        scratch_shapes=[
            pltpu.SemaphoreType.DMA(()),
            pltpu.SemaphoreType.DMA((3,)),
            pltpu.SemaphoreType.DMA((3,)),
        ],
        compiler_params=pltpu.CompilerParams(collective_id=ident, has_side_effects=True),
    )(x)


def on_device(
    hidden_in,
    attn_gain,
    w_query,
    w_key,
    w_value,
    w_out,
    cache,
    prefix_len,
    mlp_gain,
    expert_ids,
    route_weight,
    w_gate,
    w_up,
    w_down,
):
    group_count = lax.axis_size("grp")
    head_count = lax.axis_size("head")
    my_prompt = lax.axis_index("grp")
    tokens = hidden_in.shape[1]
    width = hidden_in.shape[2]
    heads_here = w_query.shape[1] // HD
    length = prefix_len[my_prompt]
    rows = hidden_in[0].astype(jnp.float32)
    normed = rms_norm(rows, attn_gain).astype(jnp.bfloat16)
    position = (length + jnp.arange(tokens)).astype(jnp.float32)
    query = jnp.dot(normed, w_query, preferred_element_type=jnp.float32).reshape(
        tokens, heads_here, HD
    )
    key_new = jnp.dot(normed, w_key, preferred_element_type=jnp.float32).reshape(
        tokens, heads_here, HD
    )
    value_new = jnp.dot(normed, w_value, preferred_element_type=jnp.float32).reshape(
        tokens, heads_here, HD
    )
    query = (rotate(query, position) * HD ** (-0.5)).astype(jnp.bfloat16)
    key_new = rotate(key_new, position).astype(jnp.bfloat16)
    value_new = value_new.astype(jnp.bfloat16)
    relaid = lax.all_to_all(cache, "grp", split_axis=1, concat_axis=2, tiled=True)
    context = relaid.shape[2]
    cache_key = relaid[0, 0].reshape(context, heads_here, HD)
    cache_value = relaid[1, 0].reshape(context, heads_here, HD)
    score_old = jnp.einsum("qhd,khd->hqk", query, cache_key, preferred_element_type=jnp.float32)
    score_new = jnp.einsum("qhd,khd->hqk", query, key_new, preferred_element_type=jnp.float32)
    allow_old = (jnp.arange(context) < length)[None, None, :]
    allow_new = (jnp.arange(tokens)[None, :] <= jnp.arange(tokens)[:, None])[None, :, :]
    score_old = jnp.where(allow_old, score_old, -1e30)
    score_new = jnp.where(allow_new, score_new, -1e30)
    top = jnp.maximum(
        jnp.max(score_old, axis=-1, keepdims=True), jnp.max(score_new, axis=-1, keepdims=True)
    )
    prob_old = jnp.where(allow_old, jnp.exp(score_old - top), 0.0)
    prob_new = jnp.where(allow_new, jnp.exp(score_new - top), 0.0)
    total = jnp.sum(prob_old, axis=-1) + jnp.sum(prob_new, axis=-1)
    numer = jnp.einsum(
        "hqk,khd->qhd",
        prob_old.astype(jnp.bfloat16),
        cache_value,
        preferred_element_type=jnp.float32,
    )
    numer = numer + jnp.einsum(
        "hqk,khd->qhd", prob_new.astype(jnp.bfloat16), value_new, preferred_element_type=jnp.float32
    )
    attended = (
        (numer / jnp.transpose(total)[:, :, None])
        .reshape(tokens, heads_here * HD)
        .astype(jnp.bfloat16)
    )
    projected = jnp.dot(attended, w_out, preferred_element_type=jnp.float32)
    gathered = head_gather(projected.astype(jnp.bfloat16), 0)
    resid = rows + jnp.sum(gathered.astype(jnp.float32), axis=0)
    mixed_in = rms_norm(resid, mlp_gain).astype(jnp.bfloat16)
    experts_here = w_gate.shape[0]
    expert_total = experts_here * group_count
    capacity = max(2, 3 * tokens * TOPK // (2 * expert_total))
    chosen = expert_ids[0].reshape(tokens * TOPK)
    weights = route_weight[0]
    pairs = tokens * TOPK
    slots = expert_total * capacity
    one_hot = (chosen[:, None] == jnp.arange(expert_total)[None, :]).astype(jnp.bfloat16)
    earlier = (jnp.arange(pairs)[None, :] < jnp.arange(pairs)[:, None]).astype(jnp.bfloat16)
    before = jnp.dot(earlier, one_hot, preferred_element_type=jnp.float32)
    slot = jnp.sum(before * one_hot.astype(jnp.float32), axis=1).astype(jnp.int32)
    target = chosen * capacity + slot
    place = (target[:, None] == jnp.arange(slots)[None, :]).reshape(tokens, TOPK, slots)
    dispatch = jnp.sum(place.astype(jnp.float32), axis=1).astype(jnp.bfloat16)
    share_width = width // head_count
    my_columns = lax.dynamic_slice_in_dim(
        mixed_in, lax.axis_index("head") * share_width, share_width, 1
    )
    outgoing = lax.dot_general(
        dispatch, my_columns, (((0,), (0,)), ((), ())), preferred_element_type=jnp.float32
    ).astype(jnp.bfloat16)
    outgoing = outgoing.reshape(group_count, experts_here, capacity, share_width)
    arrived = lax.all_to_all(outgoing, "grp", split_axis=0, concat_axis=0, tiled=True)
    arrived = head_gather(arrived, 2)
    results = []
    for expert in range(experts_here):
        inputs = arrived[:, :, expert].reshape(head_count, group_count * capacity, share_width)
        gate_w = w_gate[expert].reshape(head_count, share_width, -1)
        up_w = w_up[expert].reshape(head_count, share_width, -1)
        gate = jnp.einsum("qrc,qcf->rf", inputs, gate_w, preferred_element_type=jnp.float32)
        upper = jnp.einsum("qrc,qcf->rf", inputs, up_w, preferred_element_type=jnp.float32)
        act = (jax.nn.silu(gate) * upper).astype(jnp.bfloat16)
        output = jnp.dot(act, w_down[expert], preferred_element_type=jnp.float32).astype(
            jnp.bfloat16
        )
        results.append(output.reshape(group_count, capacity, width))
    expert_out = jnp.stack(results, axis=1)
    returned = lax.all_to_all(expert_out, "grp", split_axis=0, concat_axis=0, tiled=True)
    returned = returned.reshape(slots, width)
    weighting = jnp.sum(jnp.where(place, weights[:, :, None], 0.0), axis=1)
    combined = jnp.zeros((tokens, width), jnp.float32)
    for _ in range(3):
        piece = weighting.astype(jnp.bfloat16)
        weighting = weighting - piece.astype(jnp.float32)
        combined = combined + jnp.dot(piece, returned, preferred_element_type=jnp.float32)
    blocks = combined.reshape(tokens, head_count, share_width).transpose(1, 0, 2)
    exchanged = head_exchange(blocks.astype(jnp.bfloat16), head_count, False, 1)
    moe_share = jnp.sum(exchanged.astype(jnp.float32), axis=0)
    resid_share = lax.dynamic_slice_in_dim(
        resid, lax.axis_index("head") * share_width, share_width, 1
    )
    return (resid_share + moe_share).astype(jnp.bfloat16)[None]


def solution(mesh):
    placed = (
        P("grp", None, None),
        P(),
        P(None, "head"),
        P(None, "head"),
        P(None, "head"),
        P("head", None),
        P(None, None, "grp", "head"),
        P(),
        P(),
        P("grp", None, None),
        P("grp", None, None),
        P("grp", None, "head"),
        P("grp", None, "head"),
        P("grp", "head", None),
    )
    return jax.shard_map(
        on_device, mesh=mesh, in_specs=placed, out_specs=P("grp", None, "head"), check_vma=False
    )
```

```python
import jax
import jax.numpy as jnp
from jax import lax
from jax.experimental import pallas as pl
from jax.experimental.pallas import tpu as pltpu
from jax.sharding import PartitionSpec as P

HD = 128
TOPK = 8


def rms_norm(values, gain):
    scale = lax.rsqrt(jnp.mean(values * values, axis=-1, keepdims=True) + 1e-05)
    return values * scale * gain


def rotate(tensor, position):
    half = HD // 2
    inverse = 10000.0 ** (-(jnp.arange(half).astype(jnp.float32) * 2.0) / HD)
    angle = position[:, None] * inverse[None, :]
    cosine = jnp.cos(angle)[:, None, :]
    sine = jnp.sin(angle)[:, None, :]
    first = tensor[..., :half]
    second = tensor[..., half:]
    return jnp.concatenate(
        [first * cosine - second * sine, second * cosine + first * sine], axis=-1
    )


def peer_swap(x, across, ident):
    mesh_kind = pl.DeviceIdType.MESH

    def kernel(x_ref, o_ref, send_sem, recv_sem):
        me = lax.axis_index("head")
        group = lax.axis_index("grp")
        peer = lax.rem(me + 2, 4) if across else me + 1 - 2 * lax.rem(me, 2)
        barrier = pltpu.get_barrier_semaphore()
        pl.semaphore_signal(barrier, inc=1, device_id=(group, peer), device_id_type=mesh_kind)
        pl.semaphore_wait(barrier, 1)
        copy = pltpu.make_async_remote_copy(
            src_ref=x_ref, dst_ref=o_ref, send_sem=send_sem, recv_sem=recv_sem,
            device_id=(group, peer), device_id_type=mesh_kind,
        )
        copy.start()
        copy.wait()

    return pl.pallas_call(
        kernel,
        out_shape=jax.ShapeDtypeStruct(x.shape, x.dtype),
        in_specs=[pl.BlockSpec(memory_space=pl.ANY)],
        out_specs=pl.BlockSpec(memory_space=pl.ANY),
        scratch_shapes=[pltpu.SemaphoreType.DMA(()), pltpu.SemaphoreType.DMA(())],
        compiler_params=pltpu.CompilerParams(collective_id=ident, has_side_effects=True),
    )(x)


def head_gather(x, ident):
    mesh_kind = pl.DeviceIdType.MESH

    def kernel(x_ref, o_ref, own_sem, send_sem, recv_sem):
        me = lax.axis_index("head")
        group = lax.axis_index("grp")
        partner = me + 1 - 2 * lax.rem(me, 2)
        across = lax.rem(me + 2, 4)
        barrier = pltpu.get_barrier_semaphore()
        for peer in (partner, across):
            pl.semaphore_signal(barrier, inc=1, device_id=(group, peer), device_id_type=mesh_kind)
        pl.semaphore_wait(barrier, 2)
        own = pltpu.make_async_copy(x_ref, o_ref.at[me], own_sem)
        own.start()
        near = pltpu.make_async_remote_copy(
            src_ref=x_ref, dst_ref=o_ref.at[me], send_sem=send_sem.at[0], recv_sem=recv_sem.at[0],
            device_id=(group, partner), device_id_type=mesh_kind,
        )
        far = pltpu.make_async_remote_copy(
            src_ref=x_ref, dst_ref=o_ref.at[me], send_sem=send_sem.at[1], recv_sem=recv_sem.at[1],
            device_id=(group, across), device_id_type=mesh_kind,
        )
        near.start()
        far.start()
        far.wait_recv()
        relay = pltpu.make_async_remote_copy(
            src_ref=o_ref.at[across], dst_ref=o_ref.at[across], send_sem=send_sem.at[2],
            recv_sem=recv_sem.at[2], device_id=(group, partner), device_id_type=mesh_kind,
        )
        relay.start()
        own.wait()
        near.wait()
        far.wait_send()
        relay.wait()

    return pl.pallas_call(
        kernel,
        out_shape=jax.ShapeDtypeStruct((4,) + x.shape, x.dtype),
        in_specs=[pl.BlockSpec(memory_space=pl.ANY)],
        out_specs=pl.BlockSpec(memory_space=pl.ANY),
        scratch_shapes=[
            pltpu.SemaphoreType.DMA(()),
            pltpu.SemaphoreType.DMA((3,)),
            pltpu.SemaphoreType.DMA((3,)),
        ],
        compiler_params=pltpu.CompilerParams(collective_id=ident, has_side_effects=True),
    )(x)


def on_device(
    hidden_in,
    attn_gain,
    w_query,
    w_key,
    w_value,
    w_out,
    cache,
    prefix_len,
    mlp_gain,
    expert_ids,
    route_weight,
    w_gate,
    w_up,
    w_down,
):
    group_count = lax.axis_size("grp")
    head_count = lax.axis_size("head")
    my_prompt = lax.axis_index("grp")
    tokens = hidden_in.shape[1]
    width = hidden_in.shape[2]
    heads_here = w_query.shape[1] // HD
    length = prefix_len[my_prompt]
    rows = hidden_in[0].astype(jnp.float32)
    normed = rms_norm(rows, attn_gain).astype(jnp.bfloat16)
    position = (length + jnp.arange(tokens)).astype(jnp.float32)
    query = jnp.dot(normed, w_query, preferred_element_type=jnp.float32).reshape(
        tokens, heads_here, HD
    )
    key_new = jnp.dot(normed, w_key, preferred_element_type=jnp.float32).reshape(
        tokens, heads_here, HD
    )
    value_new = jnp.dot(normed, w_value, preferred_element_type=jnp.float32).reshape(
        tokens, heads_here, HD
    )
    query = (rotate(query, position) * HD ** (-0.5)).astype(jnp.bfloat16)
    key_new = rotate(key_new, position).astype(jnp.bfloat16)
    value_new = value_new.astype(jnp.bfloat16)
    relaid = lax.all_to_all(cache, "grp", split_axis=1, concat_axis=2, tiled=True)
    context = relaid.shape[2]
    cache_key = relaid[0, 0].reshape(context, heads_here, HD)
    cache_value = relaid[1, 0].reshape(context, heads_here, HD)
    score_old = jnp.einsum("qhd,khd->hqk", query, cache_key, preferred_element_type=jnp.float32)
    score_new = jnp.einsum("qhd,khd->hqk", query, key_new, preferred_element_type=jnp.float32)
    allow_old = (jnp.arange(context) < length)[None, None, :]
    allow_new = (jnp.arange(tokens)[None, :] <= jnp.arange(tokens)[:, None])[None, :, :]
    score_old = jnp.where(allow_old, score_old, -1e30)
    score_new = jnp.where(allow_new, score_new, -1e30)
    top = jnp.maximum(
        jnp.max(score_old, axis=-1, keepdims=True), jnp.max(score_new, axis=-1, keepdims=True)
    )
    prob_old = jnp.where(allow_old, jnp.exp(score_old - top), 0.0)
    prob_new = jnp.where(allow_new, jnp.exp(score_new - top), 0.0)
    total = jnp.sum(prob_old, axis=-1) + jnp.sum(prob_new, axis=-1)
    numer = jnp.einsum(
        "hqk,khd->qhd",
        prob_old.astype(jnp.bfloat16),
        cache_value,
        preferred_element_type=jnp.float32,
    )
    numer = numer + jnp.einsum(
        "hqk,khd->qhd", prob_new.astype(jnp.bfloat16), value_new, preferred_element_type=jnp.float32
    )
    attended = (
        (numer / jnp.transpose(total)[:, :, None])
        .reshape(tokens, heads_here * HD)
        .astype(jnp.bfloat16)
    )
    projected = jnp.dot(attended, w_out, preferred_element_type=jnp.float32)
    gathered = head_gather(projected.astype(jnp.bfloat16), 0)
    resid = rows + jnp.sum(gathered.astype(jnp.float32), axis=0)
    mixed_in = rms_norm(resid, mlp_gain).astype(jnp.bfloat16)
    experts_here = w_gate.shape[0]
    expert_total = experts_here * group_count
    capacity = max(2, 3 * tokens * TOPK // (2 * expert_total))
    chosen = expert_ids[0].reshape(tokens * TOPK)
    weights = route_weight[0]
    pairs = tokens * TOPK
    slots = expert_total * capacity
    one_hot = (chosen[:, None] == jnp.arange(expert_total)[None, :]).astype(jnp.bfloat16)
    earlier = (jnp.arange(pairs)[None, :] < jnp.arange(pairs)[:, None]).astype(jnp.bfloat16)
    before = jnp.dot(earlier, one_hot, preferred_element_type=jnp.float32)
    slot = jnp.sum(before * one_hot.astype(jnp.float32), axis=1).astype(jnp.int32)
    target = chosen * capacity + slot
    place = (target[:, None] == jnp.arange(slots)[None, :]).reshape(tokens, TOPK, slots)
    dispatch = jnp.sum(place.astype(jnp.float32), axis=1).astype(jnp.bfloat16)
    share_width = width // head_count
    head_at = lax.axis_index("head")
    core = lax.rem(head_at, 2)
    chip = head_at // 2
    other_core = 1 - core
    def halves(array, which):
        split = array.reshape(array.shape[:-1] + (2, 2, share_width))
        taken = lax.dynamic_index_in_dim(split, which, axis=split.ndim - 2, keepdims=False)
        return taken.reshape(array.shape[:-1] + (2 * share_width,))

    def row_halves(array, which):
        split = array.reshape((2, 2, share_width) + array.shape[1:])
        taken = lax.dynamic_index_in_dim(split, which, axis=1, keepdims=False)
        return taken.reshape((2 * share_width,) + array.shape[1:])

    half = 2 * share_width
    outgoing = lax.dot_general(
        dispatch, halves(mixed_in, core), (((0,), (0,)), ((), ())), preferred_element_type=jnp.float32
    ).astype(jnp.bfloat16)
    outgoing = outgoing.reshape(group_count, experts_here, capacity, half)
    arrived = lax.all_to_all(outgoing, "grp", split_axis=0, concat_axis=0, tiled=True)
    arrived_other = peer_swap(arrived, False, 1)
    mine_parts = []
    other_parts = []
    for expert in range(experts_here):
        mine = arrived[:, expert].reshape(group_count * capacity, half)
        other = arrived_other[:, expert].reshape(group_count * capacity, half)
        gate = jnp.dot(mine, row_halves(w_gate[expert], core), preferred_element_type=jnp.float32)
        gate = gate + jnp.dot(other, row_halves(w_gate[expert], other_core), preferred_element_type=jnp.float32)
        upper = jnp.dot(mine, row_halves(w_up[expert], core), preferred_element_type=jnp.float32)
        upper = upper + jnp.dot(other, row_halves(w_up[expert], other_core), preferred_element_type=jnp.float32)
        act = (jax.nn.silu(gate) * upper).astype(jnp.bfloat16)
        mine_parts.append(
            jnp.dot(act, halves(w_down[expert], core), preferred_element_type=jnp.float32)
            .astype(jnp.bfloat16)
            .reshape(group_count, capacity, half)
        )
        other_parts.append(
            jnp.dot(act, halves(w_down[expert], other_core), preferred_element_type=jnp.float32)
            .astype(jnp.bfloat16)
            .reshape(group_count, capacity, half)
        )
    mine_out = jnp.stack(mine_parts, axis=1)
    partner_out = peer_swap(jnp.stack(other_parts, axis=1), False, 2)
    pair_sum = (mine_out.astype(jnp.float32) + partner_out.astype(jnp.float32)).astype(jnp.bfloat16)
    returned = lax.all_to_all(pair_sum, "grp", split_axis=0, concat_axis=0, tiled=True)
    returned = returned.reshape(slots, half)
    weighting = jnp.sum(jnp.where(place, weights[:, :, None], 0.0), axis=1)
    combined = jnp.zeros((tokens, half), jnp.float32)
    for _ in range(3):
        piece = weighting.astype(jnp.bfloat16)
        weighting = weighting - piece.astype(jnp.float32)
        combined = combined + jnp.dot(piece, returned, preferred_element_type=jnp.float32)
    combined = combined.reshape(tokens, 2, share_width)
    keep = lax.dynamic_index_in_dim(combined, chip, axis=1, keepdims=False)
    give = lax.dynamic_index_in_dim(combined, 1 - chip, axis=1, keepdims=False)
    moe_share = keep + peer_swap(give, True, 3)
    resid_share = lax.dynamic_slice_in_dim(resid, head_at * share_width, share_width, 1)
    return (resid_share + moe_share).astype(jnp.bfloat16)[None]


def solution(mesh):
    placed = (
        P("grp", None, None),
        P(),
        P(None, "head"),
        P(None, "head"),
        P(None, "head"),
        P("head", None),
        P(None, None, "grp", "head"),
        P(),
        P(),
        P("grp", None, None),
        P("grp", None, None),
        P("grp", None, "head"),
        P("grp", None, "head"),
        P("grp", "head", None),
    )
    return jax.shard_map(
        on_device, mesh=mesh, in_specs=placed, out_specs=P("grp", None, "head"), check_vma=False
    )
```

```python
import jax
import jax.numpy as jnp
from jax import lax
from jax.experimental import pallas as pl
from jax.experimental.pallas import tpu as pltpu
from jax.sharding import PartitionSpec as P

HD = 128
TOPK = 8


def rms_norm(values, gain):
    scale = lax.rsqrt(jnp.mean(values * values, axis=-1, keepdims=True) + 1e-05)
    return values * scale * gain


def rotate(tensor, position):
    half = HD // 2
    inverse = 10000.0 ** (-(jnp.arange(half).astype(jnp.float32) * 2.0) / HD)
    angle = position[:, None] * inverse[None, :]
    cosine = jnp.cos(angle)[:, None, :]
    sine = jnp.sin(angle)[:, None, :]
    first = tensor[..., :half]
    second = tensor[..., half:]
    return jnp.concatenate(
        [first * cosine - second * sine, second * cosine + first * sine], axis=-1
    )


def peer_swap(x, across, ident):
    mesh_kind = pl.DeviceIdType.MESH

    def kernel(x_ref, o_ref, send_sem, recv_sem):
        me = lax.axis_index("head")
        group = lax.axis_index("grp")
        peer = lax.rem(me + 2, 4) if across else me + 1 - 2 * lax.rem(me, 2)
        barrier = pltpu.get_barrier_semaphore()
        pl.semaphore_signal(barrier, inc=1, device_id=(group, peer), device_id_type=mesh_kind)
        pl.semaphore_wait(barrier, 1)
        copy = pltpu.make_async_remote_copy(
            src_ref=x_ref, dst_ref=o_ref, send_sem=send_sem, recv_sem=recv_sem,
            device_id=(group, peer), device_id_type=mesh_kind,
        )
        copy.start()
        copy.wait()

    return pl.pallas_call(
        kernel,
        out_shape=jax.ShapeDtypeStruct(x.shape, x.dtype),
        in_specs=[pl.BlockSpec(memory_space=pl.ANY)],
        out_specs=pl.BlockSpec(memory_space=pl.ANY),
        scratch_shapes=[pltpu.SemaphoreType.DMA(()), pltpu.SemaphoreType.DMA(())],
        compiler_params=pltpu.CompilerParams(collective_id=ident, has_side_effects=True),
    )(x)


def head_gather(x, ident):
    mesh_kind = pl.DeviceIdType.MESH

    def kernel(x_ref, o_ref, own_sem, send_sem, recv_sem):
        me = lax.axis_index("head")
        group = lax.axis_index("grp")
        partner = me + 1 - 2 * lax.rem(me, 2)
        across = lax.rem(me + 2, 4)
        barrier = pltpu.get_barrier_semaphore()
        for peer in (partner, across):
            pl.semaphore_signal(barrier, inc=1, device_id=(group, peer), device_id_type=mesh_kind)
        pl.semaphore_wait(barrier, 2)
        own = pltpu.make_async_copy(x_ref, o_ref.at[me], own_sem)
        own.start()
        near = pltpu.make_async_remote_copy(
            src_ref=x_ref, dst_ref=o_ref.at[me], send_sem=send_sem.at[0], recv_sem=recv_sem.at[0],
            device_id=(group, partner), device_id_type=mesh_kind,
        )
        far = pltpu.make_async_remote_copy(
            src_ref=x_ref, dst_ref=o_ref.at[me], send_sem=send_sem.at[1], recv_sem=recv_sem.at[1],
            device_id=(group, across), device_id_type=mesh_kind,
        )
        near.start()
        far.start()
        far.wait_recv()
        relay = pltpu.make_async_remote_copy(
            src_ref=o_ref.at[across], dst_ref=o_ref.at[across], send_sem=send_sem.at[2],
            recv_sem=recv_sem.at[2], device_id=(group, partner), device_id_type=mesh_kind,
        )
        relay.start()
        own.wait()
        near.wait()
        far.wait_send()
        relay.wait()

    return pl.pallas_call(
        kernel,
        out_shape=jax.ShapeDtypeStruct((4,) + x.shape, x.dtype),
        in_specs=[pl.BlockSpec(memory_space=pl.ANY)],
        out_specs=pl.BlockSpec(memory_space=pl.ANY),
        scratch_shapes=[
            pltpu.SemaphoreType.DMA(()),
            pltpu.SemaphoreType.DMA((3,)),
            pltpu.SemaphoreType.DMA((3,)),
        ],
        compiler_params=pltpu.CompilerParams(collective_id=ident, has_side_effects=True),
    )(x)


def attend(length, query, key_new, value_new, relaid):
    tokens = query.shape[0]
    context = relaid.shape[2]
    heads = query.shape[1] // HD

    def kernel(length_ref, q_ref, kn_ref, vn_ref, k_ref, v_ref, o_ref):
        limit = length_ref[0]
        q = q_ref[...]
        contract = (((1,), (1,)), ((), ()))
        score_old = lax.dot_general(q, k_ref[0, 0], contract, preferred_element_type=jnp.float32)
        score_new = lax.dot_general(q, kn_ref[...], contract, preferred_element_type=jnp.float32)
        allow_old = lax.broadcasted_iota(jnp.int32, score_old.shape, 1) < limit
        allow_new = lax.broadcasted_iota(jnp.int32, score_new.shape, 1) <= lax.broadcasted_iota(
            jnp.int32, score_new.shape, 0
        )
        score_old = jnp.where(allow_old, score_old, -1e30)
        score_new = jnp.where(allow_new, score_new, -1e30)
        top = jnp.maximum(
            jnp.max(score_old, axis=1, keepdims=True), jnp.max(score_new, axis=1, keepdims=True)
        )
        prob_old = jnp.where(allow_old, jnp.exp(score_old - top), 0.0)
        prob_new = jnp.where(allow_new, jnp.exp(score_new - top), 0.0)
        total = jnp.sum(prob_old, axis=1, keepdims=True) + jnp.sum(prob_new, axis=1, keepdims=True)
        numer = jnp.dot(prob_old.astype(jnp.bfloat16), v_ref[0, 0], preferred_element_type=jnp.float32)
        numer = numer + jnp.dot(
            prob_new.astype(jnp.bfloat16), vn_ref[...], preferred_element_type=jnp.float32
        )
        o_ref[...] = (numer / total).astype(o_ref.dtype)

    per_head = pl.BlockSpec((tokens, HD), lambda h, n: (0, h))
    grid_spec = pltpu.PrefetchScalarGridSpec(
        num_scalar_prefetch=1,
        grid=(heads,),
        in_specs=[
            per_head,
            per_head,
            per_head,
            pl.BlockSpec((1, 1, context, HD), lambda h, n: (0, 0, 0, h)),
            pl.BlockSpec((1, 1, context, HD), lambda h, n: (1, 0, 0, h)),
        ],
        out_specs=per_head,
    )
    return pl.pallas_call(
        kernel,
        grid_spec=grid_spec,
        out_shape=jax.ShapeDtypeStruct((tokens, heads * HD), jnp.bfloat16),
    )(length.reshape(1), query, key_new, value_new, relaid, relaid)


def on_device(
    hidden_in,
    attn_gain,
    w_query,
    w_key,
    w_value,
    w_out,
    cache,
    prefix_len,
    mlp_gain,
    expert_ids,
    route_weight,
    w_gate,
    w_up,
    w_down,
):
    group_count = lax.axis_size("grp")
    head_count = lax.axis_size("head")
    my_prompt = lax.axis_index("grp")
    tokens = hidden_in.shape[1]
    width = hidden_in.shape[2]
    heads_here = w_query.shape[1] // HD
    length = prefix_len[my_prompt]
    rows = hidden_in[0].astype(jnp.float32)
    normed = rms_norm(rows, attn_gain).astype(jnp.bfloat16)
    position = (length + jnp.arange(tokens)).astype(jnp.float32)
    query = jnp.dot(normed, w_query, preferred_element_type=jnp.float32).reshape(
        tokens, heads_here, HD
    )
    key_new = jnp.dot(normed, w_key, preferred_element_type=jnp.float32).reshape(
        tokens, heads_here, HD
    )
    value_new = jnp.dot(normed, w_value, preferred_element_type=jnp.float32).reshape(
        tokens, heads_here, HD
    )
    query = (rotate(query, position) * HD ** (-0.5)).astype(jnp.bfloat16)
    key_new = rotate(key_new, position).astype(jnp.bfloat16)
    value_new = value_new.astype(jnp.bfloat16)
    relaid = lax.all_to_all(cache, "grp", split_axis=1, concat_axis=2, tiled=True)
    attended = attend(
        length,
        query.reshape(tokens, heads_here * HD),
        key_new.reshape(tokens, heads_here * HD),
        value_new.reshape(tokens, heads_here * HD),
        relaid,
    )
    projected = jnp.dot(attended, w_out, preferred_element_type=jnp.float32)
    gathered = head_gather(projected.astype(jnp.bfloat16), 0)
    resid = rows + jnp.sum(gathered.astype(jnp.float32), axis=0)
    mixed_in = rms_norm(resid, mlp_gain).astype(jnp.bfloat16)
    experts_here = w_gate.shape[0]
    expert_total = experts_here * group_count
    capacity = max(2, 3 * tokens * TOPK // (2 * expert_total))
    chosen = expert_ids[0].reshape(tokens * TOPK)
    weights = route_weight[0]
    pairs = tokens * TOPK
    slots = expert_total * capacity
    one_hot = (chosen[:, None] == jnp.arange(expert_total)[None, :]).astype(jnp.bfloat16)
    earlier = (jnp.arange(pairs)[None, :] < jnp.arange(pairs)[:, None]).astype(jnp.bfloat16)
    before = jnp.dot(earlier, one_hot, preferred_element_type=jnp.float32)
    slot = jnp.sum(before * one_hot.astype(jnp.float32), axis=1).astype(jnp.int32)
    target = chosen * capacity + slot
    place = (target[:, None] == jnp.arange(slots)[None, :]).reshape(tokens, TOPK, slots)
    dispatch = jnp.sum(place.astype(jnp.float32), axis=1).astype(jnp.bfloat16)
    share_width = width // head_count
    head_at = lax.axis_index("head")
    core = lax.rem(head_at, 2)
    chip = head_at // 2
    other_core = 1 - core
    def halves(array, which):
        split = array.reshape(array.shape[:-1] + (2, 2, share_width))
        taken = lax.dynamic_index_in_dim(split, which, axis=split.ndim - 2, keepdims=False)
        return taken.reshape(array.shape[:-1] + (2 * share_width,))

    def row_halves(array, which):
        split = array.reshape((2, 2, share_width) + array.shape[1:])
        taken = lax.dynamic_index_in_dim(split, which, axis=1, keepdims=False)
        return taken.reshape((2 * share_width,) + array.shape[1:])

    half = 2 * share_width
    outgoing = lax.dot_general(
        dispatch, halves(mixed_in, core), (((0,), (0,)), ((), ())), preferred_element_type=jnp.float32
    ).astype(jnp.bfloat16)
    outgoing = outgoing.reshape(group_count, experts_here, capacity, half)
    arrived = lax.all_to_all(outgoing, "grp", split_axis=0, concat_axis=0, tiled=True)
    arrived_other = peer_swap(arrived, False, 1)
    mine_parts = []
    other_parts = []
    for expert in range(experts_here):
        mine = arrived[:, expert].reshape(group_count * capacity, half)
        other = arrived_other[:, expert].reshape(group_count * capacity, half)
        gate = jnp.dot(mine, row_halves(w_gate[expert], core), preferred_element_type=jnp.float32)
        gate = gate + jnp.dot(other, row_halves(w_gate[expert], other_core), preferred_element_type=jnp.float32)
        upper = jnp.dot(mine, row_halves(w_up[expert], core), preferred_element_type=jnp.float32)
        upper = upper + jnp.dot(other, row_halves(w_up[expert], other_core), preferred_element_type=jnp.float32)
        act = (jax.nn.silu(gate) * upper).astype(jnp.bfloat16)
        mine_parts.append(
            jnp.dot(act, halves(w_down[expert], core), preferred_element_type=jnp.float32)
            .astype(jnp.bfloat16)
            .reshape(group_count, capacity, half)
        )
        other_parts.append(
            jnp.dot(act, halves(w_down[expert], other_core), preferred_element_type=jnp.float32)
            .astype(jnp.bfloat16)
            .reshape(group_count, capacity, half)
        )
    mine_out = jnp.stack(mine_parts, axis=1)
    partner_out = peer_swap(jnp.stack(other_parts, axis=1), False, 2)
    pair_sum = (mine_out.astype(jnp.float32) + partner_out.astype(jnp.float32)).astype(jnp.bfloat16)
    returned = lax.all_to_all(pair_sum, "grp", split_axis=0, concat_axis=0, tiled=True)
    returned = returned.reshape(slots, half)
    weighting = jnp.sum(jnp.where(place, weights[:, :, None], 0.0), axis=1)
    combined = jnp.zeros((tokens, half), jnp.float32)
    for _ in range(3):
        piece = weighting.astype(jnp.bfloat16)
        weighting = weighting - piece.astype(jnp.float32)
        combined = combined + jnp.dot(piece, returned, preferred_element_type=jnp.float32)
    combined = combined.reshape(tokens, 2, share_width)
    keep = lax.dynamic_index_in_dim(combined, chip, axis=1, keepdims=False)
    give = lax.dynamic_index_in_dim(combined, 1 - chip, axis=1, keepdims=False)
    moe_share = keep + peer_swap(give, True, 3)
    resid_share = lax.dynamic_slice_in_dim(resid, head_at * share_width, share_width, 1)
    return (resid_share + moe_share).astype(jnp.bfloat16)[None]


def solution(mesh):
    placed = (
        P("grp", None, None),
        P(),
        P(None, "head"),
        P(None, "head"),
        P(None, "head"),
        P("head", None),
        P(None, None, "grp", "head"),
        P(),
        P(),
        P("grp", None, None),
        P("grp", None, None),
        P("grp", None, "head"),
        P("grp", None, "head"),
        P("grp", "head", None),
    )
    return jax.shard_map(
        on_device, mesh=mesh, in_specs=placed, out_specs=P("grp", None, "head"), check_vma=False
    )
```

```python
import jax
import jax.numpy as jnp
from jax import lax
from jax.experimental import pallas as pl
from jax.experimental.pallas import tpu as pltpu
from jax.sharding import PartitionSpec as P

HD = 128
TOPK = 8


def rms_norm(values, gain):
    scale = lax.rsqrt(jnp.mean(values * values, axis=-1, keepdims=True) + 1e-05)
    return values * scale * gain


def rotate(tensor, position):
    half = HD // 2
    inverse = 10000.0 ** (-(jnp.arange(half).astype(jnp.float32) * 2.0) / HD)
    angle = position[:, None] * inverse[None, :]
    cosine = jnp.cos(angle)[:, None, :]
    sine = jnp.sin(angle)[:, None, :]
    first = tensor[..., :half]
    second = tensor[..., half:]
    return jnp.concatenate(
        [first * cosine - second * sine, second * cosine + first * sine], axis=-1
    )


def peer_swap(x, across, ident):
    mesh_kind = pl.DeviceIdType.MESH

    def kernel(x_ref, o_ref, send_sem, recv_sem):
        me = lax.axis_index("head")
        group = lax.axis_index("grp")
        peer = lax.rem(me + 2, 4) if across else me + 1 - 2 * lax.rem(me, 2)
        barrier = pltpu.get_barrier_semaphore()
        pl.semaphore_signal(barrier, inc=1, device_id=(group, peer), device_id_type=mesh_kind)
        pl.semaphore_wait(barrier, 1)
        copy = pltpu.make_async_remote_copy(
            src_ref=x_ref, dst_ref=o_ref, send_sem=send_sem, recv_sem=recv_sem,
            device_id=(group, peer), device_id_type=mesh_kind,
        )
        copy.start()
        copy.wait()

    return pl.pallas_call(
        kernel,
        out_shape=jax.ShapeDtypeStruct(x.shape, x.dtype),
        in_specs=[pl.BlockSpec(memory_space=pl.ANY)],
        out_specs=pl.BlockSpec(memory_space=pl.ANY),
        scratch_shapes=[pltpu.SemaphoreType.DMA(()), pltpu.SemaphoreType.DMA(())],
        compiler_params=pltpu.CompilerParams(collective_id=ident, has_side_effects=True),
    )(x)


def head_gather(x, ident):
    mesh_kind = pl.DeviceIdType.MESH

    def kernel(x_ref, o_ref, own_sem, send_sem, recv_sem):
        me = lax.axis_index("head")
        group = lax.axis_index("grp")
        partner = me + 1 - 2 * lax.rem(me, 2)
        across = lax.rem(me + 2, 4)
        barrier = pltpu.get_barrier_semaphore()
        for peer in (partner, across):
            pl.semaphore_signal(barrier, inc=1, device_id=(group, peer), device_id_type=mesh_kind)
        pl.semaphore_wait(barrier, 2)
        own = pltpu.make_async_copy(x_ref, o_ref.at[me], own_sem)
        own.start()
        near = pltpu.make_async_remote_copy(
            src_ref=x_ref, dst_ref=o_ref.at[me], send_sem=send_sem.at[0], recv_sem=recv_sem.at[0],
            device_id=(group, partner), device_id_type=mesh_kind,
        )
        far = pltpu.make_async_remote_copy(
            src_ref=x_ref, dst_ref=o_ref.at[me], send_sem=send_sem.at[1], recv_sem=recv_sem.at[1],
            device_id=(group, across), device_id_type=mesh_kind,
        )
        near.start()
        far.start()
        far.wait_recv()
        relay = pltpu.make_async_remote_copy(
            src_ref=o_ref.at[across], dst_ref=o_ref.at[across], send_sem=send_sem.at[2],
            recv_sem=recv_sem.at[2], device_id=(group, partner), device_id_type=mesh_kind,
        )
        relay.start()
        own.wait()
        near.wait()
        far.wait_send()
        relay.wait()

    return pl.pallas_call(
        kernel,
        out_shape=jax.ShapeDtypeStruct((4,) + x.shape, x.dtype),
        in_specs=[pl.BlockSpec(memory_space=pl.ANY)],
        out_specs=pl.BlockSpec(memory_space=pl.ANY),
        scratch_shapes=[
            pltpu.SemaphoreType.DMA(()),
            pltpu.SemaphoreType.DMA((3,)),
            pltpu.SemaphoreType.DMA((3,)),
        ],
        compiler_params=pltpu.CompilerParams(collective_id=ident, has_side_effects=True),
    )(x)


def attend(length, query, key_new, value_new, keys, values):
    tokens = query.shape[0]
    context = keys.shape[0]
    heads = query.shape[1] // HD

    def kernel(length_ref, q_ref, kn_ref, vn_ref, k_ref, v_ref, o_ref):
        limit = length_ref[0]
        q = q_ref[...]
        contract = (((1,), (1,)), ((), ()))
        score_old = lax.dot_general(q, k_ref[...], contract, preferred_element_type=jnp.float32)
        score_new = lax.dot_general(q, kn_ref[...], contract, preferred_element_type=jnp.float32)
        allow_old = lax.broadcasted_iota(jnp.int32, score_old.shape, 1) < limit
        allow_new = lax.broadcasted_iota(jnp.int32, score_new.shape, 1) <= lax.broadcasted_iota(
            jnp.int32, score_new.shape, 0
        )
        score_old = jnp.where(allow_old, score_old, -1e30)
        score_new = jnp.where(allow_new, score_new, -1e30)
        top = jnp.maximum(
            jnp.max(score_old, axis=1, keepdims=True), jnp.max(score_new, axis=1, keepdims=True)
        )
        prob_old = jnp.where(allow_old, jnp.exp(score_old - top), 0.0)
        prob_new = jnp.where(allow_new, jnp.exp(score_new - top), 0.0)
        total = jnp.sum(prob_old, axis=1, keepdims=True) + jnp.sum(prob_new, axis=1, keepdims=True)
        numer = jnp.dot(prob_old.astype(jnp.bfloat16), v_ref[...], preferred_element_type=jnp.float32)
        numer = numer + jnp.dot(
            prob_new.astype(jnp.bfloat16), vn_ref[...], preferred_element_type=jnp.float32
        )
        o_ref[...] = (numer / total).astype(o_ref.dtype)

    per_head = pl.BlockSpec((tokens, HD), lambda h, n: (0, h))
    grid_spec = pltpu.PrefetchScalarGridSpec(
        num_scalar_prefetch=1,
        grid=(heads,),
        in_specs=[
            per_head,
            per_head,
            per_head,
            pl.BlockSpec((context, HD), lambda h, n: (0, h)),
            pl.BlockSpec((context, HD), lambda h, n: (0, h)),
        ],
        out_specs=per_head,
    )
    return pl.pallas_call(
        kernel,
        grid_spec=grid_spec,
        out_shape=jax.ShapeDtypeStruct((tokens, heads * HD), jnp.bfloat16),
    )(length.reshape(1), query, key_new, value_new, keys, values)


def on_device(
    hidden_in,
    attn_gain,
    w_query,
    w_key,
    w_value,
    w_out,
    cache,
    prefix_len,
    mlp_gain,
    expert_ids,
    route_weight,
    w_gate,
    w_up,
    w_down,
):
    group_count = lax.axis_size("grp")
    head_count = lax.axis_size("head")
    my_prompt = lax.axis_index("grp")
    tokens = hidden_in.shape[1]
    width = hidden_in.shape[2]
    heads_here = w_query.shape[1] // HD
    length = prefix_len[my_prompt]
    rows = hidden_in[0].astype(jnp.float32)
    normed = rms_norm(rows, attn_gain).astype(jnp.bfloat16)
    position = (length + jnp.arange(tokens)).astype(jnp.float32)
    query = jnp.dot(normed, w_query, preferred_element_type=jnp.float32).reshape(
        tokens, heads_here, HD
    )
    key_new = jnp.dot(normed, w_key, preferred_element_type=jnp.float32).reshape(
        tokens, heads_here, HD
    )
    value_new = jnp.dot(normed, w_value, preferred_element_type=jnp.float32).reshape(
        tokens, heads_here, HD
    )
    query = (rotate(query, position) * HD ** (-0.5)).astype(jnp.bfloat16)
    key_new = rotate(key_new, position).astype(jnp.bfloat16)
    value_new = value_new.astype(jnp.bfloat16)
    keys, values = [
        lax.all_to_all(cache[part], "grp", split_axis=0, concat_axis=0, tiled=True).reshape(
            group_count * cache.shape[2], heads_here * HD
        )
        for part in range(2)
    ]
    attended = attend(
        length,
        query.reshape(tokens, heads_here * HD),
        key_new.reshape(tokens, heads_here * HD),
        value_new.reshape(tokens, heads_here * HD),
        keys,
        values,
    )
    projected = jnp.dot(attended, w_out, preferred_element_type=jnp.float32)
    gathered = head_gather(projected.astype(jnp.bfloat16), 0)
    resid = rows + jnp.sum(gathered.astype(jnp.float32), axis=0)
    mixed_in = rms_norm(resid, mlp_gain).astype(jnp.bfloat16)
    experts_here = w_gate.shape[0]
    expert_total = experts_here * group_count
    capacity = max(2, 3 * tokens * TOPK // (2 * expert_total))
    chosen = expert_ids[0].reshape(tokens * TOPK)
    weights = route_weight[0]
    pairs = tokens * TOPK
    slots = expert_total * capacity
    one_hot = (chosen[:, None] == jnp.arange(expert_total)[None, :]).astype(jnp.bfloat16)
    earlier = (jnp.arange(pairs)[None, :] < jnp.arange(pairs)[:, None]).astype(jnp.bfloat16)
    before = jnp.dot(earlier, one_hot, preferred_element_type=jnp.float32)
    slot = jnp.sum(before * one_hot.astype(jnp.float32), axis=1).astype(jnp.int32)
    target = chosen * capacity + slot
    place = (target[:, None] == jnp.arange(slots)[None, :]).reshape(tokens, TOPK, slots)
    dispatch = jnp.sum(place.astype(jnp.float32), axis=1).astype(jnp.bfloat16)
    share_width = width // head_count
    head_at = lax.axis_index("head")
    core = lax.rem(head_at, 2)
    chip = head_at // 2
    other_core = 1 - core
    def halves(array, which):
        split = array.reshape(array.shape[:-1] + (2, 2, share_width))
        taken = lax.dynamic_index_in_dim(split, which, axis=split.ndim - 2, keepdims=False)
        return taken.reshape(array.shape[:-1] + (2 * share_width,))

    def row_halves(array, which):
        split = array.reshape((2, 2, share_width) + array.shape[1:])
        taken = lax.dynamic_index_in_dim(split, which, axis=1, keepdims=False)
        return taken.reshape((2 * share_width,) + array.shape[1:])

    half = 2 * share_width
    outgoing = lax.dot_general(
        dispatch, halves(mixed_in, core), (((0,), (0,)), ((), ())), preferred_element_type=jnp.float32
    ).astype(jnp.bfloat16)
    outgoing = outgoing.reshape(group_count, experts_here, capacity, half)
    arrived = lax.all_to_all(outgoing, "grp", split_axis=0, concat_axis=0, tiled=True)
    arrived_other = peer_swap(arrived, False, 1)
    mine_parts = []
    other_parts = []
    for expert in range(experts_here):
        mine = arrived[:, expert].reshape(group_count * capacity, half)
        other = arrived_other[:, expert].reshape(group_count * capacity, half)
        gate = jnp.dot(mine, row_halves(w_gate[expert], core), preferred_element_type=jnp.float32)
        gate = gate + jnp.dot(other, row_halves(w_gate[expert], other_core), preferred_element_type=jnp.float32)
        upper = jnp.dot(mine, row_halves(w_up[expert], core), preferred_element_type=jnp.float32)
        upper = upper + jnp.dot(other, row_halves(w_up[expert], other_core), preferred_element_type=jnp.float32)
        act = (jax.nn.silu(gate) * upper).astype(jnp.bfloat16)
        mine_parts.append(
            jnp.dot(act, halves(w_down[expert], core), preferred_element_type=jnp.float32)
            .astype(jnp.bfloat16)
            .reshape(group_count, capacity, half)
        )
        other_parts.append(
            jnp.dot(act, halves(w_down[expert], other_core), preferred_element_type=jnp.float32)
            .astype(jnp.bfloat16)
            .reshape(group_count, capacity, half)
        )
    mine_out = jnp.stack(mine_parts, axis=1)
    partner_out = peer_swap(jnp.stack(other_parts, axis=1), False, 2)
    pair_sum = (mine_out.astype(jnp.float32) + partner_out.astype(jnp.float32)).astype(jnp.bfloat16)
    returned = lax.all_to_all(pair_sum, "grp", split_axis=0, concat_axis=0, tiled=True)
    returned = returned.reshape(slots, half)
    weighting = jnp.sum(jnp.where(place, weights[:, :, None], 0.0), axis=1)
    combined = jnp.zeros((tokens, half), jnp.float32)
    for _ in range(3):
        piece = weighting.astype(jnp.bfloat16)
        weighting = weighting - piece.astype(jnp.float32)
        combined = combined + jnp.dot(piece, returned, preferred_element_type=jnp.float32)
    combined = combined.reshape(tokens, 2, share_width)
    keep = lax.dynamic_index_in_dim(combined, chip, axis=1, keepdims=False)
    give = lax.dynamic_index_in_dim(combined, 1 - chip, axis=1, keepdims=False)
    moe_share = keep + peer_swap(give, True, 3)
    resid_share = lax.dynamic_slice_in_dim(resid, head_at * share_width, share_width, 1)
    return (resid_share + moe_share).astype(jnp.bfloat16)[None]


def solution(mesh):
    placed = (
        P("grp", None, None),
        P(),
        P(None, "head"),
        P(None, "head"),
        P(None, "head"),
        P("head", None),
        P(None, None, "grp", "head"),
        P(),
        P(),
        P("grp", None, None),
        P("grp", None, None),
        P("grp", None, "head"),
        P("grp", None, "head"),
        P("grp", "head", None),
    )
    return jax.shard_map(
        on_device, mesh=mesh, in_specs=placed, out_specs=P("grp", None, "head"), check_vma=False
    )
```

```python
import jax
import jax.numpy as jnp
from jax import lax
from jax.experimental import pallas as pl
from jax.experimental.pallas import tpu as pltpu
from jax.sharding import PartitionSpec as P

HD = 128
TOPK = 8


def rms_norm(values, gain):
    scale = lax.rsqrt(jnp.mean(values * values, axis=-1, keepdims=True) + 1e-05)
    return values * scale * gain


def rotate(tensor, position):
    half = HD // 2
    inverse = 10000.0 ** (-(jnp.arange(half).astype(jnp.float32) * 2.0) / HD)
    angle = position[:, None] * inverse[None, :]
    cosine = jnp.cos(angle)[:, None, :]
    sine = jnp.sin(angle)[:, None, :]
    first = tensor[..., :half]
    second = tensor[..., half:]
    return jnp.concatenate(
        [first * cosine - second * sine, second * cosine + first * sine], axis=-1
    )


def peer_swap(x, across, ident):
    mesh_kind = pl.DeviceIdType.MESH

    def kernel(x_ref, o_ref, send_sem, recv_sem):
        me = lax.axis_index("head")
        group = lax.axis_index("grp")
        peer = lax.rem(me + 2, 4) if across else me + 1 - 2 * lax.rem(me, 2)
        barrier = pltpu.get_barrier_semaphore()
        pl.semaphore_signal(barrier, inc=1, device_id=(group, peer), device_id_type=mesh_kind)
        pl.semaphore_wait(barrier, 1)
        copy = pltpu.make_async_remote_copy(
            src_ref=x_ref, dst_ref=o_ref, send_sem=send_sem, recv_sem=recv_sem,
            device_id=(group, peer), device_id_type=mesh_kind,
        )
        copy.start()
        copy.wait()

    return pl.pallas_call(
        kernel,
        out_shape=jax.ShapeDtypeStruct(x.shape, x.dtype),
        in_specs=[pl.BlockSpec(memory_space=pl.ANY)],
        out_specs=pl.BlockSpec(memory_space=pl.ANY),
        scratch_shapes=[pltpu.SemaphoreType.DMA(()), pltpu.SemaphoreType.DMA(())],
        compiler_params=pltpu.CompilerParams(collective_id=ident, has_side_effects=True),
    )(x)


def attend(length, query, key_new, value_new, keys, values):
    tokens = query.shape[0]
    context = keys.shape[0]
    heads = query.shape[1] // HD

    def kernel(length_ref, q_ref, kn_ref, vn_ref, k_ref, v_ref, o_ref):
        limit = length_ref[0]
        q = q_ref[...]
        contract = (((1,), (1,)), ((), ()))
        score_old = lax.dot_general(q, k_ref[...], contract, preferred_element_type=jnp.float32)
        score_new = lax.dot_general(q, kn_ref[...], contract, preferred_element_type=jnp.float32)
        allow_old = lax.broadcasted_iota(jnp.int32, score_old.shape, 1) < limit
        allow_new = lax.broadcasted_iota(jnp.int32, score_new.shape, 1) <= lax.broadcasted_iota(
            jnp.int32, score_new.shape, 0
        )
        score_old = jnp.where(allow_old, score_old, -1e30)
        score_new = jnp.where(allow_new, score_new, -1e30)
        top = jnp.maximum(
            jnp.max(score_old, axis=1, keepdims=True), jnp.max(score_new, axis=1, keepdims=True)
        )
        prob_old = jnp.where(allow_old, jnp.exp(score_old - top), 0.0)
        prob_new = jnp.where(allow_new, jnp.exp(score_new - top), 0.0)
        total = jnp.sum(prob_old, axis=1, keepdims=True) + jnp.sum(prob_new, axis=1, keepdims=True)
        numer = jnp.dot(prob_old.astype(jnp.bfloat16), v_ref[...], preferred_element_type=jnp.float32)
        numer = numer + jnp.dot(
            prob_new.astype(jnp.bfloat16), vn_ref[...], preferred_element_type=jnp.float32
        )
        o_ref[...] = (numer / total).astype(o_ref.dtype)

    per_head = pl.BlockSpec((tokens, HD), lambda h, n: (0, h))
    grid_spec = pltpu.PrefetchScalarGridSpec(
        num_scalar_prefetch=1,
        grid=(heads,),
        in_specs=[
            per_head,
            per_head,
            per_head,
            pl.BlockSpec((context, HD), lambda h, n: (0, h)),
            pl.BlockSpec((context, HD), lambda h, n: (0, h)),
        ],
        out_specs=per_head,
    )
    return pl.pallas_call(
        kernel,
        grid_spec=grid_spec,
        out_shape=jax.ShapeDtypeStruct((tokens, heads * HD), jnp.bfloat16),
    )(length.reshape(1), query, key_new, value_new, keys, values)


def head_reduce(x, base, ident):
    mesh_kind = pl.DeviceIdType.MESH

    def kernel(x_ref, base_ref, o_ref, slots, send_sem, recv_sem):
        me = lax.axis_index("head")
        group = lax.axis_index("grp")
        partner = me + 1 - 2 * lax.rem(me, 2)
        across = lax.rem(me + 2, 4)
        barrier = pltpu.get_barrier_semaphore()
        for peer in (partner, across):
            pl.semaphore_signal(barrier, inc=1, device_id=(group, peer), device_id_type=mesh_kind)
        pl.semaphore_wait(barrier, 2)
        near = pltpu.make_async_remote_copy(
            src_ref=x_ref, dst_ref=slots.at[0], send_sem=send_sem.at[0], recv_sem=recv_sem.at[0],
            device_id=(group, partner), device_id_type=mesh_kind,
        )
        far = pltpu.make_async_remote_copy(
            src_ref=x_ref, dst_ref=slots.at[1], send_sem=send_sem.at[1], recv_sem=recv_sem.at[1],
            device_id=(group, across), device_id_type=mesh_kind,
        )
        near.start()
        far.start()
        far.wait_recv()
        relay = pltpu.make_async_remote_copy(
            src_ref=slots.at[1], dst_ref=slots.at[2], send_sem=send_sem.at[2],
            recv_sem=recv_sem.at[2], device_id=(group, partner), device_id_type=mesh_kind,
        )
        relay.start()
        near.wait()
        far.wait_send()
        relay.wait()
        total = base_ref[...] + x_ref[...].astype(jnp.float32)
        for slot in range(3):
            total = total + slots[slot].astype(jnp.float32)
        o_ref[...] = total

    return pl.pallas_call(
        kernel,
        out_shape=jax.ShapeDtypeStruct(x.shape, jnp.float32),
        in_specs=[pl.BlockSpec(memory_space=pltpu.VMEM), pl.BlockSpec(memory_space=pltpu.VMEM)],
        out_specs=pl.BlockSpec(memory_space=pltpu.VMEM),
        scratch_shapes=[
            pltpu.VMEM((3,) + x.shape, x.dtype),
            pltpu.SemaphoreType.DMA((3,)),
            pltpu.SemaphoreType.DMA((3,)),
        ],
        compiler_params=pltpu.CompilerParams(collective_id=ident, has_side_effects=True),
    )(x, base)


def on_device(
    hidden_in,
    attn_gain,
    w_query,
    w_key,
    w_value,
    w_out,
    cache,
    prefix_len,
    mlp_gain,
    expert_ids,
    route_weight,
    w_gate,
    w_up,
    w_down,
):
    group_count = lax.axis_size("grp")
    head_count = lax.axis_size("head")
    my_prompt = lax.axis_index("grp")
    tokens = hidden_in.shape[1]
    width = hidden_in.shape[2]
    heads_here = w_query.shape[1] // HD
    length = prefix_len[my_prompt]
    rows = hidden_in[0].astype(jnp.float32)
    normed = rms_norm(rows, attn_gain).astype(jnp.bfloat16)
    position = (length + jnp.arange(tokens)).astype(jnp.float32)
    query = jnp.dot(normed, w_query, preferred_element_type=jnp.float32).reshape(
        tokens, heads_here, HD
    )
    key_new = jnp.dot(normed, w_key, preferred_element_type=jnp.float32).reshape(
        tokens, heads_here, HD
    )
    value_new = jnp.dot(normed, w_value, preferred_element_type=jnp.float32).reshape(
        tokens, heads_here, HD
    )
    query = (rotate(query, position) * HD ** (-0.5)).astype(jnp.bfloat16)
    key_new = rotate(key_new, position).astype(jnp.bfloat16)
    value_new = value_new.astype(jnp.bfloat16)
    keys, values = [
        lax.all_to_all(cache[part], "grp", split_axis=0, concat_axis=0, tiled=True).reshape(
            group_count * cache.shape[2], heads_here * HD
        )
        for part in range(2)
    ]
    attended = attend(
        length,
        query.reshape(tokens, heads_here * HD),
        key_new.reshape(tokens, heads_here * HD),
        value_new.reshape(tokens, heads_here * HD),
        keys,
        values,
    )
    projected = jnp.dot(attended, w_out, preferred_element_type=jnp.float32)
    resid = head_reduce(projected.astype(jnp.bfloat16), rows, 0)
    mixed_in = rms_norm(resid, mlp_gain).astype(jnp.bfloat16)
    experts_here = w_gate.shape[0]
    expert_total = experts_here * group_count
    capacity = max(2, 3 * tokens * TOPK // (2 * expert_total))
    chosen = expert_ids[0].reshape(tokens * TOPK)
    weights = route_weight[0]
    pairs = tokens * TOPK
    slots = expert_total * capacity
    one_hot = (chosen[:, None] == jnp.arange(expert_total)[None, :]).astype(jnp.bfloat16)
    earlier = (jnp.arange(pairs)[None, :] < jnp.arange(pairs)[:, None]).astype(jnp.bfloat16)
    before = jnp.dot(earlier, one_hot, preferred_element_type=jnp.float32)
    slot = jnp.sum(before * one_hot.astype(jnp.float32), axis=1).astype(jnp.int32)
    target = chosen * capacity + slot
    place = (target[:, None] == jnp.arange(slots)[None, :]).reshape(tokens, TOPK, slots)
    dispatch = jnp.sum(place.astype(jnp.float32), axis=1).astype(jnp.bfloat16)
    share_width = width // head_count
    head_at = lax.axis_index("head")
    core = lax.rem(head_at, 2)
    chip = head_at // 2
    other_core = 1 - core
    def halves(array, which):
        split = array.reshape(array.shape[:-1] + (2, 2, share_width))
        taken = lax.dynamic_index_in_dim(split, which, axis=split.ndim - 2, keepdims=False)
        return taken.reshape(array.shape[:-1] + (2 * share_width,))

    def row_halves(array, which):
        split = array.reshape((2, 2, share_width) + array.shape[1:])
        taken = lax.dynamic_index_in_dim(split, which, axis=1, keepdims=False)
        return taken.reshape((2 * share_width,) + array.shape[1:])

    half = 2 * share_width
    outgoing = lax.dot_general(
        dispatch, halves(mixed_in, core), (((0,), (0,)), ((), ())), preferred_element_type=jnp.float32
    ).astype(jnp.bfloat16)
    outgoing = outgoing.reshape(group_count, experts_here, capacity, half)
    arrived = lax.all_to_all(outgoing, "grp", split_axis=0, concat_axis=0, tiled=True)
    arrived_other = peer_swap(arrived, False, 1)
    mine_parts = []
    other_parts = []
    for expert in range(experts_here):
        mine = arrived[:, expert].reshape(group_count * capacity, half)
        other = arrived_other[:, expert].reshape(group_count * capacity, half)
        gate = jnp.dot(mine, row_halves(w_gate[expert], core), preferred_element_type=jnp.float32)
        gate = gate + jnp.dot(other, row_halves(w_gate[expert], other_core), preferred_element_type=jnp.float32)
        upper = jnp.dot(mine, row_halves(w_up[expert], core), preferred_element_type=jnp.float32)
        upper = upper + jnp.dot(other, row_halves(w_up[expert], other_core), preferred_element_type=jnp.float32)
        act = (jax.nn.silu(gate) * upper).astype(jnp.bfloat16)
        mine_parts.append(
            jnp.dot(act, halves(w_down[expert], core), preferred_element_type=jnp.float32)
            .astype(jnp.bfloat16)
            .reshape(group_count, capacity, half)
        )
        other_parts.append(
            jnp.dot(act, halves(w_down[expert], other_core), preferred_element_type=jnp.float32)
            .astype(jnp.bfloat16)
            .reshape(group_count, capacity, half)
        )
    mine_out = jnp.stack(mine_parts, axis=1)
    partner_out = peer_swap(jnp.stack(other_parts, axis=1), False, 2)
    pair_sum = (mine_out.astype(jnp.float32) + partner_out.astype(jnp.float32)).astype(jnp.bfloat16)
    returned = lax.all_to_all(pair_sum, "grp", split_axis=0, concat_axis=0, tiled=True)
    returned = returned.reshape(slots, half)
    weighting = jnp.sum(jnp.where(place, weights[:, :, None], 0.0), axis=1)
    pieces = []
    for _ in range(3):
        piece = weighting.astype(jnp.bfloat16)
        weighting = weighting - piece.astype(jnp.float32)
        pieces.append(piece)
    combined = jnp.dot(jnp.concatenate(pieces, axis=0), returned, preferred_element_type=jnp.float32)
    combined = combined.reshape(3, tokens, half).sum(axis=0)
    combined = combined.reshape(tokens, 2, share_width)
    keep = lax.dynamic_index_in_dim(combined, chip, axis=1, keepdims=False)
    give = lax.dynamic_index_in_dim(combined, 1 - chip, axis=1, keepdims=False)
    moe_share = keep + peer_swap(give, True, 3)
    resid_share = lax.dynamic_slice_in_dim(resid, head_at * share_width, share_width, 1)
    return (resid_share + moe_share).astype(jnp.bfloat16)[None]


def solution(mesh):
    placed = (
        P("grp", None, None),
        P(),
        P(None, "head"),
        P(None, "head"),
        P(None, "head"),
        P("head", None),
        P(None, None, "grp", "head"),
        P(),
        P(),
        P("grp", None, None),
        P("grp", None, None),
        P("grp", None, "head"),
        P("grp", None, "head"),
        P("grp", "head", None),
    )
    return jax.shard_map(
        on_device, mesh=mesh, in_specs=placed, out_specs=P("grp", None, "head"), check_vma=False
    )
```

```python
import jax
import jax.numpy as jnp
from jax import lax
from jax.experimental import pallas as pl
from jax.experimental.pallas import tpu as pltpu
from jax.sharding import PartitionSpec as P

HD = 128
TOPK = 8


def rms_norm(values, gain):
    scale = lax.rsqrt(jnp.mean(values * values, axis=-1, keepdims=True) + 1e-05)
    return values * scale * gain


def rotate(tensor, position):
    half = HD // 2
    inverse = 10000.0 ** (-(jnp.arange(half).astype(jnp.float32) * 2.0) / HD)
    angle = position[:, None] * inverse[None, :]
    cosine = jnp.cos(angle)[:, None, :]
    sine = jnp.sin(angle)[:, None, :]
    first = tensor[..., :half]
    second = tensor[..., half:]
    return jnp.concatenate(
        [first * cosine - second * sine, second * cosine + first * sine], axis=-1
    )


def peer_swap(x, across, ident):
    mesh_kind = pl.DeviceIdType.MESH

    def kernel(x_ref, o_ref, send_sem, recv_sem):
        me = lax.axis_index("head")
        group = lax.axis_index("grp")
        peer = lax.rem(me + 2, 4) if across else me + 1 - 2 * lax.rem(me, 2)
        barrier = pltpu.get_barrier_semaphore()
        pl.semaphore_signal(barrier, inc=1, device_id=(group, peer), device_id_type=mesh_kind)
        pl.semaphore_wait(barrier, 1)
        copy = pltpu.make_async_remote_copy(
            src_ref=x_ref, dst_ref=o_ref, send_sem=send_sem, recv_sem=recv_sem,
            device_id=(group, peer), device_id_type=mesh_kind,
        )
        copy.start()
        copy.wait()

    return pl.pallas_call(
        kernel,
        out_shape=jax.ShapeDtypeStruct(x.shape, x.dtype),
        in_specs=[pl.BlockSpec(memory_space=pl.ANY)],
        out_specs=pl.BlockSpec(memory_space=pl.ANY),
        scratch_shapes=[pltpu.SemaphoreType.DMA(()), pltpu.SemaphoreType.DMA(())],
        compiler_params=pltpu.CompilerParams(collective_id=ident, has_side_effects=True),
    )(x)


def attend(length, query, key_new, value_new, keys, values):
    tokens = query.shape[0]
    context = keys.shape[0]
    heads = query.shape[1] // HD

    def kernel(length_ref, q_ref, kn_ref, vn_ref, k_ref, v_ref, o_ref):
        limit = length_ref[0]
        q = q_ref[...]
        contract = (((1,), (1,)), ((), ()))
        score_old = lax.dot_general(q, k_ref[...], contract, preferred_element_type=jnp.float32)
        score_new = lax.dot_general(q, kn_ref[...], contract, preferred_element_type=jnp.float32)
        allow_old = lax.broadcasted_iota(jnp.int32, score_old.shape, 1) < limit
        allow_new = lax.broadcasted_iota(jnp.int32, score_new.shape, 1) <= lax.broadcasted_iota(
            jnp.int32, score_new.shape, 0
        )
        score_old = jnp.where(allow_old, score_old, -1e30)
        score_new = jnp.where(allow_new, score_new, -1e30)
        top = jnp.maximum(
            jnp.max(score_old, axis=1, keepdims=True), jnp.max(score_new, axis=1, keepdims=True)
        )
        prob_old = jnp.where(allow_old, jnp.exp(score_old - top), 0.0)
        prob_new = jnp.where(allow_new, jnp.exp(score_new - top), 0.0)
        total = jnp.sum(prob_old, axis=1, keepdims=True) + jnp.sum(prob_new, axis=1, keepdims=True)
        numer = jnp.dot(prob_old.astype(jnp.bfloat16), v_ref[...], preferred_element_type=jnp.float32)
        numer = numer + jnp.dot(
            prob_new.astype(jnp.bfloat16), vn_ref[...], preferred_element_type=jnp.float32
        )
        o_ref[...] = (numer / total).astype(o_ref.dtype)

    per_head = pl.BlockSpec((tokens, HD), lambda h, n: (0, h))
    grid_spec = pltpu.PrefetchScalarGridSpec(
        num_scalar_prefetch=1,
        grid=(heads,),
        in_specs=[
            per_head,
            per_head,
            per_head,
            pl.BlockSpec((context, HD), lambda h, n: (0, h)),
            pl.BlockSpec((context, HD), lambda h, n: (0, h)),
        ],
        out_specs=per_head,
    )
    return pl.pallas_call(
        kernel,
        grid_spec=grid_spec,
        out_shape=jax.ShapeDtypeStruct((tokens, heads * HD), jnp.bfloat16),
    )(length.reshape(1), query, key_new, value_new, keys, values)


def head_reduce(x, base, ident):
    mesh_kind = pl.DeviceIdType.MESH

    def kernel(x_ref, base_ref, o_ref, slots, send_sem, recv_sem):
        me = lax.axis_index("head")
        group = lax.axis_index("grp")
        partner = me + 1 - 2 * lax.rem(me, 2)
        across = lax.rem(me + 2, 4)
        barrier = pltpu.get_barrier_semaphore()
        for peer in (partner, across):
            pl.semaphore_signal(barrier, inc=1, device_id=(group, peer), device_id_type=mesh_kind)
        pl.semaphore_wait(barrier, 2)
        near = pltpu.make_async_remote_copy(
            src_ref=x_ref, dst_ref=slots.at[0], send_sem=send_sem.at[0], recv_sem=recv_sem.at[0],
            device_id=(group, partner), device_id_type=mesh_kind,
        )
        far = pltpu.make_async_remote_copy(
            src_ref=x_ref, dst_ref=slots.at[1], send_sem=send_sem.at[1], recv_sem=recv_sem.at[1],
            device_id=(group, across), device_id_type=mesh_kind,
        )
        near.start()
        far.start()
        far.wait_recv()
        relay = pltpu.make_async_remote_copy(
            src_ref=slots.at[1], dst_ref=slots.at[2], send_sem=send_sem.at[2],
            recv_sem=recv_sem.at[2], device_id=(group, partner), device_id_type=mesh_kind,
        )
        relay.start()
        near.wait()
        far.wait_send()
        relay.wait()
        total = base_ref[...] + x_ref[...].astype(jnp.float32)
        for slot in range(3):
            total = total + slots[slot].astype(jnp.float32)
        o_ref[...] = total

    return pl.pallas_call(
        kernel,
        out_shape=jax.ShapeDtypeStruct(x.shape, jnp.float32),
        in_specs=[pl.BlockSpec(memory_space=pltpu.VMEM), pl.BlockSpec(memory_space=pltpu.VMEM)],
        out_specs=pl.BlockSpec(memory_space=pltpu.VMEM),
        scratch_shapes=[
            pltpu.VMEM((3,) + x.shape, x.dtype),
            pltpu.SemaphoreType.DMA((3,)),
            pltpu.SemaphoreType.DMA((3,)),
        ],
        compiler_params=pltpu.CompilerParams(collective_id=ident, has_side_effects=True),
    )(x, base)


def on_device(
    hidden_in,
    attn_gain,
    w_query,
    w_key,
    w_value,
    w_out,
    cache,
    prefix_len,
    mlp_gain,
    expert_ids,
    route_weight,
    w_gate,
    w_up,
    w_down,
):
    group_count = lax.axis_size("grp")
    head_count = lax.axis_size("head")
    my_prompt = lax.axis_index("grp")
    tokens = hidden_in.shape[1]
    width = hidden_in.shape[2]
    heads_here = w_query.shape[1] // HD
    length = prefix_len[my_prompt]
    rows = hidden_in[0].astype(jnp.float32)
    normed = rms_norm(rows, attn_gain).astype(jnp.bfloat16)
    position = (length + jnp.arange(tokens)).astype(jnp.float32)
    query = jnp.dot(normed, w_query, preferred_element_type=jnp.float32).reshape(
        tokens, heads_here, HD
    )
    key_new = jnp.dot(normed, w_key, preferred_element_type=jnp.float32).reshape(
        tokens, heads_here, HD
    )
    value_new = jnp.dot(normed, w_value, preferred_element_type=jnp.float32).reshape(
        tokens, heads_here, HD
    )
    query = (rotate(query, position) * HD ** (-0.5)).astype(jnp.bfloat16)
    key_new = rotate(key_new, position).astype(jnp.bfloat16)
    value_new = value_new.astype(jnp.bfloat16)
    keys, values = [
        lax.all_to_all(cache[part], "grp", split_axis=0, concat_axis=0, tiled=True).reshape(
            group_count * cache.shape[2], heads_here * HD
        )
        for part in range(2)
    ]
    attended = attend(
        length,
        query.reshape(tokens, heads_here * HD),
        key_new.reshape(tokens, heads_here * HD),
        value_new.reshape(tokens, heads_here * HD),
        keys,
        values,
    )
    projected = jnp.dot(attended, w_out, preferred_element_type=jnp.float32)
    resid = head_reduce(projected.astype(jnp.bfloat16), rows, 0)
    mixed_in = rms_norm(resid, mlp_gain).astype(jnp.bfloat16)
    experts_here = w_gate.shape[0]
    expert_total = experts_here * group_count
    capacity = max(2, 3 * tokens * TOPK // (2 * expert_total))
    chosen = expert_ids[0].reshape(tokens * TOPK)
    weights = route_weight[0]
    pairs = tokens * TOPK
    slots = expert_total * capacity
    one_hot = (chosen[:, None] == jnp.arange(expert_total)[None, :]).astype(jnp.bfloat16)
    earlier = (jnp.arange(pairs)[None, :] < jnp.arange(pairs)[:, None]).astype(jnp.bfloat16)
    before = jnp.dot(earlier, one_hot, preferred_element_type=jnp.float32)
    slot = jnp.sum(before * one_hot.astype(jnp.float32), axis=1).astype(jnp.int32)
    target = chosen * capacity + slot
    place = (target[:, None] == jnp.arange(slots)[None, :]).reshape(tokens, TOPK, slots)
    dispatch = jnp.sum(place.astype(jnp.float32), axis=1).astype(jnp.bfloat16)
    share_width = width // head_count
    head_at = lax.axis_index("head")
    core = lax.rem(head_at, 2)
    chip = head_at // 2
    other_core = 1 - core
    def halves(array, which):
        split = array.reshape(array.shape[:-1] + (2, 2, share_width))
        taken = lax.dynamic_index_in_dim(split, which, axis=split.ndim - 2, keepdims=False)
        return taken.reshape(array.shape[:-1] + (2 * share_width,))

    def row_halves(array, which):
        split = array.reshape((2, 2, share_width) + array.shape[1:])
        taken = lax.dynamic_index_in_dim(split, which, axis=1, keepdims=False)
        return taken.reshape((2 * share_width,) + array.shape[1:])

    half = 2 * share_width
    outgoing = lax.dot_general(
        dispatch, halves(mixed_in, core), (((0,), (0,)), ((), ())), preferred_element_type=jnp.float32
    ).astype(jnp.bfloat16)
    outgoing = outgoing.reshape(group_count, experts_here, capacity, half)
    arrived = lax.all_to_all(outgoing, "grp", split_axis=0, concat_axis=0, tiled=True)
    partners = [(index, index ^ 1) for index in range(head_count)]
    arrived_other = [
        lax.ppermute(arrived[:, expert], "head", partners) for expert in range(experts_here)
    ]
    pair_sums = []
    for expert in range(experts_here):
        mine = arrived[:, expert].reshape(group_count * capacity, half)
        other = arrived_other[expert].reshape(group_count * capacity, half)
        gate = jnp.dot(mine, row_halves(w_gate[expert], core), preferred_element_type=jnp.float32)
        gate = gate + jnp.dot(other, row_halves(w_gate[expert], other_core), preferred_element_type=jnp.float32)
        upper = jnp.dot(mine, row_halves(w_up[expert], core), preferred_element_type=jnp.float32)
        upper = upper + jnp.dot(other, row_halves(w_up[expert], other_core), preferred_element_type=jnp.float32)
        act = (jax.nn.silu(gate) * upper).astype(jnp.bfloat16)
        mine_part = jnp.dot(act, halves(w_down[expert], core), preferred_element_type=jnp.float32)
        other_part = jnp.dot(act, halves(w_down[expert], other_core), preferred_element_type=jnp.float32)
        partner_part = lax.ppermute(other_part.astype(jnp.bfloat16), "head", partners)
        pair_sums.append(
            (mine_part.astype(jnp.bfloat16).astype(jnp.float32) + partner_part.astype(jnp.float32))
            .astype(jnp.bfloat16)
            .reshape(group_count, capacity, half)
        )
    pair_sum = jnp.stack(pair_sums, axis=1)
    returned = lax.all_to_all(pair_sum, "grp", split_axis=0, concat_axis=0, tiled=True)
    returned = returned.reshape(slots, half)
    weighting = jnp.sum(jnp.where(place, weights[:, :, None], 0.0), axis=1)
    pieces = []
    for _ in range(3):
        piece = weighting.astype(jnp.bfloat16)
        weighting = weighting - piece.astype(jnp.float32)
        pieces.append(piece)
    combined = jnp.dot(jnp.concatenate(pieces, axis=0), returned, preferred_element_type=jnp.float32)
    combined = combined.reshape(3, tokens, half).sum(axis=0)
    combined = combined.reshape(tokens, 2, share_width)
    keep = lax.dynamic_index_in_dim(combined, chip, axis=1, keepdims=False)
    give = lax.dynamic_index_in_dim(combined, 1 - chip, axis=1, keepdims=False)
    moe_share = keep + peer_swap(give, True, 3)
    resid_share = lax.dynamic_slice_in_dim(resid, head_at * share_width, share_width, 1)
    return (resid_share + moe_share).astype(jnp.bfloat16)[None]


def solution(mesh):
    placed = (
        P("grp", None, None),
        P(),
        P(None, "head"),
        P(None, "head"),
        P(None, "head"),
        P("head", None),
        P(None, None, "grp", "head"),
        P(),
        P(),
        P("grp", None, None),
        P("grp", None, None),
        P("grp", None, "head"),
        P("grp", None, "head"),
        P("grp", "head", None),
    )
    return jax.shard_map(
        on_device, mesh=mesh, in_specs=placed, out_specs=P("grp", None, "head"), check_vma=False
    )
```

```python
import jax
import jax.numpy as jnp
from jax import lax
from jax.experimental import pallas as pl
from jax.experimental.pallas import tpu as pltpu
from jax.sharding import PartitionSpec as P

HD = 128
TOPK = 8


def rms_norm(values, gain):
    scale = lax.rsqrt(jnp.mean(values * values, axis=-1, keepdims=True) + 1e-05)
    return values * scale * gain


def rotate(tensor, position):
    half = HD // 2
    inverse = 10000.0 ** (-(jnp.arange(half).astype(jnp.float32) * 2.0) / HD)
    angle = position[:, None] * inverse[None, :]
    cosine = jnp.cos(angle)[:, None, :]
    sine = jnp.sin(angle)[:, None, :]
    first = tensor[..., :half]
    second = tensor[..., half:]
    return jnp.concatenate(
        [first * cosine - second * sine, second * cosine + first * sine], axis=-1
    )


def peer_swap(x, across, ident):
    mesh_kind = pl.DeviceIdType.MESH

    def kernel(x_ref, o_ref, send_sem, recv_sem):
        me = lax.axis_index("head")
        group = lax.axis_index("grp")
        peer = lax.rem(me + 2, 4) if across else me + 1 - 2 * lax.rem(me, 2)
        barrier = pltpu.get_barrier_semaphore()
        pl.semaphore_signal(barrier, inc=1, device_id=(group, peer), device_id_type=mesh_kind)
        pl.semaphore_wait(barrier, 1)
        copy = pltpu.make_async_remote_copy(
            src_ref=x_ref, dst_ref=o_ref, send_sem=send_sem, recv_sem=recv_sem,
            device_id=(group, peer), device_id_type=mesh_kind,
        )
        copy.start()
        copy.wait()

    return pl.pallas_call(
        kernel,
        out_shape=jax.ShapeDtypeStruct(x.shape, x.dtype),
        in_specs=[pl.BlockSpec(memory_space=pl.ANY)],
        out_specs=pl.BlockSpec(memory_space=pl.ANY),
        scratch_shapes=[pltpu.SemaphoreType.DMA(()), pltpu.SemaphoreType.DMA(())],
        compiler_params=pltpu.CompilerParams(collective_id=ident, has_side_effects=True),
    )(x)


def attend(length, query, key_new, value_new, keys, values):
    tokens = query.shape[0]
    context = keys.shape[0]
    heads = query.shape[1] // HD

    def kernel(length_ref, q_ref, kn_ref, vn_ref, k_ref, v_ref, o_ref):
        limit = length_ref[0]
        q = q_ref[...]
        contract = (((1,), (1,)), ((), ()))
        score_old = lax.dot_general(q, k_ref[...], contract, preferred_element_type=jnp.float32)
        score_new = lax.dot_general(q, kn_ref[...], contract, preferred_element_type=jnp.float32)
        allow_old = lax.broadcasted_iota(jnp.int32, score_old.shape, 1) < limit
        allow_new = lax.broadcasted_iota(jnp.int32, score_new.shape, 1) <= lax.broadcasted_iota(
            jnp.int32, score_new.shape, 0
        )
        score_old = jnp.where(allow_old, score_old, -1e30)
        score_new = jnp.where(allow_new, score_new, -1e30)
        top = jnp.maximum(
            jnp.max(score_old, axis=1, keepdims=True), jnp.max(score_new, axis=1, keepdims=True)
        )
        prob_old = jnp.where(allow_old, jnp.exp(score_old - top), 0.0)
        prob_new = jnp.where(allow_new, jnp.exp(score_new - top), 0.0)
        total = jnp.sum(prob_old, axis=1, keepdims=True) + jnp.sum(prob_new, axis=1, keepdims=True)
        numer = jnp.dot(prob_old.astype(jnp.bfloat16), v_ref[...], preferred_element_type=jnp.float32)
        numer = numer + jnp.dot(
            prob_new.astype(jnp.bfloat16), vn_ref[...], preferred_element_type=jnp.float32
        )
        o_ref[...] = (numer / total).astype(o_ref.dtype)

    per_head = pl.BlockSpec((tokens, HD), lambda h, n: (0, h))
    grid_spec = pltpu.PrefetchScalarGridSpec(
        num_scalar_prefetch=1,
        grid=(heads,),
        in_specs=[
            per_head,
            per_head,
            per_head,
            pl.BlockSpec((context, HD), lambda h, n: (0, h)),
            pl.BlockSpec((context, HD), lambda h, n: (0, h)),
        ],
        out_specs=per_head,
    )
    return pl.pallas_call(
        kernel,
        grid_spec=grid_spec,
        out_shape=jax.ShapeDtypeStruct((tokens, heads * HD), jnp.bfloat16),
    )(length.reshape(1), query, key_new, value_new, keys, values)


def head_reduce(x, base, ident):
    mesh_kind = pl.DeviceIdType.MESH

    def kernel(x_ref, base_ref, o_ref, slots, send_sem, recv_sem):
        me = lax.axis_index("head")
        group = lax.axis_index("grp")
        partner = me + 1 - 2 * lax.rem(me, 2)
        across = lax.rem(me + 2, 4)
        barrier = pltpu.get_barrier_semaphore()
        for peer in (partner, across):
            pl.semaphore_signal(barrier, inc=1, device_id=(group, peer), device_id_type=mesh_kind)
        pl.semaphore_wait(barrier, 2)
        near = pltpu.make_async_remote_copy(
            src_ref=x_ref, dst_ref=slots.at[0], send_sem=send_sem.at[0], recv_sem=recv_sem.at[0],
            device_id=(group, partner), device_id_type=mesh_kind,
        )
        far = pltpu.make_async_remote_copy(
            src_ref=x_ref, dst_ref=slots.at[1], send_sem=send_sem.at[1], recv_sem=recv_sem.at[1],
            device_id=(group, across), device_id_type=mesh_kind,
        )
        near.start()
        far.start()
        far.wait_recv()
        relay = pltpu.make_async_remote_copy(
            src_ref=slots.at[1], dst_ref=slots.at[2], send_sem=send_sem.at[2],
            recv_sem=recv_sem.at[2], device_id=(group, partner), device_id_type=mesh_kind,
        )
        relay.start()
        near.wait()
        far.wait_send()
        relay.wait()
        total = base_ref[...] + x_ref[...].astype(jnp.float32)
        for slot in range(3):
            total = total + slots[slot].astype(jnp.float32)
        o_ref[...] = total

    return pl.pallas_call(
        kernel,
        out_shape=jax.ShapeDtypeStruct(x.shape, jnp.float32),
        in_specs=[pl.BlockSpec(memory_space=pltpu.VMEM), pl.BlockSpec(memory_space=pltpu.VMEM)],
        out_specs=pl.BlockSpec(memory_space=pltpu.VMEM),
        scratch_shapes=[
            pltpu.VMEM((3,) + x.shape, x.dtype),
            pltpu.SemaphoreType.DMA((3,)),
            pltpu.SemaphoreType.DMA((3,)),
        ],
        compiler_params=pltpu.CompilerParams(collective_id=ident, has_side_effects=True),
    )(x, base)


def on_device(
    hidden_in,
    attn_gain,
    w_query,
    w_key,
    w_value,
    w_out,
    cache,
    prefix_len,
    mlp_gain,
    expert_ids,
    route_weight,
    w_gate,
    w_up,
    w_down,
):
    group_count = lax.axis_size("grp")
    head_count = lax.axis_size("head")
    my_prompt = lax.axis_index("grp")
    tokens = hidden_in.shape[1]
    width = hidden_in.shape[2]
    heads_here = w_query.shape[1] // HD
    length = prefix_len[my_prompt]
    rows = hidden_in[0].astype(jnp.float32)
    normed = rms_norm(rows, attn_gain).astype(jnp.bfloat16)
    position = (length + jnp.arange(tokens)).astype(jnp.float32)
    query = jnp.dot(normed, w_query, preferred_element_type=jnp.float32).reshape(
        tokens, heads_here, HD
    )
    key_new = jnp.dot(normed, w_key, preferred_element_type=jnp.float32).reshape(
        tokens, heads_here, HD
    )
    value_new = jnp.dot(normed, w_value, preferred_element_type=jnp.float32).reshape(
        tokens, heads_here, HD
    )
    query = (rotate(query, position) * HD ** (-0.5)).astype(jnp.bfloat16)
    key_new = rotate(key_new, position).astype(jnp.bfloat16)
    value_new = value_new.astype(jnp.bfloat16)
    keys, values = [
        lax.all_to_all(cache[part], "grp", split_axis=0, concat_axis=0, tiled=True).reshape(
            group_count * cache.shape[2], heads_here * HD
        )
        for part in range(2)
    ]
    attended = attend(
        length,
        query.reshape(tokens, heads_here * HD),
        key_new.reshape(tokens, heads_here * HD),
        value_new.reshape(tokens, heads_here * HD),
        keys,
        values,
    )
    projected = jnp.dot(attended, w_out, preferred_element_type=jnp.float32)
    resid = head_reduce(projected.astype(jnp.bfloat16), rows, 0)
    mixed_in = rms_norm(resid, mlp_gain).astype(jnp.bfloat16)
    experts_here = w_gate.shape[0]
    expert_total = experts_here * group_count
    capacity = max(2, 3 * tokens * TOPK // (2 * expert_total))
    chosen = expert_ids[0].reshape(tokens * TOPK)
    weights = route_weight[0]
    pairs = tokens * TOPK
    slots = expert_total * capacity
    one_hot = (chosen[:, None] == jnp.arange(expert_total)[None, :]).astype(jnp.bfloat16)
    earlier = (jnp.arange(pairs)[None, :] < jnp.arange(pairs)[:, None]).astype(jnp.bfloat16)
    before = jnp.dot(earlier, one_hot, preferred_element_type=jnp.float32)
    slot = jnp.sum(before * one_hot.astype(jnp.float32), axis=1).astype(jnp.int32)
    target = chosen * capacity + slot
    place = (target[:, None] == jnp.arange(slots)[None, :]).reshape(tokens, TOPK, slots)
    dispatch = jnp.sum(place.astype(jnp.float32), axis=1).astype(jnp.bfloat16)
    share_width = width // head_count
    head_at = lax.axis_index("head")
    core = lax.rem(head_at, 2)
    chip = head_at // 2
    other_core = 1 - core
    def halves(array, which):
        split = array.reshape(array.shape[:-1] + (2, 2, share_width))
        taken = lax.dynamic_index_in_dim(split, which, axis=split.ndim - 2, keepdims=False)
        return taken.reshape(array.shape[:-1] + (2 * share_width,))

    def row_halves(array, which):
        split = array.reshape((2, 2, share_width) + array.shape[1:])
        taken = lax.dynamic_index_in_dim(split, which, axis=1, keepdims=False)
        return taken.reshape((2 * share_width,) + array.shape[1:])

    half = 2 * share_width
    outgoing = lax.dot_general(
        dispatch, halves(mixed_in, core), (((0,), (0,)), ((), ())), preferred_element_type=jnp.float32
    ).astype(jnp.bfloat16)
    outgoing = outgoing.reshape(group_count, experts_here, capacity, half)
    arrived = lax.all_to_all(outgoing, "grp", split_axis=0, concat_axis=0, tiled=True)
    partners = [(index, index ^ 1) for index in range(head_count)]
    arrived_other = lax.ppermute(arrived, "head", partners)
    pair_sums = []
    for expert in range(experts_here):
        mine = arrived[:, expert].reshape(group_count * capacity, half)
        other = arrived_other[:, expert].reshape(group_count * capacity, half)
        gate = jnp.dot(mine, row_halves(w_gate[expert], core), preferred_element_type=jnp.float32)
        gate = gate + jnp.dot(other, row_halves(w_gate[expert], other_core), preferred_element_type=jnp.float32)
        upper = jnp.dot(mine, row_halves(w_up[expert], core), preferred_element_type=jnp.float32)
        upper = upper + jnp.dot(other, row_halves(w_up[expert], other_core), preferred_element_type=jnp.float32)
        act = (jax.nn.silu(gate) * upper).astype(jnp.bfloat16)
        mine_part = jnp.dot(act, halves(w_down[expert], core), preferred_element_type=jnp.float32)
        other_part = jnp.dot(act, halves(w_down[expert], other_core), preferred_element_type=jnp.float32)
        partner_part = lax.ppermute(other_part.astype(jnp.bfloat16), "head", partners)
        pair_sums.append(
            (mine_part.astype(jnp.bfloat16).astype(jnp.float32) + partner_part.astype(jnp.float32))
            .astype(jnp.bfloat16)
            .reshape(group_count, capacity, half)
        )
    pair_sum = jnp.stack(pair_sums, axis=1)
    returned = lax.all_to_all(pair_sum, "grp", split_axis=0, concat_axis=0, tiled=True)
    returned = returned.reshape(slots, half)
    weighting = jnp.sum(jnp.where(place, weights[:, :, None], 0.0), axis=1)
    pieces = []
    for _ in range(3):
        piece = weighting.astype(jnp.bfloat16)
        weighting = weighting - piece.astype(jnp.float32)
        pieces.append(piece)
    combined = jnp.dot(jnp.concatenate(pieces, axis=0), returned, preferred_element_type=jnp.float32)
    combined = combined.reshape(3, tokens, half).sum(axis=0)
    combined = combined.reshape(tokens, 2, share_width)
    keep = lax.dynamic_index_in_dim(combined, chip, axis=1, keepdims=False)
    give = lax.dynamic_index_in_dim(combined, 1 - chip, axis=1, keepdims=False)
    moe_share = keep + peer_swap(give, True, 3)
    resid_share = lax.dynamic_slice_in_dim(resid, head_at * share_width, share_width, 1)
    return (resid_share + moe_share).astype(jnp.bfloat16)[None]


def solution(mesh):
    placed = (
        P("grp", None, None),
        P(),
        P(None, "head"),
        P(None, "head"),
        P(None, "head"),
        P("head", None),
        P(None, None, "grp", "head"),
        P(),
        P(),
        P("grp", None, None),
        P("grp", None, None),
        P("grp", None, "head"),
        P("grp", None, "head"),
        P("grp", "head", None),
    )
    return jax.shard_map(
        on_device, mesh=mesh, in_specs=placed, out_specs=P("grp", None, "head"), check_vma=False
    )
```

```python
import jax
import jax.numpy as jnp
from jax import lax
from jax.experimental import pallas as pl
from jax.experimental.pallas import tpu as pltpu
from jax.sharding import PartitionSpec as P

HD = 128
TOPK = 8


def rms_norm(values, gain):
    scale = lax.rsqrt(jnp.mean(values * values, axis=-1, keepdims=True) + 1e-05)
    return values * scale * gain


def rotate(tensor, position):
    half = HD // 2
    inverse = 10000.0 ** (-(jnp.arange(half).astype(jnp.float32) * 2.0) / HD)
    angle = position[:, None] * inverse[None, :]
    cosine = jnp.cos(angle)[:, None, :]
    sine = jnp.sin(angle)[:, None, :]
    first = tensor[..., :half]
    second = tensor[..., half:]
    return jnp.concatenate(
        [first * cosine - second * sine, second * cosine + first * sine], axis=-1
    )


def peer_swap(x, across, ident):
    mesh_kind = pl.DeviceIdType.MESH

    def kernel(x_ref, o_ref, send_sem, recv_sem):
        me = lax.axis_index("head")
        group = lax.axis_index("grp")
        peer = lax.rem(me + 2, 4) if across else me + 1 - 2 * lax.rem(me, 2)
        barrier = pltpu.get_barrier_semaphore()
        pl.semaphore_signal(barrier, inc=1, device_id=(group, peer), device_id_type=mesh_kind)
        pl.semaphore_wait(barrier, 1)
        copy = pltpu.make_async_remote_copy(
            src_ref=x_ref, dst_ref=o_ref, send_sem=send_sem, recv_sem=recv_sem,
            device_id=(group, peer), device_id_type=mesh_kind,
        )
        copy.start()
        copy.wait()

    return pl.pallas_call(
        kernel,
        out_shape=jax.ShapeDtypeStruct(x.shape, x.dtype),
        in_specs=[pl.BlockSpec(memory_space=pl.ANY)],
        out_specs=pl.BlockSpec(memory_space=pl.ANY),
        scratch_shapes=[pltpu.SemaphoreType.DMA(()), pltpu.SemaphoreType.DMA(())],
        compiler_params=pltpu.CompilerParams(collective_id=ident, has_side_effects=True),
    )(x)


def attend(length, query, key_new, value_new, keys, values):
    tokens = query.shape[0]
    context = keys.shape[0]
    heads = query.shape[1] // HD

    def kernel(length_ref, q_ref, kn_ref, vn_ref, k_ref, v_ref, o_ref):
        limit = length_ref[0]
        q = q_ref[...]
        contract = (((1,), (1,)), ((), ()))
        score_old = lax.dot_general(q, k_ref[...], contract, preferred_element_type=jnp.float32)
        score_new = lax.dot_general(q, kn_ref[...], contract, preferred_element_type=jnp.float32)
        allow_old = lax.broadcasted_iota(jnp.int32, score_old.shape, 1) < limit
        allow_new = lax.broadcasted_iota(jnp.int32, score_new.shape, 1) <= lax.broadcasted_iota(
            jnp.int32, score_new.shape, 0
        )
        score_old = jnp.where(allow_old, score_old, -1e30)
        score_new = jnp.where(allow_new, score_new, -1e30)
        top = jnp.maximum(
            jnp.max(score_old, axis=1, keepdims=True), jnp.max(score_new, axis=1, keepdims=True)
        )
        prob_old = jnp.where(allow_old, jnp.exp(score_old - top), 0.0)
        prob_new = jnp.where(allow_new, jnp.exp(score_new - top), 0.0)
        total = jnp.sum(prob_old, axis=1, keepdims=True) + jnp.sum(prob_new, axis=1, keepdims=True)
        numer = jnp.dot(prob_old.astype(jnp.bfloat16), v_ref[...], preferred_element_type=jnp.float32)
        numer = numer + jnp.dot(
            prob_new.astype(jnp.bfloat16), vn_ref[...], preferred_element_type=jnp.float32
        )
        o_ref[...] = (numer / total).astype(o_ref.dtype)

    per_head = pl.BlockSpec((tokens, HD), lambda h, n: (0, h))
    grid_spec = pltpu.PrefetchScalarGridSpec(
        num_scalar_prefetch=1,
        grid=(heads,),
        in_specs=[
            per_head,
            per_head,
            per_head,
            pl.BlockSpec((context, HD), lambda h, n: (0, h)),
            pl.BlockSpec((context, HD), lambda h, n: (0, h)),
        ],
        out_specs=per_head,
    )
    return pl.pallas_call(
        kernel,
        grid_spec=grid_spec,
        out_shape=jax.ShapeDtypeStruct((tokens, heads * HD), jnp.bfloat16),
    )(length.reshape(1), query, key_new, value_new, keys, values)


def head_reduce(x, base, ident):
    mesh_kind = pl.DeviceIdType.MESH

    def kernel(x_ref, base_ref, o_ref, slots, send_sem, recv_sem):
        me = lax.axis_index("head")
        group = lax.axis_index("grp")
        partner = me + 1 - 2 * lax.rem(me, 2)
        across = lax.rem(me + 2, 4)
        barrier = pltpu.get_barrier_semaphore()
        for peer in (partner, across):
            pl.semaphore_signal(barrier, inc=1, device_id=(group, peer), device_id_type=mesh_kind)
        pl.semaphore_wait(barrier, 2)
        near = pltpu.make_async_remote_copy(
            src_ref=x_ref, dst_ref=slots.at[0], send_sem=send_sem.at[0], recv_sem=recv_sem.at[0],
            device_id=(group, partner), device_id_type=mesh_kind,
        )
        far = pltpu.make_async_remote_copy(
            src_ref=x_ref, dst_ref=slots.at[1], send_sem=send_sem.at[1], recv_sem=recv_sem.at[1],
            device_id=(group, across), device_id_type=mesh_kind,
        )
        near.start()
        far.start()
        far.wait_recv()
        relay = pltpu.make_async_remote_copy(
            src_ref=slots.at[1], dst_ref=slots.at[2], send_sem=send_sem.at[2],
            recv_sem=recv_sem.at[2], device_id=(group, partner), device_id_type=mesh_kind,
        )
        relay.start()
        near.wait()
        far.wait_send()
        relay.wait()
        total = base_ref[...] + x_ref[...].astype(jnp.float32)
        for slot in range(3):
            total = total + slots[slot].astype(jnp.float32)
        o_ref[...] = total

    return pl.pallas_call(
        kernel,
        out_shape=jax.ShapeDtypeStruct(x.shape, jnp.float32),
        in_specs=[pl.BlockSpec(memory_space=pltpu.VMEM), pl.BlockSpec(memory_space=pltpu.VMEM)],
        out_specs=pl.BlockSpec(memory_space=pltpu.VMEM),
        scratch_shapes=[
            pltpu.VMEM((3,) + x.shape, x.dtype),
            pltpu.SemaphoreType.DMA((3,)),
            pltpu.SemaphoreType.DMA((3,)),
        ],
        compiler_params=pltpu.CompilerParams(collective_id=ident, has_side_effects=True),
    )(x, base)


def on_device(
    hidden_in,
    attn_gain,
    w_query,
    w_key,
    w_value,
    w_out,
    cache,
    prefix_len,
    mlp_gain,
    expert_ids,
    route_weight,
    w_gate,
    w_up,
    w_down,
):
    group_count = lax.axis_size("grp")
    head_count = lax.axis_size("head")
    my_prompt = lax.axis_index("grp")
    tokens = hidden_in.shape[1]
    width = hidden_in.shape[2]
    heads_here = w_query.shape[1] // HD
    length = prefix_len[my_prompt]
    rows = hidden_in[0].astype(jnp.float32)
    normed = rms_norm(rows, attn_gain).astype(jnp.bfloat16)
    position = (length + jnp.arange(tokens)).astype(jnp.float32)
    query = jnp.dot(normed, w_query, preferred_element_type=jnp.float32).reshape(
        tokens, heads_here, HD
    )
    key_new = jnp.dot(normed, w_key, preferred_element_type=jnp.float32).reshape(
        tokens, heads_here, HD
    )
    value_new = jnp.dot(normed, w_value, preferred_element_type=jnp.float32).reshape(
        tokens, heads_here, HD
    )
    query = (rotate(query, position) * HD ** (-0.5)).astype(jnp.bfloat16)
    key_new = rotate(key_new, position).astype(jnp.bfloat16)
    value_new = value_new.astype(jnp.bfloat16)
    keys, values = [
        lax.all_to_all(cache[part], "grp", split_axis=0, concat_axis=0, tiled=True).reshape(
            group_count * cache.shape[2], heads_here * HD
        )
        for part in range(2)
    ]
    attended = attend(
        length,
        query.reshape(tokens, heads_here * HD),
        key_new.reshape(tokens, heads_here * HD),
        value_new.reshape(tokens, heads_here * HD),
        keys,
        values,
    )
    projected = jnp.dot(attended, w_out, preferred_element_type=jnp.float32)
    resid = head_reduce(projected.astype(jnp.bfloat16), rows, 0)
    mixed_in = rms_norm(resid, mlp_gain).astype(jnp.bfloat16)
    experts_here = w_gate.shape[0]
    expert_total = experts_here * group_count
    capacity = max(2, 3 * tokens * TOPK // (2 * expert_total))
    chosen = expert_ids[0].reshape(tokens * TOPK)
    weights = route_weight[0]
    pairs = tokens * TOPK
    slots = expert_total * capacity
    one_hot = (chosen[:, None] == jnp.arange(expert_total)[None, :]).astype(jnp.bfloat16)
    earlier = (jnp.arange(pairs)[None, :] < jnp.arange(pairs)[:, None]).astype(jnp.bfloat16)
    before = jnp.dot(earlier, one_hot, preferred_element_type=jnp.float32)
    slot = jnp.sum(before * one_hot.astype(jnp.float32), axis=1).astype(jnp.int32)
    target = chosen * capacity + slot
    place = (target[:, None] == jnp.arange(slots)[None, :]).reshape(tokens, TOPK, slots)
    dispatch = jnp.sum(place.astype(jnp.float32), axis=1).astype(jnp.bfloat16)
    share_width = width // head_count
    head_at = lax.axis_index("head")
    core = lax.rem(head_at, 2)
    chip = head_at // 2
    other_core = 1 - core
    def halves(array, which):
        split = array.reshape(array.shape[:-1] + (2, 2, share_width))
        taken = lax.dynamic_index_in_dim(split, which, axis=split.ndim - 2, keepdims=False)
        return taken.reshape(array.shape[:-1] + (2 * share_width,))

    def row_halves(array, which):
        split = array.reshape((2, 2, share_width) + array.shape[1:])
        taken = lax.dynamic_index_in_dim(split, which, axis=1, keepdims=False)
        return taken.reshape((2 * share_width,) + array.shape[1:])

    half = 2 * share_width
    outgoing = lax.dot_general(
        dispatch, halves(mixed_in, core), (((0,), (0,)), ((), ())), preferred_element_type=jnp.float32
    ).astype(jnp.bfloat16)
    outgoing = outgoing.reshape(group_count, experts_here, capacity, half)
    arrived = lax.all_to_all(outgoing, "grp", split_axis=0, concat_axis=0, tiled=True)
    partners = [(index, index ^ 1) for index in range(head_count)]
    arrived_other = lax.ppermute(arrived, "head", partners)
    pair_sums = []
    for expert in range(experts_here):
        mine = arrived[:, expert].reshape(group_count * capacity, half)
        other = arrived_other[:, expert].reshape(group_count * capacity, half)
        gate = jnp.dot(mine, row_halves(w_gate[expert], core), preferred_element_type=jnp.float32)
        gate = gate + jnp.dot(other, row_halves(w_gate[expert], other_core), preferred_element_type=jnp.float32)
        upper = jnp.dot(mine, row_halves(w_up[expert], core), preferred_element_type=jnp.float32)
        upper = upper + jnp.dot(other, row_halves(w_up[expert], other_core), preferred_element_type=jnp.float32)
        act = (jax.nn.silu(gate) * upper).astype(jnp.bfloat16)
        mine_part = jnp.dot(act, halves(w_down[expert], core), preferred_element_type=jnp.float32)
        other_part = jnp.dot(act, halves(w_down[expert], other_core), preferred_element_type=jnp.float32)
        partner_part = lax.ppermute(other_part.astype(jnp.bfloat16), "head", partners)
        pair_sums.append(
            (mine_part.astype(jnp.bfloat16).astype(jnp.float32) + partner_part.astype(jnp.float32))
            .astype(jnp.bfloat16)
            .reshape(group_count, capacity, half)
        )
    pair_sum = jnp.stack(pair_sums, axis=1)
    returned = lax.all_to_all(pair_sum, "grp", split_axis=0, concat_axis=0, tiled=True)
    returned = returned.reshape(slots, half)
    weighting = jnp.sum(jnp.where(place, weights[:, :, None], 0.0), axis=1)
    pieces = []
    for _ in range(3):
        piece = weighting.astype(jnp.bfloat16)
        weighting = weighting - piece.astype(jnp.float32)
        pieces.append(piece)
    stacked = jnp.concatenate(pieces, axis=0)
    by_chip = returned.reshape(slots, 2, share_width)

    def combine_block(which):
        block = lax.dynamic_index_in_dim(by_chip, which, axis=1, keepdims=False)
        products = jnp.dot(stacked, block, preferred_element_type=jnp.float32)
        return products.reshape(3, tokens, share_width).sum(axis=0)

    across_pairs = [(index, index ^ 2) for index in range(head_count)]
    received = lax.ppermute(combine_block(1 - chip), "head", across_pairs)
    moe_share = combine_block(chip) + received
    resid_share = lax.dynamic_slice_in_dim(resid, head_at * share_width, share_width, 1)
    return (resid_share + moe_share).astype(jnp.bfloat16)[None]


def solution(mesh):
    placed = (
        P("grp", None, None),
        P(),
        P(None, "head"),
        P(None, "head"),
        P(None, "head"),
        P("head", None),
        P(None, None, "grp", "head"),
        P(),
        P(),
        P("grp", None, None),
        P("grp", None, None),
        P("grp", None, "head"),
        P("grp", None, "head"),
        P("grp", "head", None),
    )
    return jax.shard_map(
        on_device, mesh=mesh, in_specs=placed, out_specs=P("grp", None, "head"), check_vma=False
    )
```

```python
import jax
import jax.numpy as jnp
from jax import lax
from jax.experimental import pallas as pl
from jax.experimental.pallas import tpu as pltpu
from jax.sharding import PartitionSpec as P

HD = 128
TOPK = 8


def rms_norm(values, gain):
    scale = lax.rsqrt(jnp.mean(values * values, axis=-1, keepdims=True) + 1e-05)
    return values * scale * gain


def rotate(tensor, position):
    half = HD // 2
    inverse = 10000.0 ** (-(jnp.arange(half).astype(jnp.float32) * 2.0) / HD)
    angle = position[:, None] * inverse[None, :]
    cosine = jnp.cos(angle)[:, None, :]
    sine = jnp.sin(angle)[:, None, :]
    first = tensor[..., :half]
    second = tensor[..., half:]
    return jnp.concatenate(
        [first * cosine - second * sine, second * cosine + first * sine], axis=-1
    )


def peer_swap(x, across, ident):
    mesh_kind = pl.DeviceIdType.MESH

    def kernel(x_ref, o_ref, send_sem, recv_sem):
        me = lax.axis_index("head")
        group = lax.axis_index("grp")
        peer = lax.rem(me + 2, 4) if across else me + 1 - 2 * lax.rem(me, 2)
        barrier = pltpu.get_barrier_semaphore()
        pl.semaphore_signal(barrier, inc=1, device_id=(group, peer), device_id_type=mesh_kind)
        pl.semaphore_wait(barrier, 1)
        copy = pltpu.make_async_remote_copy(
            src_ref=x_ref, dst_ref=o_ref, send_sem=send_sem, recv_sem=recv_sem,
            device_id=(group, peer), device_id_type=mesh_kind,
        )
        copy.start()
        copy.wait()

    return pl.pallas_call(
        kernel,
        out_shape=jax.ShapeDtypeStruct(x.shape, x.dtype),
        in_specs=[pl.BlockSpec(memory_space=pl.ANY)],
        out_specs=pl.BlockSpec(memory_space=pl.ANY),
        scratch_shapes=[pltpu.SemaphoreType.DMA(()), pltpu.SemaphoreType.DMA(())],
        compiler_params=pltpu.CompilerParams(collective_id=ident, has_side_effects=True),
    )(x)


def attend(length, query, key_new, value_new, keys, values, w_out):
    tokens = query.shape[0]
    context = keys.shape[0]
    heads = query.shape[1] // HD

    width = w_out.shape[1]

    def kernel(length_ref, q_ref, kn_ref, vn_ref, k_ref, v_ref, w_ref, o_ref, acc_ref):
        head = pl.program_id(0)
        limit = length_ref[0]
        q = q_ref[...]
        contract = (((1,), (1,)), ((), ()))
        score_old = lax.dot_general(q, k_ref[...], contract, preferred_element_type=jnp.float32)
        score_new = lax.dot_general(q, kn_ref[...], contract, preferred_element_type=jnp.float32)
        allow_old = lax.broadcasted_iota(jnp.int32, score_old.shape, 1) < limit
        allow_new = lax.broadcasted_iota(jnp.int32, score_new.shape, 1) <= lax.broadcasted_iota(
            jnp.int32, score_new.shape, 0
        )
        score_old = jnp.where(allow_old, score_old, -1e30)
        score_new = jnp.where(allow_new, score_new, -1e30)
        top = jnp.maximum(
            jnp.max(score_old, axis=1, keepdims=True), jnp.max(score_new, axis=1, keepdims=True)
        )
        prob_old = jnp.where(allow_old, jnp.exp(score_old - top), 0.0)
        prob_new = jnp.where(allow_new, jnp.exp(score_new - top), 0.0)
        total = jnp.sum(prob_old, axis=1, keepdims=True) + jnp.sum(prob_new, axis=1, keepdims=True)
        numer = jnp.dot(prob_old.astype(jnp.bfloat16), v_ref[...], preferred_element_type=jnp.float32)
        numer = numer + jnp.dot(
            prob_new.astype(jnp.bfloat16), vn_ref[...], preferred_element_type=jnp.float32
        )
        attended = (numer / total).astype(jnp.bfloat16)
        term = jnp.dot(attended, w_ref[...], preferred_element_type=jnp.float32)

        @pl.when(head == 0)
        def _():
            acc_ref[...] = term

        @pl.when(head > 0)
        def _():
            acc_ref[...] += term

        @pl.when(head == heads - 1)
        def _():
            o_ref[...] = acc_ref[...].astype(o_ref.dtype)

    per_head = pl.BlockSpec((tokens, HD), lambda h, n: (0, h))
    grid_spec = pltpu.PrefetchScalarGridSpec(
        num_scalar_prefetch=1,
        grid=(heads,),
        in_specs=[
            per_head,
            per_head,
            per_head,
            pl.BlockSpec((context, HD), lambda h, n: (0, h)),
            pl.BlockSpec((context, HD), lambda h, n: (0, h)),
            pl.BlockSpec((HD, width), lambda h, n: (h, 0)),
        ],
        out_specs=pl.BlockSpec((tokens, width), lambda h, n: (0, 0)),
        scratch_shapes=[pltpu.VMEM((tokens, width), jnp.float32)],
    )
    return pl.pallas_call(
        kernel,
        grid_spec=grid_spec,
        out_shape=jax.ShapeDtypeStruct((tokens, width), jnp.bfloat16),
    )(length.reshape(1), query, key_new, value_new, keys, values, w_out)


def head_reduce(x, base, gain, ident):
    mesh_kind = pl.DeviceIdType.MESH

    def kernel(x_ref, base_ref, gain_ref, o_ref, normed_ref, slots, send_sem, recv_sem):
        me = lax.axis_index("head")
        group = lax.axis_index("grp")
        partner = me + 1 - 2 * lax.rem(me, 2)
        across = lax.rem(me + 2, 4)
        barrier = pltpu.get_barrier_semaphore()
        for peer in (partner, across):
            pl.semaphore_signal(barrier, inc=1, device_id=(group, peer), device_id_type=mesh_kind)
        pl.semaphore_wait(barrier, 2)
        near = pltpu.make_async_remote_copy(
            src_ref=x_ref, dst_ref=slots.at[0], send_sem=send_sem.at[0], recv_sem=recv_sem.at[0],
            device_id=(group, partner), device_id_type=mesh_kind,
        )
        far = pltpu.make_async_remote_copy(
            src_ref=x_ref, dst_ref=slots.at[1], send_sem=send_sem.at[1], recv_sem=recv_sem.at[1],
            device_id=(group, across), device_id_type=mesh_kind,
        )
        near.start()
        far.start()
        far.wait_recv()
        relay = pltpu.make_async_remote_copy(
            src_ref=slots.at[1], dst_ref=slots.at[2], send_sem=send_sem.at[2],
            recv_sem=recv_sem.at[2], device_id=(group, partner), device_id_type=mesh_kind,
        )
        relay.start()
        near.wait()
        far.wait_send()
        relay.wait()
        total = base_ref[...] + x_ref[...].astype(jnp.float32)
        for slot in range(3):
            total = total + slots[slot].astype(jnp.float32)
        o_ref[...] = total
        scale = lax.rsqrt(jnp.mean(total * total, axis=-1, keepdims=True) + 1e-05)
        normed_ref[...] = (total * scale * gain_ref[...]).astype(normed_ref.dtype)

    vmem = pl.BlockSpec(memory_space=pltpu.VMEM)
    return pl.pallas_call(
        kernel,
        out_shape=(
            jax.ShapeDtypeStruct(x.shape, jnp.float32),
            jax.ShapeDtypeStruct(x.shape, jnp.bfloat16),
        ),
        in_specs=[vmem, vmem, vmem],
        out_specs=(vmem, vmem),
        scratch_shapes=[
            pltpu.VMEM((3,) + x.shape, x.dtype),
            pltpu.SemaphoreType.DMA((3,)),
            pltpu.SemaphoreType.DMA((3,)),
        ],
        compiler_params=pltpu.CompilerParams(collective_id=ident, has_side_effects=True),
    )(x, base, gain.reshape(1, -1))


def on_device(
    hidden_in,
    attn_gain,
    w_query,
    w_key,
    w_value,
    w_out,
    cache,
    prefix_len,
    mlp_gain,
    expert_ids,
    route_weight,
    w_gate,
    w_up,
    w_down,
):
    group_count = lax.axis_size("grp")
    head_count = lax.axis_size("head")
    my_prompt = lax.axis_index("grp")
    tokens = hidden_in.shape[1]
    width = hidden_in.shape[2]
    heads_here = w_query.shape[1] // HD
    length = prefix_len[my_prompt]
    rows = hidden_in[0].astype(jnp.float32)
    normed = rms_norm(rows, attn_gain).astype(jnp.bfloat16)
    position = (length + jnp.arange(tokens)).astype(jnp.float32)
    query = jnp.dot(normed, w_query, preferred_element_type=jnp.float32).reshape(
        tokens, heads_here, HD
    )
    key_new = jnp.dot(normed, w_key, preferred_element_type=jnp.float32).reshape(
        tokens, heads_here, HD
    )
    value_new = jnp.dot(normed, w_value, preferred_element_type=jnp.float32).reshape(
        tokens, heads_here, HD
    )
    query = (rotate(query, position) * HD ** (-0.5)).astype(jnp.bfloat16)
    key_new = rotate(key_new, position).astype(jnp.bfloat16)
    value_new = value_new.astype(jnp.bfloat16)
    keys, values = [
        lax.all_to_all(cache[part], "grp", split_axis=0, concat_axis=0, tiled=True).reshape(
            group_count * cache.shape[2], heads_here * HD
        )
        for part in range(2)
    ]
    projected = attend(
        length,
        query.reshape(tokens, heads_here * HD),
        key_new.reshape(tokens, heads_here * HD),
        value_new.reshape(tokens, heads_here * HD),
        keys,
        values,
        w_out,
    )
    resid, mixed_in = head_reduce(projected, rows, mlp_gain, 0)
    experts_here = w_gate.shape[0]
    expert_total = experts_here * group_count
    capacity = max(2, 3 * tokens * TOPK // (2 * expert_total))
    chosen = expert_ids[0].reshape(tokens * TOPK)
    weights = route_weight[0]
    pairs = tokens * TOPK
    slots = expert_total * capacity
    one_hot = (chosen[:, None] == jnp.arange(expert_total)[None, :]).astype(jnp.bfloat16)
    earlier = (jnp.arange(pairs)[None, :] < jnp.arange(pairs)[:, None]).astype(jnp.bfloat16)
    before = jnp.dot(earlier, one_hot, preferred_element_type=jnp.float32)
    slot = jnp.sum(before * one_hot.astype(jnp.float32), axis=1).astype(jnp.int32)
    target = chosen * capacity + slot
    place = (target[:, None] == jnp.arange(slots)[None, :]).reshape(tokens, TOPK, slots)
    dispatch = jnp.sum(place.astype(jnp.float32), axis=1).astype(jnp.bfloat16)
    share_width = width // head_count
    head_at = lax.axis_index("head")
    core = lax.rem(head_at, 2)
    chip = head_at // 2
    other_core = 1 - core
    def halves(array, which):
        split = array.reshape(array.shape[:-1] + (2, 2, share_width))
        taken = lax.dynamic_index_in_dim(split, which, axis=split.ndim - 2, keepdims=False)
        return taken.reshape(array.shape[:-1] + (2 * share_width,))

    def row_halves(array, which):
        split = array.reshape((2, 2, share_width) + array.shape[1:])
        taken = lax.dynamic_index_in_dim(split, which, axis=1, keepdims=False)
        return taken.reshape((2 * share_width,) + array.shape[1:])

    half = 2 * share_width
    outgoing = lax.dot_general(
        dispatch, halves(mixed_in, core), (((0,), (0,)), ((), ())), preferred_element_type=jnp.float32
    ).astype(jnp.bfloat16)
    outgoing = outgoing.reshape(group_count, experts_here, capacity, half)
    arrived = lax.all_to_all(outgoing, "grp", split_axis=0, concat_axis=0, tiled=True)
    partners = [(index, index ^ 1) for index in range(head_count)]
    arrived_other = lax.ppermute(arrived, "head", partners)
    pair_sums = []
    for expert in range(experts_here):
        mine = arrived[:, expert].reshape(group_count * capacity, half)
        other = arrived_other[:, expert].reshape(group_count * capacity, half)
        gate = jnp.dot(mine, row_halves(w_gate[expert], core), preferred_element_type=jnp.float32)
        gate = gate + jnp.dot(other, row_halves(w_gate[expert], other_core), preferred_element_type=jnp.float32)
        upper = jnp.dot(mine, row_halves(w_up[expert], core), preferred_element_type=jnp.float32)
        upper = upper + jnp.dot(other, row_halves(w_up[expert], other_core), preferred_element_type=jnp.float32)
        act = (jax.nn.silu(gate) * upper).astype(jnp.bfloat16)
        mine_part = jnp.dot(act, halves(w_down[expert], core), preferred_element_type=jnp.float32)
        other_part = jnp.dot(act, halves(w_down[expert], other_core), preferred_element_type=jnp.float32)
        partner_part = lax.ppermute(other_part.astype(jnp.bfloat16), "head", partners)
        pair_sums.append(
            (mine_part.astype(jnp.bfloat16).astype(jnp.float32) + partner_part.astype(jnp.float32))
            .astype(jnp.bfloat16)
            .reshape(group_count, capacity, half)
        )
    pair_sum = jnp.stack(pair_sums, axis=1)
    returned = lax.all_to_all(pair_sum, "grp", split_axis=0, concat_axis=0, tiled=True)
    returned = returned.reshape(slots, half)
    weighting = jnp.sum(jnp.where(place, weights[:, :, None], 0.0), axis=1)
    pieces = []
    for _ in range(3):
        piece = weighting.astype(jnp.bfloat16)
        weighting = weighting - piece.astype(jnp.float32)
        pieces.append(piece)
    combined = jnp.dot(jnp.concatenate(pieces, axis=0), returned, preferred_element_type=jnp.float32)
    combined = combined.reshape(3, tokens, half).sum(axis=0)
    combined = combined.reshape(tokens, 2, share_width)
    keep = lax.dynamic_index_in_dim(combined, chip, axis=1, keepdims=False)
    give = lax.dynamic_index_in_dim(combined, 1 - chip, axis=1, keepdims=False)
    moe_share = keep + peer_swap(give, True, 3)
    resid_share = lax.dynamic_slice_in_dim(resid, head_at * share_width, share_width, 1)
    return (resid_share + moe_share).astype(jnp.bfloat16)[None]


def solution(mesh):
    placed = (
        P("grp", None, None),
        P(),
        P(None, "head"),
        P(None, "head"),
        P(None, "head"),
        P("head", None),
        P(None, None, "grp", "head"),
        P(),
        P(),
        P("grp", None, None),
        P("grp", None, None),
        P("grp", None, "head"),
        P("grp", None, "head"),
        P("grp", "head", None),
    )
    return jax.shard_map(
        on_device, mesh=mesh, in_specs=placed, out_specs=P("grp", None, "head"), check_vma=False
    )
```

```python
import jax
import jax.numpy as jnp
from jax import lax
from jax.experimental import pallas as pl
from jax.experimental.pallas import tpu as pltpu
from jax.sharding import PartitionSpec as P

HD = 128
TOPK = 8


def rms_norm(values, gain):
    scale = lax.rsqrt(jnp.mean(values * values, axis=-1, keepdims=True) + 1e-05)
    return values * scale * gain


def rotate(tensor, position):
    half = HD // 2
    inverse = 10000.0 ** (-(jnp.arange(half).astype(jnp.float32) * 2.0) / HD)
    angle = position[:, None] * inverse[None, :]
    cosine = jnp.cos(angle)[:, None, :]
    sine = jnp.sin(angle)[:, None, :]
    first = tensor[..., :half]
    second = tensor[..., half:]
    return jnp.concatenate(
        [first * cosine - second * sine, second * cosine + first * sine], axis=-1
    )


def peer_swap(x, across, ident):
    mesh_kind = pl.DeviceIdType.MESH

    def kernel(x_ref, o_ref, send_sem, recv_sem):
        me = lax.axis_index("head")
        group = lax.axis_index("grp")
        peer = lax.rem(me + 2, 4) if across else me + 1 - 2 * lax.rem(me, 2)
        barrier = pltpu.get_barrier_semaphore()
        pl.semaphore_signal(barrier, inc=1, device_id=(group, peer), device_id_type=mesh_kind)
        pl.semaphore_wait(barrier, 1)
        copy = pltpu.make_async_remote_copy(
            src_ref=x_ref, dst_ref=o_ref, send_sem=send_sem, recv_sem=recv_sem,
            device_id=(group, peer), device_id_type=mesh_kind,
        )
        copy.start()
        copy.wait()

    return pl.pallas_call(
        kernel,
        out_shape=jax.ShapeDtypeStruct(x.shape, x.dtype),
        in_specs=[pl.BlockSpec(memory_space=pl.ANY)],
        out_specs=pl.BlockSpec(memory_space=pl.ANY),
        scratch_shapes=[pltpu.SemaphoreType.DMA(()), pltpu.SemaphoreType.DMA(())],
        compiler_params=pltpu.CompilerParams(collective_id=ident, has_side_effects=True),
    )(x)


def attend(length, query, key_new, value_new, keys, values):
    tokens = query.shape[0]
    context = keys.shape[0]
    heads = query.shape[1] // HD

    chunk = min(context, 256)
    steps = context // chunk

    def kernel(length_ref, q_ref, kn_ref, vn_ref, k_ref, v_ref, o_ref):
        limit = length_ref[0]
        q = q_ref[...]
        contract = (((1,), (1,)), ((), ()))
        score_new = lax.dot_general(q, kn_ref[...], contract, preferred_element_type=jnp.float32)
        allow_new = lax.broadcasted_iota(jnp.int32, score_new.shape, 1) <= lax.broadcasted_iota(
            jnp.int32, score_new.shape, 0
        )
        score_new = jnp.where(allow_new, score_new, -1e30)

        def scores(step):
            start = pl.multiple_of(step * chunk, chunk)
            score = lax.dot_general(
                q, k_ref[pl.ds(start, chunk), :], contract, preferred_element_type=jnp.float32
            )
            allow = lax.broadcasted_iota(jnp.int32, score.shape, 1) + start < limit
            return jnp.where(allow, score, -1e30), allow, start

        def widest(step, top):
            score, _, _ = scores(step)
            return jnp.maximum(top, jnp.max(score, axis=1, keepdims=True))

        top = lax.fori_loop(0, steps, widest, jnp.max(score_new, axis=1, keepdims=True))
        prob_new = jnp.where(allow_new, jnp.exp(score_new - top), 0.0)
        total = jnp.sum(prob_new, axis=1, keepdims=True)
        numer = jnp.dot(prob_new.astype(jnp.bfloat16), vn_ref[...], preferred_element_type=jnp.float32)

        def accumulate(step, carry):
            total, numer = carry
            score, allow, start = scores(step)
            prob = jnp.where(allow, jnp.exp(score - top), 0.0)
            total = total + jnp.sum(prob, axis=1, keepdims=True)
            numer = numer + jnp.dot(
                prob.astype(jnp.bfloat16), v_ref[pl.ds(start, chunk), :], preferred_element_type=jnp.float32
            )
            return total, numer

        total, numer = lax.fori_loop(0, steps, accumulate, (total, numer))
        o_ref[...] = (numer / total).astype(o_ref.dtype)

    per_head = pl.BlockSpec((tokens, HD), lambda h, n: (0, h))
    grid_spec = pltpu.PrefetchScalarGridSpec(
        num_scalar_prefetch=1,
        grid=(heads,),
        in_specs=[
            per_head,
            per_head,
            per_head,
            pl.BlockSpec((context, HD), lambda h, n: (0, h)),
            pl.BlockSpec((context, HD), lambda h, n: (0, h)),
        ],
        out_specs=per_head,
    )
    return pl.pallas_call(
        kernel,
        grid_spec=grid_spec,
        out_shape=jax.ShapeDtypeStruct((tokens, heads * HD), jnp.bfloat16),
    )(length.reshape(1), query, key_new, value_new, keys, values)


def head_reduce(x, base, ident):
    mesh_kind = pl.DeviceIdType.MESH

    def kernel(x_ref, base_ref, o_ref, slots, send_sem, recv_sem):
        me = lax.axis_index("head")
        group = lax.axis_index("grp")
        partner = me + 1 - 2 * lax.rem(me, 2)
        across = lax.rem(me + 2, 4)
        barrier = pltpu.get_barrier_semaphore()
        for peer in (partner, across):
            pl.semaphore_signal(barrier, inc=1, device_id=(group, peer), device_id_type=mesh_kind)
        pl.semaphore_wait(barrier, 2)
        near = pltpu.make_async_remote_copy(
            src_ref=x_ref, dst_ref=slots.at[0], send_sem=send_sem.at[0], recv_sem=recv_sem.at[0],
            device_id=(group, partner), device_id_type=mesh_kind,
        )
        far = pltpu.make_async_remote_copy(
            src_ref=x_ref, dst_ref=slots.at[1], send_sem=send_sem.at[1], recv_sem=recv_sem.at[1],
            device_id=(group, across), device_id_type=mesh_kind,
        )
        near.start()
        far.start()
        far.wait_recv()
        relay = pltpu.make_async_remote_copy(
            src_ref=slots.at[1], dst_ref=slots.at[2], send_sem=send_sem.at[2],
            recv_sem=recv_sem.at[2], device_id=(group, partner), device_id_type=mesh_kind,
        )
        relay.start()
        near.wait()
        far.wait_send()
        relay.wait()
        total = base_ref[...] + x_ref[...].astype(jnp.float32)
        for slot in range(3):
            total = total + slots[slot].astype(jnp.float32)
        o_ref[...] = total

    return pl.pallas_call(
        kernel,
        out_shape=jax.ShapeDtypeStruct(x.shape, jnp.float32),
        in_specs=[pl.BlockSpec(memory_space=pltpu.VMEM), pl.BlockSpec(memory_space=pltpu.VMEM)],
        out_specs=pl.BlockSpec(memory_space=pltpu.VMEM),
        scratch_shapes=[
            pltpu.VMEM((3,) + x.shape, x.dtype),
            pltpu.SemaphoreType.DMA((3,)),
            pltpu.SemaphoreType.DMA((3,)),
        ],
        compiler_params=pltpu.CompilerParams(collective_id=ident, has_side_effects=True),
    )(x, base)


def on_device(
    hidden_in,
    attn_gain,
    w_query,
    w_key,
    w_value,
    w_out,
    cache,
    prefix_len,
    mlp_gain,
    expert_ids,
    route_weight,
    w_gate,
    w_up,
    w_down,
):
    group_count = lax.axis_size("grp")
    head_count = lax.axis_size("head")
    my_prompt = lax.axis_index("grp")
    tokens = hidden_in.shape[1]
    width = hidden_in.shape[2]
    heads_here = w_query.shape[1] // HD
    length = prefix_len[my_prompt]
    rows = hidden_in[0].astype(jnp.float32)
    normed = rms_norm(rows, attn_gain).astype(jnp.bfloat16)
    position = (length + jnp.arange(tokens)).astype(jnp.float32)
    query = jnp.dot(normed, w_query, preferred_element_type=jnp.float32).reshape(
        tokens, heads_here, HD
    )
    key_new = jnp.dot(normed, w_key, preferred_element_type=jnp.float32).reshape(
        tokens, heads_here, HD
    )
    value_new = jnp.dot(normed, w_value, preferred_element_type=jnp.float32).reshape(
        tokens, heads_here, HD
    )
    query = (rotate(query, position) * HD ** (-0.5)).astype(jnp.bfloat16)
    key_new = rotate(key_new, position).astype(jnp.bfloat16)
    value_new = value_new.astype(jnp.bfloat16)
    keys, values = [
        lax.all_to_all(cache[part], "grp", split_axis=0, concat_axis=0, tiled=True).reshape(
            group_count * cache.shape[2], heads_here * HD
        )
        for part in range(2)
    ]
    attended = attend(
        length,
        query.reshape(tokens, heads_here * HD),
        key_new.reshape(tokens, heads_here * HD),
        value_new.reshape(tokens, heads_here * HD),
        keys,
        values,
    )
    projected = jnp.dot(attended, w_out, preferred_element_type=jnp.float32)
    resid = head_reduce(projected.astype(jnp.bfloat16), rows, 0)
    mixed_in = rms_norm(resid, mlp_gain).astype(jnp.bfloat16)
    experts_here = w_gate.shape[0]
    expert_total = experts_here * group_count
    capacity = max(2, 3 * tokens * TOPK // (2 * expert_total))
    chosen = expert_ids[0].reshape(tokens * TOPK)
    weights = route_weight[0]
    pairs = tokens * TOPK
    slots = expert_total * capacity
    one_hot = (chosen[:, None] == jnp.arange(expert_total)[None, :]).astype(jnp.bfloat16)
    earlier = (jnp.arange(pairs)[None, :] < jnp.arange(pairs)[:, None]).astype(jnp.bfloat16)
    before = jnp.dot(earlier, one_hot, preferred_element_type=jnp.float32)
    slot = jnp.sum(before * one_hot.astype(jnp.float32), axis=1).astype(jnp.int32)
    target = chosen * capacity + slot
    place = (target[:, None] == jnp.arange(slots)[None, :]).reshape(tokens, TOPK, slots)
    dispatch = jnp.sum(place.astype(jnp.float32), axis=1).astype(jnp.bfloat16)
    share_width = width // head_count
    head_at = lax.axis_index("head")
    core = lax.rem(head_at, 2)
    chip = head_at // 2
    other_core = 1 - core
    def halves(array, which):
        split = array.reshape(array.shape[:-1] + (2, 2, share_width))
        taken = lax.dynamic_index_in_dim(split, which, axis=split.ndim - 2, keepdims=False)
        return taken.reshape(array.shape[:-1] + (2 * share_width,))

    def row_halves(array, which):
        split = array.reshape((2, 2, share_width) + array.shape[1:])
        taken = lax.dynamic_index_in_dim(split, which, axis=1, keepdims=False)
        return taken.reshape((2 * share_width,) + array.shape[1:])

    half = 2 * share_width
    outgoing = lax.dot_general(
        dispatch, halves(mixed_in, core), (((0,), (0,)), ((), ())), preferred_element_type=jnp.float32
    ).astype(jnp.bfloat16)
    outgoing = outgoing.reshape(group_count, experts_here, capacity, half)
    arrived = lax.all_to_all(outgoing, "grp", split_axis=0, concat_axis=0, tiled=True)
    partners = [(index, index ^ 1) for index in range(head_count)]
    arrived_other = lax.ppermute(arrived, "head", partners)
    pair_sums = []
    for expert in range(experts_here):
        mine = arrived[:, expert].reshape(group_count * capacity, half)
        other = arrived_other[:, expert].reshape(group_count * capacity, half)
        gate = jnp.dot(mine, row_halves(w_gate[expert], core), preferred_element_type=jnp.float32)
        gate = gate + jnp.dot(other, row_halves(w_gate[expert], other_core), preferred_element_type=jnp.float32)
        upper = jnp.dot(mine, row_halves(w_up[expert], core), preferred_element_type=jnp.float32)
        upper = upper + jnp.dot(other, row_halves(w_up[expert], other_core), preferred_element_type=jnp.float32)
        act = (jax.nn.silu(gate) * upper).astype(jnp.bfloat16)
        mine_part = jnp.dot(act, halves(w_down[expert], core), preferred_element_type=jnp.float32)
        other_part = jnp.dot(act, halves(w_down[expert], other_core), preferred_element_type=jnp.float32)
        partner_part = lax.ppermute(other_part.astype(jnp.bfloat16), "head", partners)
        pair_sums.append(
            (mine_part.astype(jnp.bfloat16).astype(jnp.float32) + partner_part.astype(jnp.float32))
            .astype(jnp.bfloat16)
            .reshape(group_count, capacity, half)
        )
    pair_sum = jnp.stack(pair_sums, axis=1)
    returned = lax.all_to_all(pair_sum, "grp", split_axis=0, concat_axis=0, tiled=True)
    returned = returned.reshape(slots, half)
    weighting = jnp.sum(jnp.where(place, weights[:, :, None], 0.0), axis=1)
    pieces = []
    for _ in range(3):
        piece = weighting.astype(jnp.bfloat16)
        weighting = weighting - piece.astype(jnp.float32)
        pieces.append(piece)
    combined = jnp.dot(jnp.concatenate(pieces, axis=0), returned, preferred_element_type=jnp.float32)
    combined = combined.reshape(3, tokens, half).sum(axis=0)
    combined = combined.reshape(tokens, 2, share_width)
    keep = lax.dynamic_index_in_dim(combined, chip, axis=1, keepdims=False)
    give = lax.dynamic_index_in_dim(combined, 1 - chip, axis=1, keepdims=False)
    moe_share = keep + peer_swap(give, True, 3)
    resid_share = lax.dynamic_slice_in_dim(resid, head_at * share_width, share_width, 1)
    return (resid_share + moe_share).astype(jnp.bfloat16)[None]


def solution(mesh):
    placed = (
        P("grp", None, None),
        P(),
        P(None, "head"),
        P(None, "head"),
        P(None, "head"),
        P("head", None),
        P(None, None, "grp", "head"),
        P(),
        P(),
        P("grp", None, None),
        P("grp", None, None),
        P("grp", None, "head"),
        P("grp", None, "head"),
        P("grp", "head", None),
    )
    return jax.shard_map(
        on_device, mesh=mesh, in_specs=placed, out_specs=P("grp", None, "head"), check_vma=False
    )
```

```python
import jax
import jax.numpy as jnp
from jax import lax
from jax.experimental import pallas as pl
from jax.experimental.pallas import tpu as pltpu
from jax.sharding import PartitionSpec as P

HD = 128
TOPK = 8


def rms_norm(values, gain):
    scale = lax.rsqrt(jnp.mean(values * values, axis=-1, keepdims=True) + 1e-05)
    return values * scale * gain


def rotate(tensor, position):
    half = HD // 2
    inverse = 10000.0 ** (-(jnp.arange(half).astype(jnp.float32) * 2.0) / HD)
    angle = position[:, None] * inverse[None, :]
    cosine = jnp.cos(angle)[:, None, :]
    sine = jnp.sin(angle)[:, None, :]
    first = tensor[..., :half]
    second = tensor[..., half:]
    return jnp.concatenate(
        [first * cosine - second * sine, second * cosine + first * sine], axis=-1
    )


def peer_swap(x, across, ident):
    mesh_kind = pl.DeviceIdType.MESH

    def kernel(x_ref, o_ref, send_sem, recv_sem):
        me = lax.axis_index("head")
        group = lax.axis_index("grp")
        peer = lax.rem(me + 2, 4) if across else me + 1 - 2 * lax.rem(me, 2)
        barrier = pltpu.get_barrier_semaphore()
        pl.semaphore_signal(barrier, inc=1, device_id=(group, peer), device_id_type=mesh_kind)
        pl.semaphore_wait(barrier, 1)
        copy = pltpu.make_async_remote_copy(
            src_ref=x_ref, dst_ref=o_ref, send_sem=send_sem, recv_sem=recv_sem,
            device_id=(group, peer), device_id_type=mesh_kind,
        )
        copy.start()
        copy.wait()

    return pl.pallas_call(
        kernel,
        out_shape=jax.ShapeDtypeStruct(x.shape, x.dtype),
        in_specs=[pl.BlockSpec(memory_space=pl.ANY)],
        out_specs=pl.BlockSpec(memory_space=pl.ANY),
        scratch_shapes=[pltpu.SemaphoreType.DMA(()), pltpu.SemaphoreType.DMA(())],
        compiler_params=pltpu.CompilerParams(collective_id=ident, has_side_effects=True),
    )(x)


def attend(length, query, key_new, value_new, keys, values):
    tokens = query.shape[0]
    context = keys.shape[0]
    heads = query.shape[1] // HD

    def kernel(length_ref, q_ref, kn_ref, vn_ref, k_ref, v_ref, o_ref):
        limit = length_ref[0]
        q = q_ref[...]
        contract = (((1,), (1,)), ((), ()))
        score_old = lax.dot_general(q, k_ref[...], contract, preferred_element_type=jnp.float32)
        score_new = lax.dot_general(q, kn_ref[...], contract, preferred_element_type=jnp.float32)
        allow_old = lax.broadcasted_iota(jnp.int32, score_old.shape, 1) < limit
        allow_new = lax.broadcasted_iota(jnp.int32, score_new.shape, 1) <= lax.broadcasted_iota(
            jnp.int32, score_new.shape, 0
        )
        score_old = jnp.where(allow_old, score_old, -1e30)
        score_new = jnp.where(allow_new, score_new, -1e30)
        top = jnp.maximum(
            jnp.max(score_old, axis=1, keepdims=True), jnp.max(score_new, axis=1, keepdims=True)
        )
        prob_old = jnp.where(allow_old, jnp.exp(score_old - top), 0.0)
        prob_new = jnp.where(allow_new, jnp.exp(score_new - top), 0.0)
        total = jnp.sum(prob_old, axis=1, keepdims=True) + jnp.sum(prob_new, axis=1, keepdims=True)
        numer = jnp.dot(prob_old.astype(jnp.bfloat16), v_ref[...], preferred_element_type=jnp.float32)
        numer = numer + jnp.dot(
            prob_new.astype(jnp.bfloat16), vn_ref[...], preferred_element_type=jnp.float32
        )
        o_ref[...] = (numer / total).astype(o_ref.dtype)

    per_head = pl.BlockSpec((tokens, HD), lambda h, n: (0, h))
    grid_spec = pltpu.PrefetchScalarGridSpec(
        num_scalar_prefetch=1,
        grid=(heads,),
        in_specs=[
            per_head,
            per_head,
            per_head,
            pl.BlockSpec((context, HD), lambda h, n: (0, h)),
            pl.BlockSpec((context, HD), lambda h, n: (0, h)),
        ],
        out_specs=per_head,
    )
    return pl.pallas_call(
        kernel,
        grid_spec=grid_spec,
        out_shape=jax.ShapeDtypeStruct((tokens, heads * HD), jnp.bfloat16),
    )(length.reshape(1), query, key_new, value_new, keys, values)


def head_reduce(x, base, gain, ident):
    rows, width = x.shape
    share = width // 4
    mesh_kind = pl.DeviceIdType.MESH

    def kernel(x_ref, base_ref, gain_ref, resid_ref, normed_ref, part_in, send_buf, sum_in, sq_out, sq_in,
               send_sem, recv_sem):
        me = lax.axis_index("head")
        group = lax.axis_index("grp")
        core = lax.rem(me, 2)
        partner = me + 1 - 2 * core
        across = lax.rem(me + 2, 4)
        barrier = pltpu.get_barrier_semaphore()
        for peer in (partner, across):
            pl.semaphore_signal(barrier, inc=1, device_id=(group, peer), device_id_type=mesh_kind)
        pl.semaphore_wait(barrier, 2)

        def columns(block):
            return pl.ds(pl.multiple_of(block * share, share), share)

        halves_out = []
        for half in range(2):
            copy = pltpu.make_async_remote_copy(
                src_ref=x_ref.at[:, columns(2 * half + 1 - core)], dst_ref=part_in.at[half],
                send_sem=send_sem.at[half], recv_sem=recv_sem.at[half],
                device_id=(group, partner), device_id_type=mesh_kind,
            )
            copy.start()
            halves_out.append(copy)
        for half in range(2):
            halves_out[half].wait_recv()
            mine = x_ref[:, columns(2 * half + core)].astype(jnp.float32)
            send_buf[half] = (mine + part_in[half].astype(jnp.float32)).astype(send_buf.dtype)
        swap = pltpu.make_async_remote_copy(
            src_ref=send_buf, dst_ref=sum_in, send_sem=send_sem.at[2], recv_sem=recv_sem.at[2],
            device_id=(group, across), device_id_type=mesh_kind,
        )
        swap.start()
        swap.wait_recv()
        square = jnp.zeros((rows, 1), jnp.float32)
        for half in range(2):
            total = (
                base_ref[:, columns(2 * half + core)]
                + send_buf[half].astype(jnp.float32)
                + sum_in[half].astype(jnp.float32)
            )
            resid_ref[half] = total
            square = square + jnp.sum(total * total, axis=1, keepdims=True)
        sq_out[...] = jnp.broadcast_to(square, sq_out.shape)
        last = pltpu.make_async_remote_copy(
            src_ref=sq_out, dst_ref=sq_in, send_sem=send_sem.at[3], recv_sem=recv_sem.at[3],
            device_id=(group, partner), device_id_type=mesh_kind,
        )
        last.start()
        last.wait_recv()
        scale = lax.rsqrt((square + sq_in[:, 0:1]) / width + 1e-05)
        for half in range(2):
            normed_ref[:, half * share:(half + 1) * share] = (
                resid_ref[half] * scale * gain_ref[:, columns(2 * half + core)]
            ).astype(normed_ref.dtype)
        for copy in halves_out:
            copy.wait_send()
        swap.wait_send()
        last.wait_send()

    vmem = pl.BlockSpec(memory_space=pltpu.VMEM)
    return pl.pallas_call(
        kernel,
        out_shape=(
            jax.ShapeDtypeStruct((2, rows, share), jnp.float32),
            jax.ShapeDtypeStruct((rows, 2 * share), jnp.bfloat16),
        ),
        in_specs=[vmem, vmem, vmem],
        out_specs=(vmem, vmem),
        scratch_shapes=[
            pltpu.VMEM((2, rows, share), x.dtype),
            pltpu.VMEM((2, rows, share), x.dtype),
            pltpu.VMEM((2, rows, share), x.dtype),
            pltpu.VMEM((rows, 128), jnp.float32),
            pltpu.VMEM((rows, 128), jnp.float32),
            pltpu.SemaphoreType.DMA((4,)),
            pltpu.SemaphoreType.DMA((4,)),
        ],
        compiler_params=pltpu.CompilerParams(collective_id=ident, has_side_effects=True),
    )(x, base, gain.reshape(1, -1))


def on_device(
    hidden_in,
    attn_gain,
    w_query,
    w_key,
    w_value,
    w_out,
    cache,
    prefix_len,
    mlp_gain,
    expert_ids,
    route_weight,
    w_gate,
    w_up,
    w_down,
):
    group_count = lax.axis_size("grp")
    head_count = lax.axis_size("head")
    my_prompt = lax.axis_index("grp")
    tokens = hidden_in.shape[1]
    width = hidden_in.shape[2]
    heads_here = w_query.shape[1] // HD
    length = prefix_len[my_prompt]
    rows = hidden_in[0].astype(jnp.float32)
    normed = rms_norm(rows, attn_gain).astype(jnp.bfloat16)
    position = (length + jnp.arange(tokens)).astype(jnp.float32)
    query = jnp.dot(normed, w_query, preferred_element_type=jnp.float32).reshape(
        tokens, heads_here, HD
    )
    key_new = jnp.dot(normed, w_key, preferred_element_type=jnp.float32).reshape(
        tokens, heads_here, HD
    )
    value_new = jnp.dot(normed, w_value, preferred_element_type=jnp.float32).reshape(
        tokens, heads_here, HD
    )
    query = (rotate(query, position) * HD ** (-0.5)).astype(jnp.bfloat16)
    key_new = rotate(key_new, position).astype(jnp.bfloat16)
    value_new = value_new.astype(jnp.bfloat16)
    keys, values = [
        lax.all_to_all(cache[part], "grp", split_axis=0, concat_axis=0, tiled=True).reshape(
            group_count * cache.shape[2], heads_here * HD
        )
        for part in range(2)
    ]
    attended = attend(
        length,
        query.reshape(tokens, heads_here * HD),
        key_new.reshape(tokens, heads_here * HD),
        value_new.reshape(tokens, heads_here * HD),
        keys,
        values,
    )
    projected = jnp.dot(attended, w_out, preferred_element_type=jnp.float32)
    resid_blocks, mixed_half = head_reduce(projected.astype(jnp.bfloat16), rows, mlp_gain, 0)
    experts_here = w_gate.shape[0]
    expert_total = experts_here * group_count
    capacity = max(2, 3 * tokens * TOPK // (2 * expert_total))
    chosen = expert_ids[0].reshape(tokens * TOPK)
    weights = route_weight[0]
    pairs = tokens * TOPK
    slots = expert_total * capacity
    one_hot = (chosen[:, None] == jnp.arange(expert_total)[None, :]).astype(jnp.bfloat16)
    earlier = (jnp.arange(pairs)[None, :] < jnp.arange(pairs)[:, None]).astype(jnp.bfloat16)
    before = jnp.dot(earlier, one_hot, preferred_element_type=jnp.float32)
    slot = jnp.sum(before * one_hot.astype(jnp.float32), axis=1).astype(jnp.int32)
    target = chosen * capacity + slot
    place = (target[:, None] == jnp.arange(slots)[None, :]).reshape(tokens, TOPK, slots)
    dispatch = jnp.sum(place.astype(jnp.float32), axis=1).astype(jnp.bfloat16)
    share_width = width // head_count
    head_at = lax.axis_index("head")
    core = lax.rem(head_at, 2)
    chip = head_at // 2
    other_core = 1 - core
    def halves(array, which):
        split = array.reshape(array.shape[:-1] + (2, 2, share_width))
        taken = lax.dynamic_index_in_dim(split, which, axis=split.ndim - 2, keepdims=False)
        return taken.reshape(array.shape[:-1] + (2 * share_width,))

    def row_halves(array, which):
        split = array.reshape((2, 2, share_width) + array.shape[1:])
        taken = lax.dynamic_index_in_dim(split, which, axis=1, keepdims=False)
        return taken.reshape((2 * share_width,) + array.shape[1:])

    half = 2 * share_width
    outgoing = lax.dot_general(
        dispatch, mixed_half, (((0,), (0,)), ((), ())), preferred_element_type=jnp.float32
    ).astype(jnp.bfloat16)
    outgoing = outgoing.reshape(group_count, experts_here, capacity, half)
    arrived = lax.all_to_all(outgoing, "grp", split_axis=0, concat_axis=0, tiled=True)
    partners = [(index, index ^ 1) for index in range(head_count)]
    arrived_other = lax.ppermute(arrived, "head", partners)
    pair_sums = []
    for expert in range(experts_here):
        mine = arrived[:, expert].reshape(group_count * capacity, half)
        other = arrived_other[:, expert].reshape(group_count * capacity, half)
        gate = jnp.dot(mine, row_halves(w_gate[expert], core), preferred_element_type=jnp.float32)
        gate = gate + jnp.dot(other, row_halves(w_gate[expert], other_core), preferred_element_type=jnp.float32)
        upper = jnp.dot(mine, row_halves(w_up[expert], core), preferred_element_type=jnp.float32)
        upper = upper + jnp.dot(other, row_halves(w_up[expert], other_core), preferred_element_type=jnp.float32)
        act = (jax.nn.silu(gate) * upper).astype(jnp.bfloat16)
        mine_part = jnp.dot(act, halves(w_down[expert], core), preferred_element_type=jnp.float32)
        other_part = jnp.dot(act, halves(w_down[expert], other_core), preferred_element_type=jnp.float32)
        partner_part = lax.ppermute(other_part.astype(jnp.bfloat16), "head", partners)
        pair_sums.append(
            (mine_part.astype(jnp.bfloat16).astype(jnp.float32) + partner_part.astype(jnp.float32))
            .astype(jnp.bfloat16)
            .reshape(group_count, capacity, half)
        )
    pair_sum = jnp.stack(pair_sums, axis=1)
    returned = lax.all_to_all(pair_sum, "grp", split_axis=0, concat_axis=0, tiled=True)
    returned = returned.reshape(slots, half)
    weighting = jnp.sum(jnp.where(place, weights[:, :, None], 0.0), axis=1)
    pieces = []
    for _ in range(3):
        piece = weighting.astype(jnp.bfloat16)
        weighting = weighting - piece.astype(jnp.float32)
        pieces.append(piece)
    combined = jnp.dot(jnp.concatenate(pieces, axis=0), returned, preferred_element_type=jnp.float32)
    combined = combined.reshape(3, tokens, half).sum(axis=0)
    combined = combined.reshape(tokens, 2, share_width)
    keep = lax.dynamic_index_in_dim(combined, chip, axis=1, keepdims=False)
    give = lax.dynamic_index_in_dim(combined, 1 - chip, axis=1, keepdims=False)
    moe_share = keep + peer_swap(give, True, 3)
    resid_share = lax.dynamic_index_in_dim(resid_blocks, chip, axis=0, keepdims=False)
    return (resid_share + moe_share).astype(jnp.bfloat16)[None]


def solution(mesh):
    placed = (
        P("grp", None, None),
        P(),
        P(None, "head"),
        P(None, "head"),
        P(None, "head"),
        P("head", None),
        P(None, None, "grp", "head"),
        P(),
        P(),
        P("grp", None, None),
        P("grp", None, None),
        P("grp", None, "head"),
        P("grp", None, "head"),
        P("grp", "head", None),
    )
    return jax.shard_map(
        on_device, mesh=mesh, in_specs=placed, out_specs=P("grp", None, "head"), check_vma=False
    )
```

```python
import jax
import jax.numpy as jnp
from jax import lax
from jax.experimental import pallas as pl
from jax.experimental.pallas import tpu as pltpu
from jax.sharding import PartitionSpec as P

HD = 128
TOPK = 8


def rms_norm(values, gain):
    scale = lax.rsqrt(jnp.mean(values * values, axis=-1, keepdims=True) + 1e-05)
    return values * scale * gain


def rotate(tensor, position):
    half = HD // 2
    inverse = 10000.0 ** (-(jnp.arange(half).astype(jnp.float32) * 2.0) / HD)
    angle = position[:, None] * inverse[None, :]
    cosine = jnp.cos(angle)[:, None, :]
    sine = jnp.sin(angle)[:, None, :]
    first = tensor[..., :half]
    second = tensor[..., half:]
    return jnp.concatenate(
        [first * cosine - second * sine, second * cosine + first * sine], axis=-1
    )


def peer_swap(x, across, ident):
    mesh_kind = pl.DeviceIdType.MESH

    def kernel(x_ref, o_ref, send_sem, recv_sem):
        me = lax.axis_index("head")
        group = lax.axis_index("grp")
        peer = lax.rem(me + 2, 4) if across else me + 1 - 2 * lax.rem(me, 2)
        barrier = pltpu.get_barrier_semaphore()
        pl.semaphore_signal(barrier, inc=1, device_id=(group, peer), device_id_type=mesh_kind)
        pl.semaphore_wait(barrier, 1)
        copy = pltpu.make_async_remote_copy(
            src_ref=x_ref, dst_ref=o_ref, send_sem=send_sem, recv_sem=recv_sem,
            device_id=(group, peer), device_id_type=mesh_kind,
        )
        copy.start()
        copy.wait()

    return pl.pallas_call(
        kernel,
        out_shape=jax.ShapeDtypeStruct(x.shape, x.dtype),
        in_specs=[pl.BlockSpec(memory_space=pl.ANY)],
        out_specs=pl.BlockSpec(memory_space=pl.ANY),
        scratch_shapes=[pltpu.SemaphoreType.DMA(()), pltpu.SemaphoreType.DMA(())],
        compiler_params=pltpu.CompilerParams(collective_id=ident, has_side_effects=True),
    )(x)


def attend(length, query, key_new, value_new, keys, values, w_out):
    tokens = query.shape[0]
    context = keys.shape[0]
    heads = query.shape[1] // HD

    width = w_out.shape[1]

    def kernel(length_ref, q_ref, kn_ref, vn_ref, k_ref, v_ref, w_ref, o_ref, acc_ref):
        head = pl.program_id(0)
        limit = length_ref[0]
        q = q_ref[...]
        contract = (((1,), (1,)), ((), ()))
        score_old = lax.dot_general(q, k_ref[...], contract, preferred_element_type=jnp.float32)
        score_new = lax.dot_general(q, kn_ref[...], contract, preferred_element_type=jnp.float32)
        allow_old = lax.broadcasted_iota(jnp.int32, score_old.shape, 1) < limit
        allow_new = lax.broadcasted_iota(jnp.int32, score_new.shape, 1) <= lax.broadcasted_iota(
            jnp.int32, score_new.shape, 0
        )
        score_old = jnp.where(allow_old, score_old, -1e30)
        score_new = jnp.where(allow_new, score_new, -1e30)
        top = jnp.maximum(
            jnp.max(score_old, axis=1, keepdims=True), jnp.max(score_new, axis=1, keepdims=True)
        )
        prob_old = jnp.where(allow_old, jnp.exp(score_old - top), 0.0)
        prob_new = jnp.where(allow_new, jnp.exp(score_new - top), 0.0)
        total = jnp.sum(prob_old, axis=1, keepdims=True) + jnp.sum(prob_new, axis=1, keepdims=True)
        numer = jnp.dot(prob_old.astype(jnp.bfloat16), v_ref[...], preferred_element_type=jnp.float32)
        numer = numer + jnp.dot(
            prob_new.astype(jnp.bfloat16), vn_ref[...], preferred_element_type=jnp.float32
        )
        attended = (numer / total).astype(jnp.bfloat16)
        term = jnp.dot(attended, w_ref[...], preferred_element_type=jnp.float32)

        @pl.when(head == 0)
        def _():
            acc_ref[...] = term

        @pl.when(head > 0)
        def _():
            acc_ref[...] += term

        @pl.when(head == heads - 1)
        def _():
            o_ref[...] = acc_ref[...].astype(o_ref.dtype)

    per_head = pl.BlockSpec((tokens, HD), lambda h, n: (0, h))
    grid_spec = pltpu.PrefetchScalarGridSpec(
        num_scalar_prefetch=1,
        grid=(heads,),
        in_specs=[
            per_head,
            per_head,
            per_head,
            pl.BlockSpec((context, HD), lambda h, n: (0, h)),
            pl.BlockSpec((context, HD), lambda h, n: (0, h)),
            pl.BlockSpec((HD, width), lambda h, n: (h, 0)),
        ],
        out_specs=pl.BlockSpec((tokens, width), lambda h, n: (0, 0)),
        scratch_shapes=[pltpu.VMEM((tokens, width), jnp.float32)],
    )
    return pl.pallas_call(
        kernel,
        grid_spec=grid_spec,
        out_shape=jax.ShapeDtypeStruct((tokens, width), jnp.bfloat16),
    )(length.reshape(1), query, key_new, value_new, keys, values, w_out)


def head_reduce(x, base, gain, ident):
    rows, width = x.shape
    share = width // 4
    mesh_kind = pl.DeviceIdType.MESH

    def kernel(x_ref, base_ref, gain_ref, resid_ref, normed_ref, part_in, send_buf, sum_in, sq_out, sq_in,
               send_sem, recv_sem):
        me = lax.axis_index("head")
        group = lax.axis_index("grp")
        core = lax.rem(me, 2)
        partner = me + 1 - 2 * core
        across = lax.rem(me + 2, 4)
        barrier = pltpu.get_barrier_semaphore()
        for peer in (partner, across):
            pl.semaphore_signal(barrier, inc=1, device_id=(group, peer), device_id_type=mesh_kind)
        pl.semaphore_wait(barrier, 2)

        def columns(block):
            return pl.ds(pl.multiple_of(block * share, share), share)

        halves_out = []
        for half in range(2):
            copy = pltpu.make_async_remote_copy(
                src_ref=x_ref.at[:, columns(2 * half + 1 - core)], dst_ref=part_in.at[half],
                send_sem=send_sem.at[half], recv_sem=recv_sem.at[half],
                device_id=(group, partner), device_id_type=mesh_kind,
            )
            copy.start()
            halves_out.append(copy)
        for half in range(2):
            halves_out[half].wait_recv()
            mine = x_ref[:, columns(2 * half + core)].astype(jnp.float32)
            send_buf[half] = (mine + part_in[half].astype(jnp.float32)).astype(send_buf.dtype)
        swap = pltpu.make_async_remote_copy(
            src_ref=send_buf, dst_ref=sum_in, send_sem=send_sem.at[2], recv_sem=recv_sem.at[2],
            device_id=(group, across), device_id_type=mesh_kind,
        )
        swap.start()
        swap.wait_recv()
        square = jnp.zeros((rows, 1), jnp.float32)
        for half in range(2):
            total = (
                base_ref[:, columns(2 * half + core)]
                + send_buf[half].astype(jnp.float32)
                + sum_in[half].astype(jnp.float32)
            )
            resid_ref[half] = total
            square = square + jnp.sum(total * total, axis=1, keepdims=True)
        sq_out[...] = jnp.broadcast_to(square, sq_out.shape)
        last = pltpu.make_async_remote_copy(
            src_ref=sq_out, dst_ref=sq_in, send_sem=send_sem.at[3], recv_sem=recv_sem.at[3],
            device_id=(group, partner), device_id_type=mesh_kind,
        )
        last.start()
        last.wait_recv()
        scale = lax.rsqrt((square + sq_in[:, 0:1]) / width + 1e-05)
        for half in range(2):
            normed_ref[:, half * share:(half + 1) * share] = (
                resid_ref[half] * scale * gain_ref[:, columns(2 * half + core)]
            ).astype(normed_ref.dtype)
        for copy in halves_out:
            copy.wait_send()
        swap.wait_send()
        last.wait_send()

    vmem = pl.BlockSpec(memory_space=pltpu.VMEM)
    return pl.pallas_call(
        kernel,
        out_shape=(
            jax.ShapeDtypeStruct((2, rows, share), jnp.float32),
            jax.ShapeDtypeStruct((rows, 2 * share), jnp.bfloat16),
        ),
        in_specs=[vmem, vmem, vmem],
        out_specs=(vmem, vmem),
        scratch_shapes=[
            pltpu.VMEM((2, rows, share), x.dtype),
            pltpu.VMEM((2, rows, share), x.dtype),
            pltpu.VMEM((2, rows, share), x.dtype),
            pltpu.VMEM((rows, 128), jnp.float32),
            pltpu.VMEM((rows, 128), jnp.float32),
            pltpu.SemaphoreType.DMA((4,)),
            pltpu.SemaphoreType.DMA((4,)),
        ],
        compiler_params=pltpu.CompilerParams(collective_id=ident, has_side_effects=True),
    )(x, base, gain.reshape(1, -1))


def on_device(
    hidden_in,
    attn_gain,
    w_query,
    w_key,
    w_value,
    w_out,
    cache,
    prefix_len,
    mlp_gain,
    expert_ids,
    route_weight,
    w_gate,
    w_up,
    w_down,
):
    group_count = lax.axis_size("grp")
    head_count = lax.axis_size("head")
    my_prompt = lax.axis_index("grp")
    tokens = hidden_in.shape[1]
    width = hidden_in.shape[2]
    heads_here = w_query.shape[1] // HD
    length = prefix_len[my_prompt]
    rows = hidden_in[0].astype(jnp.float32)
    normed = rms_norm(rows, attn_gain).astype(jnp.bfloat16)
    position = (length + jnp.arange(tokens)).astype(jnp.float32)
    query = jnp.dot(normed, w_query, preferred_element_type=jnp.float32).reshape(
        tokens, heads_here, HD
    )
    key_new = jnp.dot(normed, w_key, preferred_element_type=jnp.float32).reshape(
        tokens, heads_here, HD
    )
    value_new = jnp.dot(normed, w_value, preferred_element_type=jnp.float32).reshape(
        tokens, heads_here, HD
    )
    query = (rotate(query, position) * HD ** (-0.5)).astype(jnp.bfloat16)
    key_new = rotate(key_new, position).astype(jnp.bfloat16)
    value_new = value_new.astype(jnp.bfloat16)
    keys, values = [
        lax.all_to_all(cache[part], "grp", split_axis=0, concat_axis=0, tiled=True).reshape(
            group_count * cache.shape[2], heads_here * HD
        )
        for part in range(2)
    ]
    projected = attend(
        length,
        query.reshape(tokens, heads_here * HD),
        key_new.reshape(tokens, heads_here * HD),
        value_new.reshape(tokens, heads_here * HD),
        keys,
        values,
        w_out,
    )
    resid_blocks, mixed_half = head_reduce(projected, rows, mlp_gain, 0)
    experts_here = w_gate.shape[0]
    expert_total = experts_here * group_count
    capacity = max(2, 3 * tokens * TOPK // (2 * expert_total))
    chosen = expert_ids[0].reshape(tokens * TOPK)
    weights = route_weight[0]
    pairs = tokens * TOPK
    slots = expert_total * capacity
    one_hot = (chosen[:, None] == jnp.arange(expert_total)[None, :]).astype(jnp.bfloat16)
    earlier = (jnp.arange(pairs)[None, :] < jnp.arange(pairs)[:, None]).astype(jnp.bfloat16)
    before = jnp.dot(earlier, one_hot, preferred_element_type=jnp.float32)
    slot = jnp.sum(before * one_hot.astype(jnp.float32), axis=1).astype(jnp.int32)
    target = chosen * capacity + slot
    place = (target[:, None] == jnp.arange(slots)[None, :]).reshape(tokens, TOPK, slots)
    dispatch = jnp.sum(place.astype(jnp.float32), axis=1).astype(jnp.bfloat16)
    share_width = width // head_count
    head_at = lax.axis_index("head")
    core = lax.rem(head_at, 2)
    chip = head_at // 2
    other_core = 1 - core
    def halves(array, which):
        split = array.reshape(array.shape[:-1] + (2, 2, share_width))
        taken = lax.dynamic_index_in_dim(split, which, axis=split.ndim - 2, keepdims=False)
        return taken.reshape(array.shape[:-1] + (2 * share_width,))

    def row_halves(array, which):
        split = array.reshape((2, 2, share_width) + array.shape[1:])
        taken = lax.dynamic_index_in_dim(split, which, axis=1, keepdims=False)
        return taken.reshape((2 * share_width,) + array.shape[1:])

    half = 2 * share_width
    outgoing = lax.dot_general(
        dispatch, mixed_half, (((0,), (0,)), ((), ())), preferred_element_type=jnp.float32
    ).astype(jnp.bfloat16)
    outgoing = outgoing.reshape(group_count, experts_here, capacity, half)
    arrived = lax.all_to_all(outgoing, "grp", split_axis=0, concat_axis=0, tiled=True)
    partners = [(index, index ^ 1) for index in range(head_count)]
    arrived_other = lax.ppermute(arrived, "head", partners)
    pair_sums = []
    for expert in range(experts_here):
        mine = arrived[:, expert].reshape(group_count * capacity, half)
        other = arrived_other[:, expert].reshape(group_count * capacity, half)
        gate = jnp.dot(mine, row_halves(w_gate[expert], core), preferred_element_type=jnp.float32)
        gate = gate + jnp.dot(other, row_halves(w_gate[expert], other_core), preferred_element_type=jnp.float32)
        upper = jnp.dot(mine, row_halves(w_up[expert], core), preferred_element_type=jnp.float32)
        upper = upper + jnp.dot(other, row_halves(w_up[expert], other_core), preferred_element_type=jnp.float32)
        act = (jax.nn.silu(gate) * upper).astype(jnp.bfloat16)
        mine_part = jnp.dot(act, halves(w_down[expert], core), preferred_element_type=jnp.float32)
        other_part = jnp.dot(act, halves(w_down[expert], other_core), preferred_element_type=jnp.float32)
        partner_part = lax.ppermute(other_part.astype(jnp.bfloat16), "head", partners)
        pair_sums.append(
            (mine_part.astype(jnp.bfloat16).astype(jnp.float32) + partner_part.astype(jnp.float32))
            .astype(jnp.bfloat16)
            .reshape(group_count, capacity, half)
        )
    pair_sum = jnp.stack(pair_sums, axis=1)
    returned = lax.all_to_all(pair_sum, "grp", split_axis=0, concat_axis=0, tiled=True)
    returned = returned.reshape(slots, half)
    weighting = jnp.sum(jnp.where(place, weights[:, :, None], 0.0), axis=1)
    pieces = []
    for _ in range(3):
        piece = weighting.astype(jnp.bfloat16)
        weighting = weighting - piece.astype(jnp.float32)
        pieces.append(piece)
    combined = jnp.dot(jnp.concatenate(pieces, axis=0), returned, preferred_element_type=jnp.float32)
    combined = combined.reshape(3, tokens, half).sum(axis=0)
    combined = combined.reshape(tokens, 2, share_width)
    keep = lax.dynamic_index_in_dim(combined, chip, axis=1, keepdims=False)
    give = lax.dynamic_index_in_dim(combined, 1 - chip, axis=1, keepdims=False)
    moe_share = keep + peer_swap(give, True, 3)
    resid_share = lax.dynamic_index_in_dim(resid_blocks, chip, axis=0, keepdims=False)
    return (resid_share + moe_share).astype(jnp.bfloat16)[None]


def solution(mesh):
    placed = (
        P("grp", None, None),
        P(),
        P(None, "head"),
        P(None, "head"),
        P(None, "head"),
        P("head", None),
        P(None, None, "grp", "head"),
        P(),
        P(),
        P("grp", None, None),
        P("grp", None, None),
        P("grp", None, "head"),
        P("grp", None, "head"),
        P("grp", "head", None),
    )
    return jax.shard_map(
        on_device, mesh=mesh, in_specs=placed, out_specs=P("grp", None, "head"), check_vma=False
    )
```

```python
import jax
import jax.numpy as jnp
from jax import lax
from jax.experimental import pallas as pl
from jax.experimental.pallas import tpu as pltpu
from jax.sharding import PartitionSpec as P

HD = 128
TOPK = 8


def rms_norm(values, gain):
    scale = lax.rsqrt(jnp.mean(values * values, axis=-1, keepdims=True) + 1e-05)
    return values * scale * gain


def rotate(tensor, position):
    half = HD // 2
    inverse = 10000.0 ** (-(jnp.arange(half).astype(jnp.float32) * 2.0) / HD)
    angle = position[:, None] * inverse[None, :]
    cosine = jnp.cos(angle)[:, None, :]
    sine = jnp.sin(angle)[:, None, :]
    first = tensor[..., :half]
    second = tensor[..., half:]
    return jnp.concatenate(
        [first * cosine - second * sine, second * cosine + first * sine], axis=-1
    )


def peer_swap(x, across, ident):
    mesh_kind = pl.DeviceIdType.MESH

    def kernel(x_ref, o_ref, send_sem, recv_sem):
        me = lax.axis_index("head")
        group = lax.axis_index("grp")
        peer = lax.rem(me + 2, 4) if across else me + 1 - 2 * lax.rem(me, 2)
        barrier = pltpu.get_barrier_semaphore()
        pl.semaphore_signal(barrier, inc=1, device_id=(group, peer), device_id_type=mesh_kind)
        pl.semaphore_wait(barrier, 1)
        copy = pltpu.make_async_remote_copy(
            src_ref=x_ref, dst_ref=o_ref, send_sem=send_sem, recv_sem=recv_sem,
            device_id=(group, peer), device_id_type=mesh_kind,
        )
        copy.start()
        copy.wait()

    return pl.pallas_call(
        kernel,
        out_shape=jax.ShapeDtypeStruct(x.shape, x.dtype),
        in_specs=[pl.BlockSpec(memory_space=pl.ANY)],
        out_specs=pl.BlockSpec(memory_space=pl.ANY),
        scratch_shapes=[pltpu.SemaphoreType.DMA(()), pltpu.SemaphoreType.DMA(())],
        compiler_params=pltpu.CompilerParams(collective_id=ident, has_side_effects=True),
    )(x)


def attend(length, query, key_new, value_new, keys, values):
    tokens = query.shape[0]
    context = keys.shape[0]
    heads = query.shape[1] // HD

    def kernel(length_ref, q_ref, kn_ref, vn_ref, k_ref, v_ref, o_ref):
        limit = length_ref[0]
        q = q_ref[...]
        contract = (((1,), (1,)), ((), ()))
        score_old = lax.dot_general(q, k_ref[...], contract, preferred_element_type=jnp.float32)
        score_new = lax.dot_general(q, kn_ref[...], contract, preferred_element_type=jnp.float32)
        allow_old = lax.broadcasted_iota(jnp.int32, score_old.shape, 1) < limit
        allow_new = lax.broadcasted_iota(jnp.int32, score_new.shape, 1) <= lax.broadcasted_iota(
            jnp.int32, score_new.shape, 0
        )
        score_old = jnp.where(allow_old, score_old, -1e30)
        score_new = jnp.where(allow_new, score_new, -1e30)
        top = jnp.maximum(
            jnp.max(score_old, axis=1, keepdims=True), jnp.max(score_new, axis=1, keepdims=True)
        )
        prob_old = jnp.where(allow_old, jnp.exp(score_old - top), 0.0)
        prob_new = jnp.where(allow_new, jnp.exp(score_new - top), 0.0)
        total = jnp.sum(prob_old, axis=1, keepdims=True) + jnp.sum(prob_new, axis=1, keepdims=True)
        numer = jnp.dot(prob_old.astype(jnp.bfloat16), v_ref[...], preferred_element_type=jnp.float32)
        numer = numer + jnp.dot(
            prob_new.astype(jnp.bfloat16), vn_ref[...], preferred_element_type=jnp.float32
        )
        o_ref[...] = (numer / total).astype(o_ref.dtype)

    per_head = pl.BlockSpec((tokens, HD), lambda h, n: (0, h))
    grid_spec = pltpu.PrefetchScalarGridSpec(
        num_scalar_prefetch=1,
        grid=(heads,),
        in_specs=[
            per_head,
            per_head,
            per_head,
            pl.BlockSpec((context, HD), lambda h, n: (0, h)),
            pl.BlockSpec((context, HD), lambda h, n: (0, h)),
        ],
        out_specs=per_head,
    )
    return pl.pallas_call(
        kernel,
        grid_spec=grid_spec,
        out_shape=jax.ShapeDtypeStruct((tokens, heads * HD), jnp.bfloat16),
    )(length.reshape(1), query, key_new, value_new, keys, values)


def head_reduce(x, base, gain, ident):
    rows, width = x.shape
    share = width // 4
    mesh_kind = pl.DeviceIdType.MESH

    def kernel(x_ref, base_ref, gain_ref, resid_ref, normed_ref, part_in, send_buf, sum_in, sq_out, sq_in,
               send_sem, recv_sem):
        me = lax.axis_index("head")
        group = lax.axis_index("grp")
        core = lax.rem(me, 2)
        partner = me + 1 - 2 * core
        across = lax.rem(me + 2, 4)
        barrier = pltpu.get_barrier_semaphore()
        for peer in (partner, across):
            pl.semaphore_signal(barrier, inc=1, device_id=(group, peer), device_id_type=mesh_kind)
        pl.semaphore_wait(barrier, 2)

        def columns(block):
            return pl.ds(pl.multiple_of(block * share, share), share)

        halves_out = []
        for half in range(2):
            copy = pltpu.make_async_remote_copy(
                src_ref=x_ref.at[:, columns(2 * half + 1 - core)], dst_ref=part_in.at[half],
                send_sem=send_sem.at[half], recv_sem=recv_sem.at[half],
                device_id=(group, partner), device_id_type=mesh_kind,
            )
            copy.start()
            halves_out.append(copy)
        for half in range(2):
            halves_out[half].wait_recv()
            mine = x_ref[:, columns(2 * half + core)].astype(jnp.float32)
            send_buf[half] = (mine + part_in[half].astype(jnp.float32)).astype(send_buf.dtype)
        swap = pltpu.make_async_remote_copy(
            src_ref=send_buf, dst_ref=sum_in, send_sem=send_sem.at[2], recv_sem=recv_sem.at[2],
            device_id=(group, across), device_id_type=mesh_kind,
        )
        swap.start()
        swap.wait_recv()
        square = jnp.zeros((rows, 1), jnp.float32)
        for half in range(2):
            total = (
                base_ref[:, columns(2 * half + core)]
                + send_buf[half].astype(jnp.float32)
                + sum_in[half].astype(jnp.float32)
            )
            resid_ref[half] = total
            square = square + jnp.sum(total * total, axis=1, keepdims=True)
        sq_out[...] = jnp.broadcast_to(square, sq_out.shape)
        last = pltpu.make_async_remote_copy(
            src_ref=sq_out, dst_ref=sq_in, send_sem=send_sem.at[3], recv_sem=recv_sem.at[3],
            device_id=(group, partner), device_id_type=mesh_kind,
        )
        last.start()
        last.wait_recv()
        scale = lax.rsqrt((square + sq_in[:, 0:1]) / width + 1e-05)
        for half in range(2):
            normed_ref[:, half * share:(half + 1) * share] = (
                resid_ref[half] * scale * gain_ref[:, columns(2 * half + core)]
            ).astype(normed_ref.dtype)
        for copy in halves_out:
            copy.wait_send()
        swap.wait_send()
        last.wait_send()

    vmem = pl.BlockSpec(memory_space=pltpu.VMEM)
    return pl.pallas_call(
        kernel,
        out_shape=(
            jax.ShapeDtypeStruct((2, rows, share), jnp.float32),
            jax.ShapeDtypeStruct((rows, 2 * share), jnp.bfloat16),
        ),
        in_specs=[vmem, vmem, vmem],
        out_specs=(vmem, vmem),
        scratch_shapes=[
            pltpu.VMEM((2, rows, share), x.dtype),
            pltpu.VMEM((2, rows, share), x.dtype),
            pltpu.VMEM((2, rows, share), x.dtype),
            pltpu.VMEM((rows, 128), jnp.float32),
            pltpu.VMEM((rows, 128), jnp.float32),
            pltpu.SemaphoreType.DMA((4,)),
            pltpu.SemaphoreType.DMA((4,)),
        ],
        compiler_params=pltpu.CompilerParams(collective_id=ident, has_side_effects=True),
    )(x, base, gain.reshape(1, -1))


def on_device(
    hidden_in,
    attn_gain,
    w_query,
    w_key,
    w_value,
    w_out,
    cache,
    prefix_len,
    mlp_gain,
    expert_ids,
    route_weight,
    w_gate,
    w_up,
    w_down,
):
    group_count = lax.axis_size("grp")
    head_count = lax.axis_size("head")
    my_prompt = lax.axis_index("grp")
    tokens = hidden_in.shape[1]
    width = hidden_in.shape[2]
    heads_here = w_query.shape[1] // HD
    length = prefix_len[my_prompt]
    rows = hidden_in[0].astype(jnp.float32)
    normed = rms_norm(rows, attn_gain).astype(jnp.bfloat16)
    position = (length + jnp.arange(tokens)).astype(jnp.float32)
    query = jnp.dot(normed, w_query, preferred_element_type=jnp.float32).reshape(
        tokens, heads_here, HD
    )
    key_new = jnp.dot(normed, w_key, preferred_element_type=jnp.float32).reshape(
        tokens, heads_here, HD
    )
    value_new = jnp.dot(normed, w_value, preferred_element_type=jnp.float32).reshape(
        tokens, heads_here, HD
    )
    query = (rotate(query, position) * HD ** (-0.5)).astype(jnp.bfloat16)
    key_new = rotate(key_new, position).astype(jnp.bfloat16)
    value_new = value_new.astype(jnp.bfloat16)
    keys, values = [
        lax.all_to_all(cache[part], "grp", split_axis=0, concat_axis=0, tiled=True).reshape(
            group_count * cache.shape[2], heads_here * HD
        )
        for part in range(2)
    ]
    attended = attend(
        length,
        query.reshape(tokens, heads_here * HD),
        key_new.reshape(tokens, heads_here * HD),
        value_new.reshape(tokens, heads_here * HD),
        keys,
        values,
    )
    projected = jnp.dot(attended, w_out, preferred_element_type=jnp.float32)
    resid_blocks, mixed_half = head_reduce(projected.astype(jnp.bfloat16), rows, mlp_gain, 0)
    experts_here = w_gate.shape[0]
    expert_total = experts_here * group_count
    capacity = max(2, 3 * tokens * TOPK // (2 * expert_total))
    chosen = expert_ids[0].reshape(tokens * TOPK)
    weights = route_weight[0]
    pairs = tokens * TOPK
    slots = expert_total * capacity
    one_hot = (chosen[:, None] == jnp.arange(expert_total)[None, :]).astype(jnp.bfloat16)
    earlier = (jnp.arange(pairs)[None, :] < jnp.arange(pairs)[:, None]).astype(jnp.bfloat16)
    before = jnp.dot(earlier, one_hot, preferred_element_type=jnp.float32)
    slot = jnp.sum(before * one_hot.astype(jnp.float32), axis=1).astype(jnp.int32)
    target = chosen * capacity + slot
    place = (target[:, None] == jnp.arange(slots)[None, :]).reshape(tokens, TOPK, slots)
    dispatch = jnp.sum(place.astype(jnp.float32), axis=1).astype(jnp.bfloat16)
    share_width = width // head_count
    head_at = lax.axis_index("head")
    core = lax.rem(head_at, 2)
    chip = head_at // 2
    other_core = 1 - core
    def halves(array, which):
        split = array.reshape(array.shape[:-1] + (2, 2, share_width))
        taken = lax.dynamic_index_in_dim(split, which, axis=split.ndim - 2, keepdims=False)
        return taken.reshape(array.shape[:-1] + (2 * share_width,))

    def row_halves(array, which):
        split = array.reshape((2, 2, share_width) + array.shape[1:])
        taken = lax.dynamic_index_in_dim(split, which, axis=1, keepdims=False)
        return taken.reshape((2 * share_width,) + array.shape[1:])

    half = 2 * share_width
    outgoing = lax.dot_general(
        dispatch, mixed_half, (((0,), (0,)), ((), ())), preferred_element_type=jnp.float32
    ).astype(jnp.bfloat16)
    outgoing = outgoing.reshape(group_count, experts_here, capacity, half)
    arrived = lax.all_to_all(outgoing, "grp", split_axis=0, concat_axis=0, tiled=True)
    partners = [(index, index ^ 1) for index in range(head_count)]
    arrived_other = lax.ppermute(arrived, "head", partners)
    pair_sums = []
    for expert in range(experts_here):
        mine = arrived[:, expert].reshape(group_count * capacity, half)
        other = arrived_other[:, expert].reshape(group_count * capacity, half)
        gate = jnp.dot(mine, row_halves(w_gate[expert], core), preferred_element_type=jnp.float32)
        gate = gate + jnp.dot(other, row_halves(w_gate[expert], other_core), preferred_element_type=jnp.float32)
        upper = jnp.dot(mine, row_halves(w_up[expert], core), preferred_element_type=jnp.float32)
        upper = upper + jnp.dot(other, row_halves(w_up[expert], other_core), preferred_element_type=jnp.float32)
        act = (jax.nn.silu(gate) * upper).astype(jnp.bfloat16)
        mine_part = jnp.dot(act, halves(w_down[expert], core), preferred_element_type=jnp.float32)
        other_part = jnp.dot(act, halves(w_down[expert], other_core), preferred_element_type=jnp.float32)
        partner_part = lax.ppermute(other_part.astype(jnp.bfloat16), "head", partners)
        pair_sums.append(
            (mine_part.astype(jnp.bfloat16).astype(jnp.float32) + partner_part.astype(jnp.float32))
            .astype(jnp.bfloat16)
            .reshape(group_count, capacity, half)
        )
    pair_sum = jnp.stack(pair_sums, axis=1)
    returned = lax.all_to_all(pair_sum, "grp", split_axis=0, concat_axis=0, tiled=True)
    returned = returned.reshape(slots, half)
    weighting = jnp.sum(jnp.where(place, weights[:, :, None], 0.0), axis=1)
    pieces = []
    for _ in range(3):
        piece = weighting.astype(jnp.bfloat16)
        weighting = weighting - piece.astype(jnp.float32)
        pieces.append(piece)
    combined = jnp.dot(jnp.concatenate(pieces, axis=0), returned, preferred_element_type=jnp.float32)
    combined = combined.reshape(3, tokens, half).sum(axis=0)
    combined = combined.reshape(tokens, 2, share_width)
    keep = lax.dynamic_index_in_dim(combined, chip, axis=1, keepdims=False)
    give = lax.dynamic_index_in_dim(combined, 1 - chip, axis=1, keepdims=False)
    moe_share = keep + peer_swap(give.astype(jnp.bfloat16), True, 3).astype(jnp.float32)
    resid_share = lax.dynamic_index_in_dim(resid_blocks, chip, axis=0, keepdims=False)
    return (resid_share + moe_share).astype(jnp.bfloat16)[None]


def solution(mesh):
    placed = (
        P("grp", None, None),
        P(),
        P(None, "head"),
        P(None, "head"),
        P(None, "head"),
        P("head", None),
        P(None, None, "grp", "head"),
        P(),
        P(),
        P("grp", None, None),
        P("grp", None, None),
        P("grp", None, "head"),
        P("grp", None, "head"),
        P("grp", "head", None),
    )
    return jax.shard_map(
        on_device, mesh=mesh, in_specs=placed, out_specs=P("grp", None, "head"), check_vma=False
    )
```

```python
import jax
import jax.numpy as jnp
from jax import lax
from jax.experimental import pallas as pl
from jax.experimental.pallas import tpu as pltpu
from jax.sharding import PartitionSpec as P

HD = 128
TOPK = 8


def rms_norm(values, gain):
    scale = lax.rsqrt(jnp.mean(values * values, axis=-1, keepdims=True) + 1e-05)
    return values * scale * gain


def rotate(tensor, position):
    half = HD // 2
    inverse = 10000.0 ** (-(jnp.arange(half).astype(jnp.float32) * 2.0) / HD)
    angle = position[:, None] * inverse[None, :]
    cosine = jnp.cos(angle)[:, None, :]
    sine = jnp.sin(angle)[:, None, :]
    first = tensor[..., :half]
    second = tensor[..., half:]
    return jnp.concatenate(
        [first * cosine - second * sine, second * cosine + first * sine], axis=-1
    )


def peer_swap(x, across, ident):
    mesh_kind = pl.DeviceIdType.MESH

    def kernel(x_ref, o_ref, send_sem, recv_sem):
        me = lax.axis_index("head")
        group = lax.axis_index("grp")
        peer = lax.rem(me + 2, 4) if across else me + 1 - 2 * lax.rem(me, 2)
        barrier = pltpu.get_barrier_semaphore()
        pl.semaphore_signal(barrier, inc=1, device_id=(group, peer), device_id_type=mesh_kind)
        pl.semaphore_wait(barrier, 1)
        copy = pltpu.make_async_remote_copy(
            src_ref=x_ref, dst_ref=o_ref, send_sem=send_sem, recv_sem=recv_sem,
            device_id=(group, peer), device_id_type=mesh_kind,
        )
        copy.start()
        copy.wait()

    return pl.pallas_call(
        kernel,
        out_shape=jax.ShapeDtypeStruct(x.shape, x.dtype),
        in_specs=[pl.BlockSpec(memory_space=pl.ANY)],
        out_specs=pl.BlockSpec(memory_space=pl.ANY),
        scratch_shapes=[pltpu.SemaphoreType.DMA(()), pltpu.SemaphoreType.DMA(())],
        compiler_params=pltpu.CompilerParams(collective_id=ident, has_side_effects=True),
    )(x)


def attend(length, query, key_new, value_new, keys, values):
    tokens = query.shape[0]
    context = keys.shape[0]
    heads = query.shape[1] // HD

    def kernel(length_ref, q_ref, kn_ref, vn_ref, k_ref, v_ref, o_ref):
        limit = length_ref[0]
        q = q_ref[...]
        contract = (((1,), (1,)), ((), ()))
        score_old = lax.dot_general(q, k_ref[...], contract, preferred_element_type=jnp.float32)
        score_new = lax.dot_general(q, kn_ref[...], contract, preferred_element_type=jnp.float32)
        allow_old = lax.broadcasted_iota(jnp.int32, score_old.shape, 1) < limit
        allow_new = lax.broadcasted_iota(jnp.int32, score_new.shape, 1) <= lax.broadcasted_iota(
            jnp.int32, score_new.shape, 0
        )
        score_old = jnp.where(allow_old, score_old, -1e30)
        score_new = jnp.where(allow_new, score_new, -1e30)
        top = jnp.maximum(
            jnp.max(score_old, axis=1, keepdims=True), jnp.max(score_new, axis=1, keepdims=True)
        )
        prob_old = jnp.where(allow_old, jnp.exp(score_old - top), 0.0)
        prob_new = jnp.where(allow_new, jnp.exp(score_new - top), 0.0)
        total = jnp.sum(prob_old, axis=1, keepdims=True) + jnp.sum(prob_new, axis=1, keepdims=True)
        numer = jnp.dot(prob_old.astype(jnp.bfloat16), v_ref[...], preferred_element_type=jnp.float32)
        numer = numer + jnp.dot(
            prob_new.astype(jnp.bfloat16), vn_ref[...], preferred_element_type=jnp.float32
        )
        o_ref[...] = (numer / total).astype(o_ref.dtype)

    per_head = pl.BlockSpec((tokens, HD), lambda h, n: (0, h))
    grid_spec = pltpu.PrefetchScalarGridSpec(
        num_scalar_prefetch=1,
        grid=(heads,),
        in_specs=[
            per_head,
            per_head,
            per_head,
            pl.BlockSpec((context, HD), lambda h, n: (0, h)),
            pl.BlockSpec((context, HD), lambda h, n: (0, h)),
        ],
        out_specs=per_head,
    )
    return pl.pallas_call(
        kernel,
        grid_spec=grid_spec,
        out_shape=jax.ShapeDtypeStruct((tokens, heads * HD), jnp.bfloat16),
    )(length.reshape(1), query, key_new, value_new, keys, values)


def head_reduce(x, base, gain, ident):
    rows, width = x.shape
    share = width // 4
    mesh_kind = pl.DeviceIdType.MESH

    def kernel(x_ref, base_ref, gain_ref, resid_ref, normed_ref, part_in, send_buf, sum_in, sq_out, sq_in,
               send_sem, recv_sem):
        me = lax.axis_index("head")
        group = lax.axis_index("grp")
        core = lax.rem(me, 2)
        partner = me + 1 - 2 * core
        across = lax.rem(me + 2, 4)
        barrier = pltpu.get_barrier_semaphore()
        for peer in (partner, across):
            pl.semaphore_signal(barrier, inc=1, device_id=(group, peer), device_id_type=mesh_kind)
        pl.semaphore_wait(barrier, 2)

        def columns(block):
            return pl.ds(pl.multiple_of(block * share, share), share)

        halves_out = []
        for half in range(2):
            copy = pltpu.make_async_remote_copy(
                src_ref=x_ref.at[:, columns(2 * half + 1 - core)], dst_ref=part_in.at[half],
                send_sem=send_sem.at[half], recv_sem=recv_sem.at[half],
                device_id=(group, partner), device_id_type=mesh_kind,
            )
            copy.start()
            halves_out.append(copy)
        for half in range(2):
            halves_out[half].wait_recv()
            mine = x_ref[:, columns(2 * half + core)].astype(jnp.float32)
            send_buf[half] = (mine + part_in[half].astype(jnp.float32)).astype(send_buf.dtype)
        swap = pltpu.make_async_remote_copy(
            src_ref=send_buf, dst_ref=sum_in, send_sem=send_sem.at[2], recv_sem=recv_sem.at[2],
            device_id=(group, across), device_id_type=mesh_kind,
        )
        swap.start()
        swap.wait_recv()
        square = jnp.zeros((rows, 1), jnp.float32)
        for half in range(2):
            total = (
                base_ref[:, columns(2 * half + core)]
                + send_buf[half].astype(jnp.float32)
                + sum_in[half].astype(jnp.float32)
            )
            resid_ref[half] = total
            square = square + jnp.sum(total * total, axis=1, keepdims=True)
        sq_out[...] = jnp.broadcast_to(square, sq_out.shape)
        last = pltpu.make_async_remote_copy(
            src_ref=sq_out, dst_ref=sq_in, send_sem=send_sem.at[3], recv_sem=recv_sem.at[3],
            device_id=(group, partner), device_id_type=mesh_kind,
        )
        last.start()
        last.wait_recv()
        scale = lax.rsqrt((square + sq_in[:, 0:1]) / width + 1e-05)
        for half in range(2):
            normed_ref[:, half * share:(half + 1) * share] = (
                resid_ref[half] * scale * gain_ref[:, columns(2 * half + core)]
            ).astype(normed_ref.dtype)
        for copy in halves_out:
            copy.wait_send()
        swap.wait_send()
        last.wait_send()

    vmem = pl.BlockSpec(memory_space=pltpu.VMEM)
    return pl.pallas_call(
        kernel,
        out_shape=(
            jax.ShapeDtypeStruct((2, rows, share), jnp.float32),
            jax.ShapeDtypeStruct((rows, 2 * share), jnp.bfloat16),
        ),
        in_specs=[vmem, vmem, vmem],
        out_specs=(vmem, vmem),
        scratch_shapes=[
            pltpu.VMEM((2, rows, share), x.dtype),
            pltpu.VMEM((2, rows, share), x.dtype),
            pltpu.VMEM((2, rows, share), x.dtype),
            pltpu.VMEM((rows, 128), jnp.float32),
            pltpu.VMEM((rows, 128), jnp.float32),
            pltpu.SemaphoreType.DMA((4,)),
            pltpu.SemaphoreType.DMA((4,)),
        ],
        compiler_params=pltpu.CompilerParams(collective_id=ident, has_side_effects=True),
    )(x, base, gain.reshape(1, -1))


def on_device(
    hidden_in,
    attn_gain,
    w_query,
    w_key,
    w_value,
    w_out,
    cache,
    prefix_len,
    mlp_gain,
    expert_ids,
    route_weight,
    w_gate,
    w_up,
    w_down,
):
    group_count = lax.axis_size("grp")
    head_count = lax.axis_size("head")
    my_prompt = lax.axis_index("grp")
    tokens = hidden_in.shape[1]
    width = hidden_in.shape[2]
    heads_here = w_query.shape[1] // HD
    length = prefix_len[my_prompt]
    rows = hidden_in[0].astype(jnp.float32)
    normed = rms_norm(rows, attn_gain).astype(jnp.bfloat16)
    position = (length + jnp.arange(tokens)).astype(jnp.float32)
    query = jnp.dot(normed, w_query, preferred_element_type=jnp.float32).reshape(
        tokens, heads_here, HD
    )
    key_new = jnp.dot(normed, w_key, preferred_element_type=jnp.float32).reshape(
        tokens, heads_here, HD
    )
    value_new = jnp.dot(normed, w_value, preferred_element_type=jnp.float32).reshape(
        tokens, heads_here, HD
    )
    query = (rotate(query, position) * HD ** (-0.5)).astype(jnp.bfloat16)
    key_new = rotate(key_new, position).astype(jnp.bfloat16)
    value_new = value_new.astype(jnp.bfloat16)
    keys, values = [
        lax.all_to_all(cache[part], "grp", split_axis=0, concat_axis=0, tiled=True).reshape(
            group_count * cache.shape[2], heads_here * HD
        )
        for part in range(2)
    ]
    attended = attend(
        length,
        query.reshape(tokens, heads_here * HD),
        key_new.reshape(tokens, heads_here * HD),
        value_new.reshape(tokens, heads_here * HD),
        keys,
        values,
    )
    projected = jnp.dot(attended, w_out, preferred_element_type=jnp.float32)
    resid_blocks, mixed_half = head_reduce(projected.astype(jnp.bfloat16), rows, mlp_gain, 0)
    experts_here = w_gate.shape[0]
    expert_total = experts_here * group_count
    capacity = max(2, 3 * tokens * TOPK // (2 * expert_total))
    chosen = expert_ids[0].reshape(tokens * TOPK)
    weights = route_weight[0]
    pairs = tokens * TOPK
    slots = expert_total * capacity
    one_hot = (chosen[:, None] == jnp.arange(expert_total)[None, :]).astype(jnp.bfloat16)
    earlier = (jnp.arange(pairs)[None, :] < jnp.arange(pairs)[:, None]).astype(jnp.bfloat16)
    before = jnp.dot(earlier, one_hot, preferred_element_type=jnp.float32)
    slot = jnp.sum(before * one_hot.astype(jnp.float32), axis=1).astype(jnp.int32)
    target = chosen * capacity + slot
    place = (target[:, None] == jnp.arange(slots)[None, :]).reshape(tokens, TOPK, slots)
    dispatch = jnp.sum(place.astype(jnp.float32), axis=1).astype(jnp.bfloat16)
    share_width = width // head_count
    head_at = lax.axis_index("head")
    core = lax.rem(head_at, 2)
    chip = head_at // 2
    other_core = 1 - core
    def halves(array, which):
        split = array.reshape(array.shape[:-1] + (2, 2, share_width))
        taken = lax.dynamic_index_in_dim(split, which, axis=split.ndim - 2, keepdims=False)
        return taken.reshape(array.shape[:-1] + (2 * share_width,))

    def row_halves(array, which):
        split = array.reshape((2, 2, share_width) + array.shape[1:])
        taken = lax.dynamic_index_in_dim(split, which, axis=1, keepdims=False)
        return taken.reshape((2 * share_width,) + array.shape[1:])

    half = 2 * share_width
    outgoing = lax.dot_general(
        dispatch, mixed_half, (((0,), (0,)), ((), ())), preferred_element_type=jnp.float32
    ).astype(jnp.bfloat16)
    outgoing = outgoing.reshape(group_count, experts_here, capacity, half)
    arrived = lax.all_to_all(outgoing, "grp", split_axis=0, concat_axis=0, tiled=True)
    partners = [(index, index ^ 1) for index in range(head_count)]
    arrived_other = lax.ppermute(arrived, "head", partners)
    pair_sums = []
    for expert in range(experts_here):
        mine = arrived[:, expert].reshape(group_count * capacity, half)
        other = arrived_other[:, expert].reshape(group_count * capacity, half)
        gate = jnp.dot(mine, row_halves(w_gate[expert], core), preferred_element_type=jnp.float32)
        gate = gate + jnp.dot(other, row_halves(w_gate[expert], other_core), preferred_element_type=jnp.float32)
        upper = jnp.dot(mine, row_halves(w_up[expert], core), preferred_element_type=jnp.float32)
        upper = upper + jnp.dot(other, row_halves(w_up[expert], other_core), preferred_element_type=jnp.float32)
        act = (jax.nn.silu(gate) * upper).astype(jnp.bfloat16)
        mine_part = jnp.dot(act, halves(w_down[expert], core), preferred_element_type=jnp.float32)
        other_part = jnp.dot(act, halves(w_down[expert], other_core), preferred_element_type=jnp.float32)
        partner_part = lax.ppermute(other_part.astype(jnp.bfloat16), "head", partners)
        pair_sums.append(
            (
                mine_part.astype(jnp.bfloat16).reshape(group_count, capacity, half),
                partner_part.reshape(group_count, capacity, half),
            )
        )
    mine_all = jnp.stack([mine for mine, _ in pair_sums], axis=1).astype(jnp.float32)
    partner_all = jnp.stack([other for _, other in pair_sums], axis=1).astype(jnp.float32)
    pair_sum = (mine_all + partner_all).astype(jnp.bfloat16)
    returned = lax.all_to_all(pair_sum, "grp", split_axis=0, concat_axis=0, tiled=True)
    returned = returned.reshape(slots, half)
    weighting = jnp.sum(jnp.where(place, weights[:, :, None], 0.0), axis=1)
    pieces = []
    for _ in range(3):
        piece = weighting.astype(jnp.bfloat16)
        weighting = weighting - piece.astype(jnp.float32)
        pieces.append(piece)
    combined = jnp.dot(jnp.concatenate(pieces, axis=0), returned, preferred_element_type=jnp.float32)
    combined = combined.reshape(3, tokens, half).sum(axis=0)
    combined = combined.reshape(tokens, 2, share_width)
    keep = lax.dynamic_index_in_dim(combined, chip, axis=1, keepdims=False)
    give = lax.dynamic_index_in_dim(combined, 1 - chip, axis=1, keepdims=False)
    moe_share = keep + peer_swap(give.astype(jnp.bfloat16), True, 3).astype(jnp.float32)
    resid_share = lax.dynamic_index_in_dim(resid_blocks, chip, axis=0, keepdims=False)
    return (resid_share + moe_share).astype(jnp.bfloat16)[None]


def solution(mesh):
    placed = (
        P("grp", None, None),
        P(),
        P(None, "head"),
        P(None, "head"),
        P(None, "head"),
        P("head", None),
        P(None, None, "grp", "head"),
        P(),
        P(),
        P("grp", None, None),
        P("grp", None, None),
        P("grp", None, "head"),
        P("grp", None, "head"),
        P("grp", "head", None),
    )
    return jax.shard_map(
        on_device, mesh=mesh, in_specs=placed, out_specs=P("grp", None, "head"), check_vma=False
    )
```

```python
import jax
import jax.numpy as jnp
from jax import lax
from jax.experimental import pallas as pl
from jax.experimental.pallas import tpu as pltpu
from jax.sharding import PartitionSpec as P

HD = 128
TOPK = 8


def rms_norm(values, gain):
    scale = lax.rsqrt(jnp.mean(values * values, axis=-1, keepdims=True) + 1e-05)
    return values * scale * gain


def rotate(tensor, position):
    half = HD // 2
    inverse = 10000.0 ** (-(jnp.arange(half).astype(jnp.float32) * 2.0) / HD)
    angle = position[:, None] * inverse[None, :]
    cosine = jnp.cos(angle)[:, None, :]
    sine = jnp.sin(angle)[:, None, :]
    first = tensor[..., :half]
    second = tensor[..., half:]
    return jnp.concatenate(
        [first * cosine - second * sine, second * cosine + first * sine], axis=-1
    )


def peer_swap(x, across, ident):
    mesh_kind = pl.DeviceIdType.MESH

    def kernel(x_ref, o_ref, send_sem, recv_sem):
        me = lax.axis_index("head")
        group = lax.axis_index("grp")
        peer = lax.rem(me + 2, 4) if across else me + 1 - 2 * lax.rem(me, 2)
        barrier = pltpu.get_barrier_semaphore()
        pl.semaphore_signal(barrier, inc=1, device_id=(group, peer), device_id_type=mesh_kind)
        pl.semaphore_wait(barrier, 1)
        copy = pltpu.make_async_remote_copy(
            src_ref=x_ref, dst_ref=o_ref, send_sem=send_sem, recv_sem=recv_sem,
            device_id=(group, peer), device_id_type=mesh_kind,
        )
        copy.start()
        copy.wait()

    return pl.pallas_call(
        kernel,
        out_shape=jax.ShapeDtypeStruct(x.shape, x.dtype),
        in_specs=[pl.BlockSpec(memory_space=pl.ANY)],
        out_specs=pl.BlockSpec(memory_space=pl.ANY),
        scratch_shapes=[pltpu.SemaphoreType.DMA(()), pltpu.SemaphoreType.DMA(())],
        compiler_params=pltpu.CompilerParams(collective_id=ident, has_side_effects=True),
    )(x)


def attend(length, query, key_new, value_new, keys, values):
    tokens = query.shape[0]
    context = keys.shape[0]
    heads = query.shape[1] // HD

    def kernel(length_ref, q_ref, kn_ref, vn_ref, k_ref, v_ref, o_ref):
        limit = length_ref[0]
        q = q_ref[...]
        contract = (((1,), (1,)), ((), ()))
        score_old = lax.dot_general(q, k_ref[...], contract, preferred_element_type=jnp.float32)
        score_new = lax.dot_general(q, kn_ref[...], contract, preferred_element_type=jnp.float32)
        allow_old = lax.broadcasted_iota(jnp.int32, score_old.shape, 1) < limit
        allow_new = lax.broadcasted_iota(jnp.int32, score_new.shape, 1) <= lax.broadcasted_iota(
            jnp.int32, score_new.shape, 0
        )
        score_old = jnp.where(allow_old, score_old, -1e30)
        score_new = jnp.where(allow_new, score_new, -1e30)
        top = jnp.maximum(
            jnp.max(score_old, axis=1, keepdims=True), jnp.max(score_new, axis=1, keepdims=True)
        )
        prob_old = jnp.where(allow_old, jnp.exp(score_old - top), 0.0)
        prob_new = jnp.where(allow_new, jnp.exp(score_new - top), 0.0)
        total = jnp.sum(prob_old, axis=1, keepdims=True) + jnp.sum(prob_new, axis=1, keepdims=True)
        numer = jnp.dot(prob_old.astype(jnp.bfloat16), v_ref[...], preferred_element_type=jnp.float32)
        numer = numer + jnp.dot(
            prob_new.astype(jnp.bfloat16), vn_ref[...], preferred_element_type=jnp.float32
        )
        o_ref[...] = (numer / total).astype(o_ref.dtype)

    per_head = pl.BlockSpec((tokens, HD), lambda h, n: (0, h))
    grid_spec = pltpu.PrefetchScalarGridSpec(
        num_scalar_prefetch=1,
        grid=(heads,),
        in_specs=[
            per_head,
            per_head,
            per_head,
            pl.BlockSpec((context, HD), lambda h, n: (0, h)),
            pl.BlockSpec((context, HD), lambda h, n: (0, h)),
        ],
        out_specs=per_head,
    )
    return pl.pallas_call(
        kernel,
        grid_spec=grid_spec,
        out_shape=jax.ShapeDtypeStruct((tokens, heads * HD), jnp.bfloat16),
    )(length.reshape(1), query, key_new, value_new, keys, values)


def head_reduce(x, base, gain, ident):
    rows, width = x.shape
    share = width // 4
    mesh_kind = pl.DeviceIdType.MESH

    def kernel(x_ref, base_ref, gain_ref, resid_ref, normed_ref, part_in, send_buf, sum_in, sq_out, sq_in,
               send_sem, recv_sem):
        me = lax.axis_index("head")
        group = lax.axis_index("grp")
        core = lax.rem(me, 2)
        partner = me + 1 - 2 * core
        across = lax.rem(me + 2, 4)
        barrier = pltpu.get_barrier_semaphore()
        for peer in (partner, across):
            pl.semaphore_signal(barrier, inc=1, device_id=(group, peer), device_id_type=mesh_kind)
        pl.semaphore_wait(barrier, 2)

        def columns(block):
            return pl.ds(pl.multiple_of(block * share, share), share)

        halves_out = []
        for half in range(2):
            copy = pltpu.make_async_remote_copy(
                src_ref=x_ref.at[:, columns(2 * half + 1 - core)], dst_ref=part_in.at[half],
                send_sem=send_sem.at[half], recv_sem=recv_sem.at[half],
                device_id=(group, partner), device_id_type=mesh_kind,
            )
            copy.start()
            halves_out.append(copy)
        for half in range(2):
            halves_out[half].wait_recv()
            mine = x_ref[:, columns(2 * half + core)].astype(jnp.float32)
            send_buf[half] = (mine + part_in[half].astype(jnp.float32)).astype(send_buf.dtype)
        swap = pltpu.make_async_remote_copy(
            src_ref=send_buf, dst_ref=sum_in, send_sem=send_sem.at[2], recv_sem=recv_sem.at[2],
            device_id=(group, across), device_id_type=mesh_kind,
        )
        swap.start()
        swap.wait_recv()
        square = jnp.zeros((rows, 1), jnp.float32)
        for half in range(2):
            total = (
                base_ref[:, columns(2 * half + core)]
                + send_buf[half].astype(jnp.float32)
                + sum_in[half].astype(jnp.float32)
            )
            resid_ref[half] = total
            square = square + jnp.sum(total * total, axis=1, keepdims=True)
        sq_out[...] = jnp.broadcast_to(square, sq_out.shape)
        last = pltpu.make_async_remote_copy(
            src_ref=sq_out, dst_ref=sq_in, send_sem=send_sem.at[3], recv_sem=recv_sem.at[3],
            device_id=(group, partner), device_id_type=mesh_kind,
        )
        last.start()
        last.wait_recv()
        scale = lax.rsqrt((square + sq_in[:, 0:1]) / width + 1e-05)
        for half in range(2):
            normed_ref[:, half * share:(half + 1) * share] = (
                resid_ref[half] * scale * gain_ref[:, columns(2 * half + core)]
            ).astype(normed_ref.dtype)
        for copy in halves_out:
            copy.wait_send()
        swap.wait_send()
        last.wait_send()

    vmem = pl.BlockSpec(memory_space=pltpu.VMEM)
    return pl.pallas_call(
        kernel,
        out_shape=(
            jax.ShapeDtypeStruct((2, rows, share), jnp.float32),
            jax.ShapeDtypeStruct((rows, 2 * share), jnp.bfloat16),
        ),
        in_specs=[vmem, vmem, vmem],
        out_specs=(vmem, vmem),
        scratch_shapes=[
            pltpu.VMEM((2, rows, share), x.dtype),
            pltpu.VMEM((2, rows, share), x.dtype),
            pltpu.VMEM((2, rows, share), x.dtype),
            pltpu.VMEM((rows, 128), jnp.float32),
            pltpu.VMEM((rows, 128), jnp.float32),
            pltpu.SemaphoreType.DMA((4,)),
            pltpu.SemaphoreType.DMA((4,)),
        ],
        compiler_params=pltpu.CompilerParams(collective_id=ident, has_side_effects=True),
    )(x, base, gain.reshape(1, -1))


def on_device(
    hidden_in,
    attn_gain,
    w_query,
    w_key,
    w_value,
    w_out,
    cache,
    prefix_len,
    mlp_gain,
    expert_ids,
    route_weight,
    w_gate,
    w_up,
    w_down,
):
    group_count = lax.axis_size("grp")
    head_count = lax.axis_size("head")
    my_prompt = lax.axis_index("grp")
    tokens = hidden_in.shape[1]
    width = hidden_in.shape[2]
    heads_here = w_query.shape[1] // HD
    length = prefix_len[my_prompt]
    rows = hidden_in[0].astype(jnp.float32)
    normed = rms_norm(rows, attn_gain).astype(jnp.bfloat16)
    position = (length + jnp.arange(tokens)).astype(jnp.float32)
    query = jnp.dot(normed, w_query, preferred_element_type=jnp.float32).reshape(
        tokens, heads_here, HD
    )
    key_new = jnp.dot(normed, w_key, preferred_element_type=jnp.float32).reshape(
        tokens, heads_here, HD
    )
    value_new = jnp.dot(normed, w_value, preferred_element_type=jnp.float32).reshape(
        tokens, heads_here, HD
    )
    query = (rotate(query, position) * HD ** (-0.5)).astype(jnp.bfloat16)
    key_new = rotate(key_new, position).astype(jnp.bfloat16)
    value_new = value_new.astype(jnp.bfloat16)
    keys, values = [
        lax.all_to_all(cache[part], "grp", split_axis=0, concat_axis=0, tiled=True).reshape(
            group_count * cache.shape[2], heads_here * HD
        )
        for part in range(2)
    ]
    attended = attend(
        length,
        query.reshape(tokens, heads_here * HD),
        key_new.reshape(tokens, heads_here * HD),
        value_new.reshape(tokens, heads_here * HD),
        keys,
        values,
    )
    projected = jnp.dot(attended, w_out, preferred_element_type=jnp.float32)
    resid_blocks, mixed_half = head_reduce(projected.astype(jnp.bfloat16), rows, mlp_gain, 0)
    experts_here = w_gate.shape[0]
    expert_total = experts_here * group_count
    capacity = max(2, 3 * tokens * TOPK // (2 * expert_total))
    chosen = expert_ids[0].reshape(tokens * TOPK)
    weights = route_weight[0]
    pairs = tokens * TOPK
    slots = expert_total * capacity
    one_hot = (chosen[:, None] == jnp.arange(expert_total)[None, :]).astype(jnp.bfloat16)
    earlier = (jnp.arange(pairs)[None, :] < jnp.arange(pairs)[:, None]).astype(jnp.bfloat16)
    before = jnp.dot(earlier, one_hot, preferred_element_type=jnp.float32)
    slot = jnp.sum(before * one_hot.astype(jnp.float32), axis=1).astype(jnp.int32)
    target = chosen * capacity + slot
    place = (target[:, None] == jnp.arange(slots)[None, :]).reshape(tokens, TOPK, slots)
    dispatch = jnp.sum(place.astype(jnp.float32), axis=1).astype(jnp.bfloat16)
    share_width = width // head_count
    head_at = lax.axis_index("head")
    core = lax.rem(head_at, 2)
    chip = head_at // 2
    other_core = 1 - core
    def halves(array, which):
        split = array.reshape(array.shape[:-1] + (2, 2, share_width))
        taken = lax.dynamic_index_in_dim(split, which, axis=split.ndim - 2, keepdims=False)
        return taken.reshape(array.shape[:-1] + (2 * share_width,))

    def row_halves(array, which):
        split = array.reshape((2, 2, share_width) + array.shape[1:])
        taken = lax.dynamic_index_in_dim(split, which, axis=1, keepdims=False)
        return taken.reshape((2 * share_width,) + array.shape[1:])

    half = 2 * share_width
    outgoing = lax.dot_general(
        dispatch, mixed_half, (((0,), (0,)), ((), ())), preferred_element_type=jnp.float32
    ).astype(jnp.bfloat16)
    outgoing = outgoing.reshape(group_count, experts_here, capacity, half)
    arrived = lax.all_to_all(outgoing, "grp", split_axis=0, concat_axis=0, tiled=True)
    partners = [(index, index ^ 1) for index in range(head_count)]
    arrived_other = lax.ppermute(arrived, "head", partners)
    pair_sums = []
    for expert in range(experts_here):
        mine = arrived[:, expert].reshape(group_count * capacity, half)
        other = arrived_other[:, expert].reshape(group_count * capacity, half)
        gate = jnp.dot(mine, row_halves(w_gate[expert], core), preferred_element_type=jnp.float32)
        gate = gate + jnp.dot(other, row_halves(w_gate[expert], other_core), preferred_element_type=jnp.float32)
        upper = jnp.dot(mine, row_halves(w_up[expert], core), preferred_element_type=jnp.float32)
        upper = upper + jnp.dot(other, row_halves(w_up[expert], other_core), preferred_element_type=jnp.float32)
        act = (jax.nn.silu(gate) * upper).astype(jnp.bfloat16)
        mine_part = jnp.dot(act, halves(w_down[expert], core), preferred_element_type=jnp.float32)
        other_part = jnp.dot(act, halves(w_down[expert], other_core), preferred_element_type=jnp.float32)
        partner_part = lax.ppermute(other_part.astype(jnp.bfloat16), "head", partners)
        pair_sums.append(
            (mine_part.astype(jnp.bfloat16).astype(jnp.float32) + partner_part.astype(jnp.float32))
            .astype(jnp.bfloat16)
            .reshape(group_count, capacity, half)
        )
    pair_sum = jnp.stack(pair_sums, axis=1)
    returned = lax.all_to_all(pair_sum, "grp", split_axis=0, concat_axis=0, tiled=True)
    returned = returned.reshape(slots, half)
    weighting = jnp.sum(jnp.where(place, weights[:, :, None], 0.0), axis=1)
    pieces = []
    for _ in range(3):
        piece = weighting.astype(jnp.bfloat16)
        weighting = weighting - piece.astype(jnp.float32)
        pieces.append(piece)
    combined = jnp.dot(jnp.concatenate(pieces, axis=0), returned, preferred_element_type=jnp.float32)
    combined = combined.reshape(3, tokens, half).sum(axis=0)
    first_block = combined[:, :share_width]
    second_block = combined[:, share_width:]
    keep = jnp.where(chip == 0, first_block, second_block)
    give = jnp.where(chip == 0, second_block, first_block)
    moe_share = keep + peer_swap(give.astype(jnp.bfloat16), True, 3).astype(jnp.float32)
    resid_share = lax.dynamic_index_in_dim(resid_blocks, chip, axis=0, keepdims=False)
    return (resid_share + moe_share).astype(jnp.bfloat16)[None]


def solution(mesh):
    placed = (
        P("grp", None, None),
        P(),
        P(None, "head"),
        P(None, "head"),
        P(None, "head"),
        P("head", None),
        P(None, None, "grp", "head"),
        P(),
        P(),
        P("grp", None, None),
        P("grp", None, None),
        P("grp", None, "head"),
        P("grp", None, "head"),
        P("grp", "head", None),
    )
    return jax.shard_map(
        on_device, mesh=mesh, in_specs=placed, out_specs=P("grp", None, "head"), check_vma=False
    )
```

```python
import jax
import jax.numpy as jnp
from jax import lax
from jax.experimental import pallas as pl
from jax.experimental.pallas import tpu as pltpu
from jax.sharding import PartitionSpec as P

HD = 128
TOPK = 8


def rms_norm(values, gain):
    scale = lax.rsqrt(jnp.mean(values * values, axis=-1, keepdims=True) + 1e-05)
    return values * scale * gain


def rotate(tensor, position):
    half = HD // 2
    inverse = 10000.0 ** (-(jnp.arange(half).astype(jnp.float32) * 2.0) / HD)
    angle = position[:, None] * inverse[None, :]
    cosine = jnp.cos(angle)[:, None, :]
    sine = jnp.sin(angle)[:, None, :]
    first = tensor[..., :half]
    second = tensor[..., half:]
    return jnp.concatenate(
        [first * cosine - second * sine, second * cosine + first * sine], axis=-1
    )


def peer_swap(x, across, ident):
    mesh_kind = pl.DeviceIdType.MESH

    def kernel(x_ref, o_ref, send_sem, recv_sem):
        me = lax.axis_index("head")
        group = lax.axis_index("grp")
        peer = lax.rem(me + 2, 4) if across else me + 1 - 2 * lax.rem(me, 2)
        barrier = pltpu.get_barrier_semaphore()
        pl.semaphore_signal(barrier, inc=1, device_id=(group, peer), device_id_type=mesh_kind)
        pl.semaphore_wait(barrier, 1)
        copy = pltpu.make_async_remote_copy(
            src_ref=x_ref, dst_ref=o_ref, send_sem=send_sem, recv_sem=recv_sem,
            device_id=(group, peer), device_id_type=mesh_kind,
        )
        copy.start()
        copy.wait()

    return pl.pallas_call(
        kernel,
        out_shape=jax.ShapeDtypeStruct(x.shape, x.dtype),
        in_specs=[pl.BlockSpec(memory_space=pl.ANY)],
        out_specs=pl.BlockSpec(memory_space=pl.ANY),
        scratch_shapes=[pltpu.SemaphoreType.DMA(()), pltpu.SemaphoreType.DMA(())],
        compiler_params=pltpu.CompilerParams(collective_id=ident, has_side_effects=True),
    )(x)


def attend(length, query, key_new, value_new, keys, values):
    tokens = query.shape[0]
    context = keys.shape[0]
    heads = query.shape[1] // HD

    def kernel(length_ref, q_ref, kn_ref, vn_ref, k_ref, v_ref, o_ref):
        limit = length_ref[0]
        q = q_ref[...]
        contract = (((1,), (1,)), ((), ()))
        score_old = lax.dot_general(q, k_ref[...], contract, preferred_element_type=jnp.float32)
        score_new = lax.dot_general(q, kn_ref[...], contract, preferred_element_type=jnp.float32)
        allow_old = lax.broadcasted_iota(jnp.int32, score_old.shape, 1) < limit
        allow_new = lax.broadcasted_iota(jnp.int32, score_new.shape, 1) <= lax.broadcasted_iota(
            jnp.int32, score_new.shape, 0
        )
        score_old = jnp.where(allow_old, score_old, -1e30)
        score_new = jnp.where(allow_new, score_new, -1e30)
        top = jnp.maximum(
            jnp.max(score_old, axis=1, keepdims=True), jnp.max(score_new, axis=1, keepdims=True)
        )
        prob_old = jnp.where(allow_old, jnp.exp(score_old - top), 0.0)
        prob_new = jnp.where(allow_new, jnp.exp(score_new - top), 0.0)
        total = jnp.sum(prob_old, axis=1, keepdims=True) + jnp.sum(prob_new, axis=1, keepdims=True)
        numer = jnp.dot(prob_old.astype(jnp.bfloat16), v_ref[...], preferred_element_type=jnp.float32)
        numer = numer + jnp.dot(
            prob_new.astype(jnp.bfloat16), vn_ref[...], preferred_element_type=jnp.float32
        )
        o_ref[...] = (numer / total).astype(o_ref.dtype)

    per_head = pl.BlockSpec((tokens, HD), lambda h, n: (0, h))
    grid_spec = pltpu.PrefetchScalarGridSpec(
        num_scalar_prefetch=1,
        grid=(heads,),
        in_specs=[
            per_head,
            per_head,
            per_head,
            pl.BlockSpec((context, HD), lambda h, n: (0, h)),
            pl.BlockSpec((context, HD), lambda h, n: (0, h)),
        ],
        out_specs=per_head,
    )
    return pl.pallas_call(
        kernel,
        grid_spec=grid_spec,
        out_shape=jax.ShapeDtypeStruct((tokens, heads * HD), jnp.bfloat16),
    )(length.reshape(1), query, key_new, value_new, keys, values)


def head_reduce(x, base, gain, ident):
    rows, width = x.shape
    share = width // 4
    mesh_kind = pl.DeviceIdType.MESH

    def kernel(x_ref, base_ref, gain_ref, resid_ref, normed_ref, part_in, send_buf, sum_in, sq_out, sq_in,
               send_sem, recv_sem):
        me = lax.axis_index("head")
        group = lax.axis_index("grp")
        core = lax.rem(me, 2)
        partner = me + 1 - 2 * core
        across = lax.rem(me + 2, 4)
        barrier = pltpu.get_barrier_semaphore()
        for peer in (partner, across):
            pl.semaphore_signal(barrier, inc=1, device_id=(group, peer), device_id_type=mesh_kind)
        pl.semaphore_wait(barrier, 2)

        def columns(block):
            return pl.ds(pl.multiple_of(block * share, share), share)

        halves_out = []
        for half in range(2):
            copy = pltpu.make_async_remote_copy(
                src_ref=x_ref.at[:, columns(2 * half + 1 - core)], dst_ref=part_in.at[half],
                send_sem=send_sem.at[half], recv_sem=recv_sem.at[half],
                device_id=(group, partner), device_id_type=mesh_kind,
            )
            copy.start()
            halves_out.append(copy)
        for half in range(2):
            halves_out[half].wait_recv()
            mine = x_ref[:, columns(2 * half + core)].astype(jnp.float32)
            send_buf[half] = (mine + part_in[half].astype(jnp.float32)).astype(send_buf.dtype)
        swap = pltpu.make_async_remote_copy(
            src_ref=send_buf, dst_ref=sum_in, send_sem=send_sem.at[2], recv_sem=recv_sem.at[2],
            device_id=(group, across), device_id_type=mesh_kind,
        )
        swap.start()
        swap.wait_recv()
        square = jnp.zeros((rows, 1), jnp.float32)
        for half in range(2):
            total = (
                base_ref[:, columns(2 * half + core)]
                + send_buf[half].astype(jnp.float32)
                + sum_in[half].astype(jnp.float32)
            )
            resid_ref[half] = total
            square = square + jnp.sum(total * total, axis=1, keepdims=True)
        sq_out[...] = jnp.broadcast_to(square, sq_out.shape)
        last = pltpu.make_async_remote_copy(
            src_ref=sq_out, dst_ref=sq_in, send_sem=send_sem.at[3], recv_sem=recv_sem.at[3],
            device_id=(group, partner), device_id_type=mesh_kind,
        )
        last.start()
        last.wait_recv()
        scale = lax.rsqrt((square + sq_in[:, 0:1]) / width + 1e-05)
        for half in range(2):
            normed_ref[:, half * share:(half + 1) * share] = (
                resid_ref[half] * scale * gain_ref[:, columns(2 * half + core)]
            ).astype(normed_ref.dtype)
        for copy in halves_out:
            copy.wait_send()
        swap.wait_send()
        last.wait_send()

    vmem = pl.BlockSpec(memory_space=pltpu.VMEM)
    return pl.pallas_call(
        kernel,
        out_shape=(
            jax.ShapeDtypeStruct((2, rows, share), jnp.float32),
            jax.ShapeDtypeStruct((rows, 2 * share), jnp.bfloat16),
        ),
        in_specs=[vmem, vmem, vmem],
        out_specs=(vmem, vmem),
        scratch_shapes=[
            pltpu.VMEM((2, rows, share), x.dtype),
            pltpu.VMEM((2, rows, share), x.dtype),
            pltpu.VMEM((2, rows, share), x.dtype),
            pltpu.VMEM((rows, 128), jnp.float32),
            pltpu.VMEM((rows, 128), jnp.float32),
            pltpu.SemaphoreType.DMA((4,)),
            pltpu.SemaphoreType.DMA((4,)),
        ],
        compiler_params=pltpu.CompilerParams(collective_id=ident, has_side_effects=True),
    )(x, base, gain.reshape(1, -1))


def on_device(
    hidden_in,
    attn_gain,
    w_query,
    w_key,
    w_value,
    w_out,
    cache,
    prefix_len,
    mlp_gain,
    expert_ids,
    route_weight,
    w_gate,
    w_up,
    w_down,
):
    group_count = lax.axis_size("grp")
    head_count = lax.axis_size("head")
    my_prompt = lax.axis_index("grp")
    tokens = hidden_in.shape[1]
    width = hidden_in.shape[2]
    heads_here = w_query.shape[1] // HD
    length = prefix_len[my_prompt]
    rows = hidden_in[0].astype(jnp.float32)
    normed = rms_norm(rows, attn_gain).astype(jnp.bfloat16)
    position = (length + jnp.arange(tokens)).astype(jnp.float32)
    query = jnp.dot(normed, w_query, preferred_element_type=jnp.float32).reshape(
        tokens, heads_here, HD
    )
    key_new = jnp.dot(normed, w_key, preferred_element_type=jnp.float32).reshape(
        tokens, heads_here, HD
    )
    value_new = jnp.dot(normed, w_value, preferred_element_type=jnp.float32).reshape(
        tokens, heads_here, HD
    )
    query = (rotate(query, position) * HD ** (-0.5)).astype(jnp.bfloat16)
    key_new = rotate(key_new, position).astype(jnp.bfloat16)
    value_new = value_new.astype(jnp.bfloat16)
    keys, values = [
        lax.all_to_all(cache[part], "grp", split_axis=0, concat_axis=0, tiled=True).reshape(
            group_count * cache.shape[2], heads_here * HD
        )
        for part in range(2)
    ]
    attended = attend(
        length,
        query.reshape(tokens, heads_here * HD),
        key_new.reshape(tokens, heads_here * HD),
        value_new.reshape(tokens, heads_here * HD),
        keys,
        values,
    )
    projected = jnp.dot(attended, w_out, preferred_element_type=jnp.float32)
    resid_blocks, mixed_half = head_reduce(projected.astype(jnp.bfloat16), rows, mlp_gain, 0)
    experts_here = w_gate.shape[0]
    expert_total = experts_here * group_count
    capacity = max(2, 3 * tokens * TOPK // (2 * expert_total))
    chosen = expert_ids[0].reshape(tokens * TOPK)
    weights = route_weight[0]
    pairs = tokens * TOPK
    slots = expert_total * capacity
    one_hot = (chosen[:, None] == jnp.arange(expert_total)[None, :]).astype(jnp.bfloat16)
    earlier = (jnp.arange(pairs)[None, :] < jnp.arange(pairs)[:, None]).astype(jnp.bfloat16)
    before = jnp.dot(earlier, one_hot, preferred_element_type=jnp.float32)
    slot = jnp.sum(before * one_hot.astype(jnp.float32), axis=1).astype(jnp.int32)
    target = chosen * capacity + slot
    place = (target[:, None] == jnp.arange(slots)[None, :]).reshape(tokens, TOPK, slots)
    dispatch = jnp.sum(place.astype(jnp.float32), axis=1).astype(jnp.bfloat16)
    share_width = width // head_count
    head_at = lax.axis_index("head")
    core = lax.rem(head_at, 2)
    chip = head_at // 2
    other_core = 1 - core
    def halves(array, which):
        split = array.reshape(array.shape[:-1] + (2, 2, share_width))
        taken = jnp.where(which == 0, split[..., 0, :], split[..., 1, :])
        return taken.reshape(array.shape[:-1] + (2 * share_width,))

    def row_halves(array, which):
        split = array.reshape((2, 2, share_width) + array.shape[1:])
        taken = jnp.where(which == 0, split[:, 0], split[:, 1])
        return taken.reshape((2 * share_width,) + array.shape[1:])

    half = 2 * share_width
    outgoing = lax.dot_general(
        dispatch, mixed_half, (((0,), (0,)), ((), ())), preferred_element_type=jnp.float32
    ).astype(jnp.bfloat16)
    outgoing = outgoing.reshape(group_count, experts_here, capacity, half)
    arrived = lax.all_to_all(outgoing, "grp", split_axis=0, concat_axis=0, tiled=True)
    partners = [(index, index ^ 1) for index in range(head_count)]
    arrived_other = lax.ppermute(arrived, "head", partners)
    pair_sums = []
    for expert in range(experts_here):
        mine = arrived[:, expert].reshape(group_count * capacity, half)
        other = arrived_other[:, expert].reshape(group_count * capacity, half)
        gate = jnp.dot(mine, row_halves(w_gate[expert], core), preferred_element_type=jnp.float32)
        gate = gate + jnp.dot(other, row_halves(w_gate[expert], other_core), preferred_element_type=jnp.float32)
        upper = jnp.dot(mine, row_halves(w_up[expert], core), preferred_element_type=jnp.float32)
        upper = upper + jnp.dot(other, row_halves(w_up[expert], other_core), preferred_element_type=jnp.float32)
        act = (jax.nn.silu(gate) * upper).astype(jnp.bfloat16)
        mine_part = jnp.dot(act, halves(w_down[expert], core), preferred_element_type=jnp.float32)
        other_part = jnp.dot(act, halves(w_down[expert], other_core), preferred_element_type=jnp.float32)
        partner_part = lax.ppermute(other_part.astype(jnp.bfloat16), "head", partners)
        pair_sums.append(
            (mine_part.astype(jnp.bfloat16).astype(jnp.float32) + partner_part.astype(jnp.float32))
            .astype(jnp.bfloat16)
            .reshape(group_count, capacity, half)
        )
    pair_sum = jnp.stack(pair_sums, axis=1)
    returned = lax.all_to_all(pair_sum, "grp", split_axis=0, concat_axis=0, tiled=True)
    returned = returned.reshape(slots, half)
    weighting = jnp.sum(jnp.where(place, weights[:, :, None], 0.0), axis=1)
    pieces = []
    for _ in range(3):
        piece = weighting.astype(jnp.bfloat16)
        weighting = weighting - piece.astype(jnp.float32)
        pieces.append(piece)
    combined = jnp.dot(jnp.concatenate(pieces, axis=0), returned, preferred_element_type=jnp.float32)
    combined = combined.reshape(3, tokens, half).sum(axis=0)
    first_block = combined[:, :share_width]
    second_block = combined[:, share_width:]
    keep = jnp.where(chip == 0, first_block, second_block)
    give = jnp.where(chip == 0, second_block, first_block)
    moe_share = keep + peer_swap(give.astype(jnp.bfloat16), True, 3).astype(jnp.float32)
    resid_share = lax.dynamic_index_in_dim(resid_blocks, chip, axis=0, keepdims=False)
    return (resid_share + moe_share).astype(jnp.bfloat16)[None]


def solution(mesh):
    placed = (
        P("grp", None, None),
        P(),
        P(None, "head"),
        P(None, "head"),
        P(None, "head"),
        P("head", None),
        P(None, None, "grp", "head"),
        P(),
        P(),
        P("grp", None, None),
        P("grp", None, None),
        P("grp", None, "head"),
        P("grp", None, "head"),
        P("grp", "head", None),
    )
    return jax.shard_map(
        on_device, mesh=mesh, in_specs=placed, out_specs=P("grp", None, "head"), check_vma=False
    )
```

```python
import jax
import jax.numpy as jnp
from jax import lax
from jax.experimental import pallas as pl
from jax.experimental.pallas import tpu as pltpu
from jax.sharding import PartitionSpec as P

HD = 128
TOPK = 8


def rms_norm(values, gain):
    scale = lax.rsqrt(jnp.mean(values * values, axis=-1, keepdims=True) + 1e-05)
    return values * scale * gain


def rotate(tensor, position):
    half = HD // 2
    inverse = 10000.0 ** (-(jnp.arange(half).astype(jnp.float32) * 2.0) / HD)
    angle = position[:, None] * inverse[None, :]
    cosine = jnp.cos(angle)[:, None, :]
    sine = jnp.sin(angle)[:, None, :]
    first = tensor[..., :half]
    second = tensor[..., half:]
    return jnp.concatenate(
        [first * cosine - second * sine, second * cosine + first * sine], axis=-1
    )


def peer_swap(x, across, ident):
    mesh_kind = pl.DeviceIdType.MESH

    def kernel(x_ref, o_ref, send_sem, recv_sem):
        me = lax.axis_index("head")
        group = lax.axis_index("grp")
        peer = lax.rem(me + 2, 4) if across else me + 1 - 2 * lax.rem(me, 2)
        barrier = pltpu.get_barrier_semaphore()
        pl.semaphore_signal(barrier, inc=1, device_id=(group, peer), device_id_type=mesh_kind)
        pl.semaphore_wait(barrier, 1)
        copy = pltpu.make_async_remote_copy(
            src_ref=x_ref, dst_ref=o_ref, send_sem=send_sem, recv_sem=recv_sem,
            device_id=(group, peer), device_id_type=mesh_kind,
        )
        copy.start()
        copy.wait()

    return pl.pallas_call(
        kernel,
        out_shape=jax.ShapeDtypeStruct(x.shape, x.dtype),
        in_specs=[pl.BlockSpec(memory_space=pl.ANY)],
        out_specs=pl.BlockSpec(memory_space=pl.ANY),
        scratch_shapes=[pltpu.SemaphoreType.DMA(()), pltpu.SemaphoreType.DMA(())],
        compiler_params=pltpu.CompilerParams(collective_id=ident, has_side_effects=True),
    )(x)


def attend(length, query, key_new, value_new, keys, values):
    tokens = query.shape[0]
    context = keys.shape[0]
    heads = query.shape[1] // HD

    def kernel(length_ref, q_ref, kn_ref, vn_ref, k_ref, v_ref, o_ref):
        limit = length_ref[0]
        q = q_ref[...]
        contract = (((1,), (1,)), ((), ()))
        score_old = lax.dot_general(q, k_ref[...], contract, preferred_element_type=jnp.float32)
        score_new = lax.dot_general(q, kn_ref[...], contract, preferred_element_type=jnp.float32)
        allow_old = lax.broadcasted_iota(jnp.int32, score_old.shape, 1) < limit
        allow_new = lax.broadcasted_iota(jnp.int32, score_new.shape, 1) <= lax.broadcasted_iota(
            jnp.int32, score_new.shape, 0
        )
        score_old = jnp.where(allow_old, score_old, -1e30)
        score_new = jnp.where(allow_new, score_new, -1e30)
        top = jnp.maximum(
            jnp.max(score_old, axis=1, keepdims=True), jnp.max(score_new, axis=1, keepdims=True)
        )
        prob_old = jnp.where(allow_old, jnp.exp(score_old - top), 0.0)
        prob_new = jnp.where(allow_new, jnp.exp(score_new - top), 0.0)
        total = jnp.sum(prob_old, axis=1, keepdims=True) + jnp.sum(prob_new, axis=1, keepdims=True)
        numer = jnp.dot(prob_old.astype(jnp.bfloat16), v_ref[...], preferred_element_type=jnp.float32)
        numer = numer + jnp.dot(
            prob_new.astype(jnp.bfloat16), vn_ref[...], preferred_element_type=jnp.float32
        )
        o_ref[...] = (numer / total).astype(o_ref.dtype)

    per_head = pl.BlockSpec((tokens, HD), lambda h, n: (0, h))
    grid_spec = pltpu.PrefetchScalarGridSpec(
        num_scalar_prefetch=1,
        grid=(heads,),
        in_specs=[
            per_head,
            per_head,
            per_head,
            pl.BlockSpec((context, HD), lambda h, n: (0, h)),
            pl.BlockSpec((context, HD), lambda h, n: (0, h)),
        ],
        out_specs=per_head,
    )
    return pl.pallas_call(
        kernel,
        grid_spec=grid_spec,
        out_shape=jax.ShapeDtypeStruct((tokens, heads * HD), jnp.bfloat16),
    )(length.reshape(1), query, key_new, value_new, keys, values)


def head_reduce(x, base, gain, ident):
    rows, width = x.shape
    share = width // 4
    mesh_kind = pl.DeviceIdType.MESH

    def kernel(x_ref, base_ref, gain_ref, resid_ref, normed_ref, part_in, send_buf, sum_in, sq_out, sq_in,
               send_sem, recv_sem):
        me = lax.axis_index("head")
        group = lax.axis_index("grp")
        core = lax.rem(me, 2)
        partner = me + 1 - 2 * core
        across = lax.rem(me + 2, 4)
        barrier = pltpu.get_barrier_semaphore()
        for peer in (partner, across):
            pl.semaphore_signal(barrier, inc=1, device_id=(group, peer), device_id_type=mesh_kind)
        pl.semaphore_wait(barrier, 2)

        def columns(block):
            return pl.ds(pl.multiple_of(block * share, share), share)

        halves_out = []
        for half in range(2):
            copy = pltpu.make_async_remote_copy(
                src_ref=x_ref.at[:, columns(2 * half + 1 - core)], dst_ref=part_in.at[half],
                send_sem=send_sem.at[half], recv_sem=recv_sem.at[half],
                device_id=(group, partner), device_id_type=mesh_kind,
            )
            copy.start()
            halves_out.append(copy)
        swaps = []
        for half in range(2):
            halves_out[half].wait_recv()
            mine = x_ref[:, columns(2 * half + core)].astype(jnp.float32)
            send_buf[half] = (mine + part_in[half].astype(jnp.float32)).astype(send_buf.dtype)
            swap = pltpu.make_async_remote_copy(
                src_ref=send_buf.at[half], dst_ref=sum_in.at[half], send_sem=send_sem.at[2 + half],
                recv_sem=recv_sem.at[2 + half], device_id=(group, across), device_id_type=mesh_kind,
            )
            swap.start()
            swaps.append(swap)
        for swap in swaps:
            swap.wait_recv()
        square = jnp.zeros((rows, 1), jnp.float32)
        for half in range(2):
            total = (
                base_ref[:, columns(2 * half + core)]
                + send_buf[half].astype(jnp.float32)
                + sum_in[half].astype(jnp.float32)
            )
            resid_ref[half] = total
            square = square + jnp.sum(total * total, axis=1, keepdims=True)
        sq_out[...] = jnp.broadcast_to(square, sq_out.shape)
        last = pltpu.make_async_remote_copy(
            src_ref=sq_out, dst_ref=sq_in, send_sem=send_sem.at[4], recv_sem=recv_sem.at[4],
            device_id=(group, partner), device_id_type=mesh_kind,
        )
        last.start()
        last.wait_recv()
        scale = lax.rsqrt((square + sq_in[:, 0:1]) / width + 1e-05)
        for half in range(2):
            normed_ref[:, half * share:(half + 1) * share] = (
                resid_ref[half] * scale * gain_ref[:, columns(2 * half + core)]
            ).astype(normed_ref.dtype)
        for copy in halves_out:
            copy.wait_send()
        for swap in swaps:
            swap.wait_send()
        last.wait_send()

    vmem = pl.BlockSpec(memory_space=pltpu.VMEM)
    return pl.pallas_call(
        kernel,
        out_shape=(
            jax.ShapeDtypeStruct((2, rows, share), jnp.float32),
            jax.ShapeDtypeStruct((rows, 2 * share), jnp.bfloat16),
        ),
        in_specs=[vmem, vmem, vmem],
        out_specs=(vmem, vmem),
        scratch_shapes=[
            pltpu.VMEM((2, rows, share), x.dtype),
            pltpu.VMEM((2, rows, share), x.dtype),
            pltpu.VMEM((2, rows, share), x.dtype),
            pltpu.VMEM((rows, 128), jnp.float32),
            pltpu.VMEM((rows, 128), jnp.float32),
            pltpu.SemaphoreType.DMA((5,)),
            pltpu.SemaphoreType.DMA((5,)),
        ],
        compiler_params=pltpu.CompilerParams(collective_id=ident, has_side_effects=True),
    )(x, base, gain.reshape(1, -1))


def on_device(
    hidden_in,
    attn_gain,
    w_query,
    w_key,
    w_value,
    w_out,
    cache,
    prefix_len,
    mlp_gain,
    expert_ids,
    route_weight,
    w_gate,
    w_up,
    w_down,
):
    group_count = lax.axis_size("grp")
    head_count = lax.axis_size("head")
    my_prompt = lax.axis_index("grp")
    tokens = hidden_in.shape[1]
    width = hidden_in.shape[2]
    heads_here = w_query.shape[1] // HD
    length = prefix_len[my_prompt]
    rows = hidden_in[0].astype(jnp.float32)
    normed = rms_norm(rows, attn_gain).astype(jnp.bfloat16)
    position = (length + jnp.arange(tokens)).astype(jnp.float32)
    query = jnp.dot(normed, w_query, preferred_element_type=jnp.float32).reshape(
        tokens, heads_here, HD
    )
    key_new = jnp.dot(normed, w_key, preferred_element_type=jnp.float32).reshape(
        tokens, heads_here, HD
    )
    value_new = jnp.dot(normed, w_value, preferred_element_type=jnp.float32).reshape(
        tokens, heads_here, HD
    )
    query = (rotate(query, position) * HD ** (-0.5)).astype(jnp.bfloat16)
    key_new = rotate(key_new, position).astype(jnp.bfloat16)
    value_new = value_new.astype(jnp.bfloat16)
    keys, values = [
        lax.all_to_all(cache[part], "grp", split_axis=0, concat_axis=0, tiled=True).reshape(
            group_count * cache.shape[2], heads_here * HD
        )
        for part in range(2)
    ]
    attended = attend(
        length,
        query.reshape(tokens, heads_here * HD),
        key_new.reshape(tokens, heads_here * HD),
        value_new.reshape(tokens, heads_here * HD),
        keys,
        values,
    )
    projected = jnp.dot(attended, w_out, preferred_element_type=jnp.float32)
    resid_blocks, mixed_half = head_reduce(projected.astype(jnp.bfloat16), rows, mlp_gain, 0)
    experts_here = w_gate.shape[0]
    expert_total = experts_here * group_count
    capacity = max(2, 3 * tokens * TOPK // (2 * expert_total))
    chosen = expert_ids[0].reshape(tokens * TOPK)
    weights = route_weight[0]
    pairs = tokens * TOPK
    slots = expert_total * capacity
    one_hot = (chosen[:, None] == jnp.arange(expert_total)[None, :]).astype(jnp.bfloat16)
    earlier = (jnp.arange(pairs)[None, :] < jnp.arange(pairs)[:, None]).astype(jnp.bfloat16)
    before = jnp.dot(earlier, one_hot, preferred_element_type=jnp.float32)
    slot = jnp.sum(before * one_hot.astype(jnp.float32), axis=1).astype(jnp.int32)
    target = chosen * capacity + slot
    place = (target[:, None] == jnp.arange(slots)[None, :]).reshape(tokens, TOPK, slots)
    dispatch = jnp.sum(place.astype(jnp.float32), axis=1).astype(jnp.bfloat16)
    share_width = width // head_count
    head_at = lax.axis_index("head")
    core = lax.rem(head_at, 2)
    chip = head_at // 2
    other_core = 1 - core
    def halves(array, which):
        split = array.reshape(array.shape[:-1] + (2, 2, share_width))
        taken = lax.dynamic_index_in_dim(split, which, axis=split.ndim - 2, keepdims=False)
        return taken.reshape(array.shape[:-1] + (2 * share_width,))

    def row_halves(array, which):
        split = array.reshape((2, 2, share_width) + array.shape[1:])
        taken = lax.dynamic_index_in_dim(split, which, axis=1, keepdims=False)
        return taken.reshape((2 * share_width,) + array.shape[1:])

    half = 2 * share_width
    outgoing = lax.dot_general(
        dispatch, mixed_half, (((0,), (0,)), ((), ())), preferred_element_type=jnp.float32
    ).astype(jnp.bfloat16)
    outgoing = outgoing.reshape(group_count, experts_here, capacity, half)
    arrived = lax.all_to_all(outgoing, "grp", split_axis=0, concat_axis=0, tiled=True)
    partners = [(index, index ^ 1) for index in range(head_count)]
    arrived_other = lax.ppermute(arrived, "head", partners)
    pair_sums = []
    for expert in range(experts_here):
        mine = arrived[:, expert].reshape(group_count * capacity, half)
        other = arrived_other[:, expert].reshape(group_count * capacity, half)
        gate = jnp.dot(mine, row_halves(w_gate[expert], core), preferred_element_type=jnp.float32)
        gate = gate + jnp.dot(other, row_halves(w_gate[expert], other_core), preferred_element_type=jnp.float32)
        upper = jnp.dot(mine, row_halves(w_up[expert], core), preferred_element_type=jnp.float32)
        upper = upper + jnp.dot(other, row_halves(w_up[expert], other_core), preferred_element_type=jnp.float32)
        act = (jax.nn.silu(gate) * upper).astype(jnp.bfloat16)
        mine_part = jnp.dot(act, halves(w_down[expert], core), preferred_element_type=jnp.float32)
        other_part = jnp.dot(act, halves(w_down[expert], other_core), preferred_element_type=jnp.float32)
        partner_part = lax.ppermute(other_part.astype(jnp.bfloat16), "head", partners)
        pair_sums.append(
            (mine_part.astype(jnp.bfloat16).astype(jnp.float32) + partner_part.astype(jnp.float32))
            .astype(jnp.bfloat16)
            .reshape(group_count, capacity, half)
        )
    pair_sum = jnp.stack(pair_sums, axis=1)
    returned = lax.all_to_all(pair_sum, "grp", split_axis=0, concat_axis=0, tiled=True)
    returned = returned.reshape(slots, half)
    weighting = jnp.sum(jnp.where(place, weights[:, :, None], 0.0), axis=1)
    pieces = []
    for _ in range(3):
        piece = weighting.astype(jnp.bfloat16)
        weighting = weighting - piece.astype(jnp.float32)
        pieces.append(piece)
    combined = jnp.dot(jnp.concatenate(pieces, axis=0), returned, preferred_element_type=jnp.float32)
    combined = combined.reshape(3, tokens, half).sum(axis=0)
    first_block = combined[:, :share_width]
    second_block = combined[:, share_width:]
    keep = jnp.where(chip == 0, first_block, second_block)
    give = jnp.where(chip == 0, second_block, first_block)
    moe_share = keep + peer_swap(give.astype(jnp.bfloat16), True, 3).astype(jnp.float32)
    resid_share = lax.dynamic_index_in_dim(resid_blocks, chip, axis=0, keepdims=False)
    return (resid_share + moe_share).astype(jnp.bfloat16)[None]


def solution(mesh):
    placed = (
        P("grp", None, None),
        P(),
        P(None, "head"),
        P(None, "head"),
        P(None, "head"),
        P("head", None),
        P(None, None, "grp", "head"),
        P(),
        P(),
        P("grp", None, None),
        P("grp", None, None),
        P("grp", None, "head"),
        P("grp", None, "head"),
        P("grp", "head", None),
    )
    return jax.shard_map(
        on_device, mesh=mesh, in_specs=placed, out_specs=P("grp", None, "head"), check_vma=False
    )
```

```python
import jax
import jax.numpy as jnp
from jax import lax
from jax.experimental import pallas as pl
from jax.experimental.pallas import tpu as pltpu
from jax.sharding import PartitionSpec as P

HD = 128
TOPK = 8


def rms_norm(values, gain):
    scale = lax.rsqrt(jnp.mean(values * values, axis=-1, keepdims=True) + 1e-05)
    return values * scale * gain


def rotate(tensor, position):
    half = HD // 2
    inverse = 10000.0 ** (-(jnp.arange(half).astype(jnp.float32) * 2.0) / HD)
    angle = position[:, None] * inverse[None, :]
    cosine = jnp.cos(angle)[:, None, :]
    sine = jnp.sin(angle)[:, None, :]
    first = tensor[..., :half]
    second = tensor[..., half:]
    return jnp.concatenate(
        [first * cosine - second * sine, second * cosine + first * sine], axis=-1
    )


def peer_swap(x, across, ident):
    mesh_kind = pl.DeviceIdType.MESH

    def kernel(x_ref, o_ref, send_sem, recv_sem):
        me = lax.axis_index("head")
        group = lax.axis_index("grp")
        peer = lax.rem(me + 2, 4) if across else me + 1 - 2 * lax.rem(me, 2)
        barrier = pltpu.get_barrier_semaphore()
        pl.semaphore_signal(barrier, inc=1, device_id=(group, peer), device_id_type=mesh_kind)
        pl.semaphore_wait(barrier, 1)
        copy = pltpu.make_async_remote_copy(
            src_ref=x_ref, dst_ref=o_ref, send_sem=send_sem, recv_sem=recv_sem,
            device_id=(group, peer), device_id_type=mesh_kind,
        )
        copy.start()
        copy.wait()

    return pl.pallas_call(
        kernel,
        out_shape=jax.ShapeDtypeStruct(x.shape, x.dtype),
        in_specs=[pl.BlockSpec(memory_space=pltpu.VMEM)],
        out_specs=pl.BlockSpec(memory_space=pltpu.VMEM),
        scratch_shapes=[pltpu.SemaphoreType.DMA(()), pltpu.SemaphoreType.DMA(())],
        compiler_params=pltpu.CompilerParams(collective_id=ident, has_side_effects=True),
    )(x)


def attend(length, query, key_new, value_new, keys, values):
    tokens = query.shape[0]
    context = keys.shape[0]
    heads = query.shape[1] // HD

    def kernel(length_ref, q_ref, kn_ref, vn_ref, k_ref, v_ref, o_ref):
        limit = length_ref[0]
        q = q_ref[...]
        contract = (((1,), (1,)), ((), ()))
        score_old = lax.dot_general(q, k_ref[...], contract, preferred_element_type=jnp.float32)
        score_new = lax.dot_general(q, kn_ref[...], contract, preferred_element_type=jnp.float32)
        allow_old = lax.broadcasted_iota(jnp.int32, score_old.shape, 1) < limit
        allow_new = lax.broadcasted_iota(jnp.int32, score_new.shape, 1) <= lax.broadcasted_iota(
            jnp.int32, score_new.shape, 0
        )
        score_old = jnp.where(allow_old, score_old, -1e30)
        score_new = jnp.where(allow_new, score_new, -1e30)
        top = jnp.maximum(
            jnp.max(score_old, axis=1, keepdims=True), jnp.max(score_new, axis=1, keepdims=True)
        )
        prob_old = jnp.where(allow_old, jnp.exp(score_old - top), 0.0)
        prob_new = jnp.where(allow_new, jnp.exp(score_new - top), 0.0)
        total = jnp.sum(prob_old, axis=1, keepdims=True) + jnp.sum(prob_new, axis=1, keepdims=True)
        numer = jnp.dot(prob_old.astype(jnp.bfloat16), v_ref[...], preferred_element_type=jnp.float32)
        numer = numer + jnp.dot(
            prob_new.astype(jnp.bfloat16), vn_ref[...], preferred_element_type=jnp.float32
        )
        o_ref[...] = (numer / total).astype(o_ref.dtype)

    per_head = pl.BlockSpec((tokens, HD), lambda h, n: (0, h))
    grid_spec = pltpu.PrefetchScalarGridSpec(
        num_scalar_prefetch=1,
        grid=(heads,),
        in_specs=[
            per_head,
            per_head,
            per_head,
            pl.BlockSpec((context, HD), lambda h, n: (0, h)),
            pl.BlockSpec((context, HD), lambda h, n: (0, h)),
        ],
        out_specs=per_head,
    )
    return pl.pallas_call(
        kernel,
        grid_spec=grid_spec,
        out_shape=jax.ShapeDtypeStruct((tokens, heads * HD), jnp.bfloat16),
    )(length.reshape(1), query, key_new, value_new, keys, values)


def head_reduce(x, base, gain, ident):
    rows, width = x.shape
    share = width // 4
    mesh_kind = pl.DeviceIdType.MESH

    def kernel(x_ref, base_ref, gain_ref, resid_ref, normed_ref, part_in, send_buf, sum_in, sq_out, sq_in,
               send_sem, recv_sem):
        me = lax.axis_index("head")
        group = lax.axis_index("grp")
        core = lax.rem(me, 2)
        partner = me + 1 - 2 * core
        across = lax.rem(me + 2, 4)
        barrier = pltpu.get_barrier_semaphore()
        for peer in (partner, across):
            pl.semaphore_signal(barrier, inc=1, device_id=(group, peer), device_id_type=mesh_kind)
        pl.semaphore_wait(barrier, 2)

        def columns(block):
            return pl.ds(pl.multiple_of(block * share, share), share)

        halves_out = []
        for half in range(2):
            copy = pltpu.make_async_remote_copy(
                src_ref=x_ref.at[:, columns(2 * half + 1 - core)], dst_ref=part_in.at[half],
                send_sem=send_sem.at[half], recv_sem=recv_sem.at[half],
                device_id=(group, partner), device_id_type=mesh_kind,
            )
            copy.start()
            halves_out.append(copy)
        swaps = []
        for half in range(2):
            halves_out[half].wait_recv()
            mine = x_ref[:, columns(2 * half + core)].astype(jnp.float32)
            send_buf[half] = (mine + part_in[half].astype(jnp.float32)).astype(send_buf.dtype)
            swap = pltpu.make_async_remote_copy(
                src_ref=send_buf.at[half], dst_ref=sum_in.at[half], send_sem=send_sem.at[2 + half],
                recv_sem=recv_sem.at[2 + half], device_id=(group, across), device_id_type=mesh_kind,
            )
            swap.start()
            swaps.append(swap)
        for swap in swaps:
            swap.wait_recv()
        square = jnp.zeros((rows, 1), jnp.float32)
        for half in range(2):
            total = (
                base_ref[:, columns(2 * half + core)]
                + send_buf[half].astype(jnp.float32)
                + sum_in[half].astype(jnp.float32)
            )
            resid_ref[half] = total
            square = square + jnp.sum(total * total, axis=1, keepdims=True)
        sq_out[...] = jnp.broadcast_to(square, sq_out.shape)
        last = pltpu.make_async_remote_copy(
            src_ref=sq_out, dst_ref=sq_in, send_sem=send_sem.at[4], recv_sem=recv_sem.at[4],
            device_id=(group, partner), device_id_type=mesh_kind,
        )
        last.start()
        last.wait_recv()
        scale = lax.rsqrt((square + sq_in[:, 0:1]) / width + 1e-05)
        for half in range(2):
            normed_ref[:, half * share:(half + 1) * share] = (
                resid_ref[half] * scale * gain_ref[:, columns(2 * half + core)]
            ).astype(normed_ref.dtype)
        for copy in halves_out:
            copy.wait_send()
        for swap in swaps:
            swap.wait_send()
        last.wait_send()

    vmem = pl.BlockSpec(memory_space=pltpu.VMEM)
    return pl.pallas_call(
        kernel,
        out_shape=(
            jax.ShapeDtypeStruct((2, rows, share), jnp.float32),
            jax.ShapeDtypeStruct((rows, 2 * share), jnp.bfloat16),
        ),
        in_specs=[vmem, vmem, vmem],
        out_specs=(vmem, vmem),
        scratch_shapes=[
            pltpu.VMEM((2, rows, share), x.dtype),
            pltpu.VMEM((2, rows, share), x.dtype),
            pltpu.VMEM((2, rows, share), x.dtype),
            pltpu.VMEM((rows, 128), jnp.float32),
            pltpu.VMEM((rows, 128), jnp.float32),
            pltpu.SemaphoreType.DMA((5,)),
            pltpu.SemaphoreType.DMA((5,)),
        ],
        compiler_params=pltpu.CompilerParams(collective_id=ident, has_side_effects=True),
    )(x, base, gain.reshape(1, -1))


def on_device(
    hidden_in,
    attn_gain,
    w_query,
    w_key,
    w_value,
    w_out,
    cache,
    prefix_len,
    mlp_gain,
    expert_ids,
    route_weight,
    w_gate,
    w_up,
    w_down,
):
    group_count = lax.axis_size("grp")
    head_count = lax.axis_size("head")
    my_prompt = lax.axis_index("grp")
    tokens = hidden_in.shape[1]
    width = hidden_in.shape[2]
    heads_here = w_query.shape[1] // HD
    length = prefix_len[my_prompt]
    rows = hidden_in[0].astype(jnp.float32)
    normed = rms_norm(rows, attn_gain).astype(jnp.bfloat16)
    position = (length + jnp.arange(tokens)).astype(jnp.float32)
    query = jnp.dot(normed, w_query, preferred_element_type=jnp.float32).reshape(
        tokens, heads_here, HD
    )
    key_new = jnp.dot(normed, w_key, preferred_element_type=jnp.float32).reshape(
        tokens, heads_here, HD
    )
    value_new = jnp.dot(normed, w_value, preferred_element_type=jnp.float32).reshape(
        tokens, heads_here, HD
    )
    query = (rotate(query, position) * HD ** (-0.5)).astype(jnp.bfloat16)
    key_new = rotate(key_new, position).astype(jnp.bfloat16)
    value_new = value_new.astype(jnp.bfloat16)
    keys, values = [
        lax.all_to_all(cache[part], "grp", split_axis=0, concat_axis=0, tiled=True).reshape(
            group_count * cache.shape[2], heads_here * HD
        )
        for part in range(2)
    ]
    attended = attend(
        length,
        query.reshape(tokens, heads_here * HD),
        key_new.reshape(tokens, heads_here * HD),
        value_new.reshape(tokens, heads_here * HD),
        keys,
        values,
    )
    projected = jnp.dot(attended, w_out, preferred_element_type=jnp.float32)
    resid_blocks, mixed_half = head_reduce(projected.astype(jnp.bfloat16), rows, mlp_gain, 0)
    experts_here = w_gate.shape[0]
    expert_total = experts_here * group_count
    capacity = max(2, 3 * tokens * TOPK // (2 * expert_total))
    chosen = expert_ids[0].reshape(tokens * TOPK)
    weights = route_weight[0]
    pairs = tokens * TOPK
    slots = expert_total * capacity
    one_hot = (chosen[:, None] == jnp.arange(expert_total)[None, :]).astype(jnp.bfloat16)
    earlier = (jnp.arange(pairs)[None, :] < jnp.arange(pairs)[:, None]).astype(jnp.bfloat16)
    before = jnp.dot(earlier, one_hot, preferred_element_type=jnp.float32)
    slot = jnp.sum(before * one_hot.astype(jnp.float32), axis=1).astype(jnp.int32)
    target = chosen * capacity + slot
    place = (target[:, None] == jnp.arange(slots)[None, :]).reshape(tokens, TOPK, slots)
    dispatch = jnp.sum(place.astype(jnp.float32), axis=1).astype(jnp.bfloat16)
    share_width = width // head_count
    head_at = lax.axis_index("head")
    core = lax.rem(head_at, 2)
    chip = head_at // 2
    other_core = 1 - core
    def halves(array, which):
        split = array.reshape(array.shape[:-1] + (2, 2, share_width))
        taken = lax.dynamic_index_in_dim(split, which, axis=split.ndim - 2, keepdims=False)
        return taken.reshape(array.shape[:-1] + (2 * share_width,))

    def row_halves(array, which):
        split = array.reshape((2, 2, share_width) + array.shape[1:])
        taken = lax.dynamic_index_in_dim(split, which, axis=1, keepdims=False)
        return taken.reshape((2 * share_width,) + array.shape[1:])

    half = 2 * share_width
    outgoing = lax.dot_general(
        dispatch, mixed_half, (((0,), (0,)), ((), ())), preferred_element_type=jnp.float32
    ).astype(jnp.bfloat16)
    outgoing = outgoing.reshape(group_count, experts_here, capacity, half)
    arrived = lax.all_to_all(outgoing, "grp", split_axis=0, concat_axis=0, tiled=True)
    partners = [(index, index ^ 1) for index in range(head_count)]
    arrived_other = lax.ppermute(arrived, "head", partners)
    pair_sums = []
    for expert in range(experts_here):
        mine = arrived[:, expert].reshape(group_count * capacity, half)
        other = arrived_other[:, expert].reshape(group_count * capacity, half)
        gate = jnp.dot(mine, row_halves(w_gate[expert], core), preferred_element_type=jnp.float32)
        gate = gate + jnp.dot(other, row_halves(w_gate[expert], other_core), preferred_element_type=jnp.float32)
        upper = jnp.dot(mine, row_halves(w_up[expert], core), preferred_element_type=jnp.float32)
        upper = upper + jnp.dot(other, row_halves(w_up[expert], other_core), preferred_element_type=jnp.float32)
        act = (jax.nn.silu(gate) * upper).astype(jnp.bfloat16)
        mine_part = jnp.dot(act, halves(w_down[expert], core), preferred_element_type=jnp.float32)
        other_part = jnp.dot(act, halves(w_down[expert], other_core), preferred_element_type=jnp.float32)
        partner_part = lax.ppermute(other_part.astype(jnp.bfloat16), "head", partners)
        pair_sums.append(
            (mine_part.astype(jnp.bfloat16).astype(jnp.float32) + partner_part.astype(jnp.float32))
            .astype(jnp.bfloat16)
            .reshape(group_count, capacity, half)
        )
    pair_sum = jnp.stack(pair_sums, axis=1)
    returned = lax.all_to_all(pair_sum, "grp", split_axis=0, concat_axis=0, tiled=True)
    returned = returned.reshape(slots, half)
    weighting = jnp.sum(jnp.where(place, weights[:, :, None], 0.0), axis=1)
    pieces = []
    for _ in range(3):
        piece = weighting.astype(jnp.bfloat16)
        weighting = weighting - piece.astype(jnp.float32)
        pieces.append(piece)
    combined = jnp.dot(jnp.concatenate(pieces, axis=0), returned, preferred_element_type=jnp.float32)
    combined = combined.reshape(3, tokens, half).sum(axis=0)
    first_block = combined[:, :share_width]
    second_block = combined[:, share_width:]
    keep = jnp.where(chip == 0, first_block, second_block)
    give = jnp.where(chip == 0, second_block, first_block)
    moe_share = keep + peer_swap(give.astype(jnp.bfloat16), True, 3).astype(jnp.float32)
    resid_share = lax.dynamic_index_in_dim(resid_blocks, chip, axis=0, keepdims=False)
    return (resid_share + moe_share).astype(jnp.bfloat16)[None]


def solution(mesh):
    placed = (
        P("grp", None, None),
        P(),
        P(None, "head"),
        P(None, "head"),
        P(None, "head"),
        P("head", None),
        P(None, None, "grp", "head"),
        P(),
        P(),
        P("grp", None, None),
        P("grp", None, None),
        P("grp", None, "head"),
        P("grp", None, "head"),
        P("grp", "head", None),
    )
    return jax.shard_map(
        on_device, mesh=mesh, in_specs=placed, out_specs=P("grp", None, "head"), check_vma=False
    )
```
